128 devices in a mesh: mem: 8 (over x, core), tile: 16 (over z, y).
Axes of the slice: x: 4, y: 4, z: 4, core: 2. Of those that a mesh axis runs over, the one named last changes fastest.
Arguments:
- members: bfloat16 [16, 137, 8192], P('mem', None, 'tile'), may hold values from -18 to 18
- vertical: bfloat16 [137, 137], replicated, may hold values from 0 to 1, as said below
- jacobian: bfloat16 [2048, 231, 137], P('tile'), may hold values from -0.5 to 0.5
- sketch_bits: int32 [3, 2048, 231], P(None, 'tile'), may hold values from 0 to 1
- test_bits: int32 [3, 2048, 231], P(None, 'tile'), may hold values from 0 to 1
- obs_column: int32 [2048], P('tile'), may hold values from 0 to 8191, as said below
- obs_slot: int32 [2048], P('tile'), may hold values from 0 to 31, as said below
Outputs:
- image_q: float32 [3, 2048, 231], P(None, 'tile')
- image_w: float32 [3, 2048, 231], P(None, 'tile')
- trace_mean: float32 [], replicated
- sketch_rayleigh: float32 [], replicated
The draws below stay inside these ranges and needn't reach their ends.
Inputs may be any that keep to these rules, and one draw needn't show every extreme that they name: The observations of owner d are rows d * 128 to (d + 1) * 128 - 1; an observation's column lies in tile obs_column // 512. `obs_slot`: among one owner's observations whose columns lie in the same tile the slots are distinct, so at most 32 of them lie in one tile; every owner has exactly 32 observations in some tile. A vertical correlation matrix: symmetric, positive semidefinite, with ones on the diagonal.
All inputs are finite; a program needn't handle non-finite values.
Results may differ from the reference program's by a relative error of at most 0.0053.
Values may be sent and summed in bfloat16 or wider, within the bound.
No kernel may reach another device: no remote copies, remote signals or barrier semaphores. Data moves between devices by JAX's collectives and lax.ppermute only.
A program may use at most 128 MiB of HBM per device.

```python
import jax
import jax.numpy as jnp
from jax import lax

LEV = 137
CHAN = 231
CB = 32
CA = 16
OBS_DEV = 128
K = 3
STEPS = 6
NCOL = 8192
MEMBERS = 16
NOBS = 2048
N_TILE = 16


correlation_scale = 3.0


def observation_layout(key):
    base_key = jax.random.fold_in(key, 4242)
    capacity = OBS_DEV // 4

    def one_owner(owner_id):
        keys = jax.random.split(jax.random.fold_in(base_key, owner_id), 5)
        weight = jax.random.randint(keys[0], (N_TILE,), 0, 4096)
        decline = jax.random.randint(keys[1], (N_TILE,), 1, 257)
        leader = jax.random.randint(keys[2], (), 0, N_TILE)
        tile_ids = jnp.arange(N_TILE)
        weight = jnp.where(tile_ids == leader, 1 << 19, weight)
        slot_ids = jnp.arange(capacity)
        score = weight[:, None] - slot_ids[None, :] * decline[:, None] + 65536
        score = score * (N_TILE * capacity) + (tile_ids[:, None] * capacity + slot_ids[None, :])
        _, chosen = lax.top_k(score.reshape(-1), OBS_DEV)
        order = jax.random.permutation(keys[3], OBS_DEV)
        chosen = chosen[order]
        source = chosen // capacity
        slot_of = chosen % capacity
        column = source * (CA * CB) + jax.random.randint(keys[4], (OBS_DEV,), 0, CA * CB)
        return (column, slot_of)
    columns, slots_all = jax.vmap(one_owner)(jnp.arange(N_TILE))
    return (columns.reshape(-1).astype(jnp.int32), slots_all.reshape(-1).astype(jnp.int32))


def draw_obs_column(key, part):
    return observation_layout(key)[0]


def draw_obs_slot(key, part):
    return observation_layout(key)[1]


def draw_vertical(key, part):
    level_key = jax.random.fold_in(key, 7311)
    spacing = jax.random.uniform(level_key, (LEV,), jnp.float32, 0.75, 1.5)
    height = jnp.cumsum(spacing)
    distance = jnp.abs(height[:, None] - height[None, :])
    return jnp.exp(-distance / correlation_scale).astype(jnp.bfloat16)


def plant(array, stream_key, least, top_value):
    dims = array.shape
    spot = [jax.random.randint(jax.random.fold_in(stream_key, axis), (), 0, dims[axis]) for axis in range(len(dims))]
    array = array.at[tuple(spot)].set(least)
    longest = dims.index(max(dims))
    spot[longest] = (spot[longest] + 1) % dims[longest]
    return array.at[tuple(spot)].set(top_value)


def level_of(rng, extent, shards, low, high):
    def one(dim, blocks):
        heights = jax.random.uniform(jax.random.fold_in(jax.random.fold_in(rng, 6), dim), (blocks,), jnp.float32, low / len(shards), high / len(shards))
        return jnp.repeat(jnp.exp(heights), extent[dim] // blocks).reshape((-1,) + (1,) * (len(extent) - dim - 1))

    level = one(*shards[0])
    for cut in shards[1:]:
        level = level * one(*cut)
    return level


def centred(stream_key, shape, width, most, cuts=(), held_as=jnp.bfloat16):
    drawn = width * jax.random.normal(stream_key, shape, jnp.float32)
    if cuts:
        drawn = drawn * level_of(stream_key, shape, cuts, -0.22, 0.18)
    return jnp.clip(drawn, -most, most).astype(held_as)


def setup_inputs(seed: int = 0) -> dict:
    key_list = jax.random.split(jax.random.key(seed), 8)
    members = centred(key_list[0], (MEMBERS, LEV, NCOL), 3.0, 18.0, ((0, 8), (2, 16)))
    vertical = draw_vertical(jax.random.fold_in(key_list[7], 71), 0)
    jacobian = centred(key_list[2], (NOBS, CHAN, LEV), LEV ** -0.5, 0.5, ((0, 16),))
    sketch_bits = plant(jax.random.randint(key_list[3], (K, NOBS, CHAN), 0, 2), jax.random.fold_in(key_list[3], 1), 0, 1).astype(jnp.int32)
    test_bits = plant(jax.random.randint(key_list[4], (K, NOBS, CHAN), 0, 2), jax.random.fold_in(key_list[4], 1), 0, 1).astype(jnp.int32)
    obs_column = draw_obs_column(jax.random.fold_in(key_list[7], 71), 0)
    obs_slot = draw_obs_slot(jax.random.fold_in(key_list[7], 71), 0)
    return {"members": members, "vertical": vertical, "jacobian": jacobian, "sketch_bits": sketch_bits, "test_bits": test_bits, "obs_column": obs_column, "obs_slot": obs_slot}


diffusion_rate = 0.2
highest = lax.Precision.HIGHEST

def round_trip(values):
    return lax.optimization_barrier(values.astype(jnp.bfloat16)).astype(jnp.float32)

def relax_global(state):
    places = jnp.arange(state.shape[-1]) % CB
    west_ok = (places > 0).astype(state.dtype)
    east_ok = (places < CB - 1).astype(state.dtype)
    for _ in range(STEPS):
        north = jnp.roll(state, CB, axis=-1)
        south = jnp.roll(state, -CB, axis=-1)
        west = jnp.roll(state, 1, axis=-1)
        east = jnp.roll(state, -1, axis=-1)
        state = state + diffusion_rate * (north - state + (south - state) + west_ok * (west - state) + east_ok * (east - state))
    return state

def apply_operator(vectors, members, vertical, jacobian, obs_column):
    probes = vectors.shape[0]
    jacobian_f = jacobian.astype(jnp.float32)
    rounded = round_trip(vectors)
    adjoint = jnp.einsum('ocl,poc->plo', jacobian_f, rounded).astype(jnp.bfloat16)
    field_sum = jnp.zeros((probes, LEV, NCOL), jnp.float32).at[:, :, obs_column].add(adjoint.astype(jnp.float32))
    vertical_f = vertical.astype(jnp.float32)

    def member_term(carry, member):
        member_f = member.astype(jnp.float32)
        product = round_trip(member_f[None] * field_sum)
        mixed = jnp.einsum('kl,plc->pkc', vertical_f, product)
        return (carry + member_f[None] * relax_global(mixed), None)
    summed, _ = lax.scan(member_term, jnp.zeros((probes, LEV, NCOL), jnp.float32), members)
    covariance = summed / (MEMBERS - 1)
    profile = covariance[:, :, obs_column].astype(jnp.bfloat16).astype(jnp.float32)
    return jnp.einsum('ocl,plo->poc', jacobian_f, profile)

def reference(members, vertical, jacobian, sketch_bits, test_bits, obs_column, obs_slot):
    count = float(NOBS * CHAN)
    sketch = (2 * sketch_bits - 1).astype(jnp.float32)
    test = (2 * test_bits - 1).astype(jnp.float32)
    sketch_image = apply_operator(sketch, members, vertical, jacobian, obs_column)
    columns = []
    for index in range(K):
        residue = sketch_image[index]
        if index > 0:
            stacked = jnp.stack(columns)
            inner = jnp.einsum('ioc,oc->i', stacked, residue, precision=highest)
            residue = residue - jnp.einsum('i,ioc->oc', inner, stacked, precision=highest) / count
        square_sum = jnp.sum(residue * residue)
        columns.append(residue * jnp.sqrt(count / square_sum))
    basis = jnp.stack(columns)
    intersection = jnp.einsum('ioc,joc->ij', basis, test, precision=highest) / count
    remainder = test - jnp.einsum('ij,ioc->joc', intersection, basis, precision=highest)
    images = apply_operator(jnp.concatenate([basis, remainder], axis=0), members, vertical, jacobian, obs_column)
    image_q = images[:K]
    image_w = images[K:]
    trace_q = jnp.sum(basis * image_q)
    trace_mean = trace_q / (count * count) + jnp.sum(remainder * image_w) / (K * count)
    sketch_rayleigh = trace_q / (K * count)
    return (image_q, image_w, trace_mean, sketch_rayleigh)
```

```python
import functools

import jax
import jax.numpy as jnp
import numpy as np
from jax import lax
from jax.experimental import pallas as pl
from jax.experimental.pallas import tpu as pltpu
from jax.sharding import Mesh
from jax.sharding import PartitionSpec as P

CB = 32
NX = 256
K = 3
STEPS = 6
TILE = ("tile_0", "tile_1")
TILES = 16
HALF = 72
FULL = 2 * HALF
CAP = 32
OBS = 128
GROUP = 16


F32 = jnp.float32
BF16 = jnp.bfloat16
VMEM_SPEC = pl.BlockSpec(memory_space=pltpu.VMEM)
SMEM_SPEC = pl.BlockSpec(memory_space=pltpu.SMEM)
NT = (((1,), (1,)), ((), ()))

WALK_SCALE = 1.3338


def walk_table():
    walks = np.zeros((2 * STEPS + 1, 2 * STEPS + 1))
    walks[STEPS, STEPS] = 1
    for _ in range(STEPS):
        grown = walks.copy()
        grown[1:] += walks[:-1]
        grown[:-1] += walks[1:]
        grown[:, 1:] += walks[:, :-1]
        grown[:, :-1] += walks[:, 1:]
        walks = grown

    def count(a, d):
        return walks[STEPS + a, STEPS + d] if d <= STEPS else 0.0

    table = np.zeros((STEPS + 1, CB, CB), np.float32)
    for a in range(STEPS + 1):
        for b in range(CB):
            for c in range(CB):
                table[a, b, c] = (
                    count(a, abs(b - c)) + count(a, b + c + 1) + count(a, 2 * CB - 1 - b - c)
                )
    return table * WALK_SCALE


def dot(a, b, dims=(((1,), (0,)), ((), ()))):
    return lax.dot_general(a, b, dims, preferred_element_type=F32)


def signs_kernel(core_ref, v_ref, jac_ref, out_ref, rows, turned):
    step = pl.program_id(0)

    @pl.when(step == 0)
    def _():
        rows[...] = jnp.zeros_like(rows)

    for o in range(GROUP):
        r = dot(v_ref[o], jac_ref[o])
        for p in range(2 * K):
            rows[p, pl.ds(step * GROUP + o, 1), 0:137] = r[p : p + 1, :]

    @pl.when(step == pl.num_programs(0) - 1)
    def _():
        start = pl.multiple_of(core_ref[0] * HALF, 8)
        for p in range(2 * K):
            turned[...] = rows[p].T
            out_ref[p * HALF : (p + 1) * HALF, :] = turned[pl.ds(start, HALF), :].astype(BF16)


def sign_adjoints(core, v, jacobian):
    obs, channels, levels = jacobian.shape
    return pl.pallas_call(
        signs_kernel,
        grid=(obs // GROUP,),
        in_specs=[
            SMEM_SPEC,
            pl.BlockSpec((GROUP, 8, channels), lambda i: (i, 0, 0)),
            pl.BlockSpec((GROUP, channels, levels), lambda i: (i, 0, 0)),
        ],
        out_specs=pl.BlockSpec((2 * K * HALF, OBS), lambda i: (0, 0)),
        out_shape=jax.ShapeDtypeStruct((2 * K * HALF, OBS), BF16),
        scratch_shapes=[pltpu.VMEM((2 * K, OBS, 256), F32), pltpu.VMEM((256, OBS), F32)],
    )(core, v, jacobian)


def images_kernel(core_ref, prof_ref, test_ref, jac_ref, img_ref, adj_ref, gram_ref, prof, rows, turned):
    step = pl.program_id(0)

    @pl.when(step == 0)
    def _():
        rows[...] = jnp.zeros_like(rows)
        prof[...] = jnp.zeros_like(prof)
        for p in range(2 * K):
            turned[...] = jnp.zeros_like(turned)
            turned[0:FULL, :] = prof_ref[p * FULL : (p + 1) * FULL, :].astype(F32)
            prof[:, p, :] = turned[...].T

    for o in range(GROUP):
        at = step * GROUP + o
        jac = jac_ref[o]
        r = dot(prof[at][:, 0:137].astype(BF16), jac, NT)
        back = dot(r.astype(BF16), jac)
        for p in range(2 * K):
            img_ref[p, pl.ds(at, 1), :] = r[p : p + 1, :]
        for p in range(K):
            rows[p, pl.ds(at, 1), 0:137] = back[p : p + 1, :]

    @pl.when(step == pl.num_programs(0) - 1)
    def _():
        start = pl.multiple_of(core_ref[0] * HALF, 8)
        for p in range(K):
            turned[...] = rows[p].T
            adj_ref[p * HALF : (p + 1) * HALF, :] = turned[pl.ds(start, HALF), :].astype(BF16)
        for i in range(K):
            for j in range(K):
                gram_ref[i * K + j] = jnp.sum(img_ref[i] * img_ref[j])
                gram_ref[K * K + i * K + j] = jnp.sum(img_ref[i] * test_ref[j])


def images(core, profiles, test, jacobian):
    obs, channels, levels = jacobian.shape
    return pl.pallas_call(
        images_kernel,
        grid=(obs // GROUP,),
        in_specs=[
            SMEM_SPEC,
            pl.BlockSpec((2 * K * FULL, OBS), lambda i: (0, 0)),
            pl.BlockSpec((K, OBS, channels), lambda i: (0, 0, 0)),
            pl.BlockSpec((GROUP, channels, levels), lambda i: (i, 0, 0)),
        ],
        out_specs=[
            pl.BlockSpec((2 * K, OBS, channels), lambda i: (0, 0, 0)),
            pl.BlockSpec((K * HALF, OBS), lambda i: (0, 0)),
            SMEM_SPEC,
        ],
        out_shape=[
            jax.ShapeDtypeStruct((2 * K, OBS, channels), F32),
            jax.ShapeDtypeStruct((K * HALF, OBS), BF16),
            jax.ShapeDtypeStruct((2 * K * K,), F32),
        ],
        scratch_shapes=[
            pltpu.VMEM((OBS, 8, 256), F32),
            pltpu.VMEM((K, OBS, 256), F32),
            pltpu.VMEM((256, OBS), F32),
        ],
    )(core, profiles, test, jacobian)


def outputs_kernel(coef_ref, prof_ref, test_ref, img_ref, jac_ref, q_ref, w_ref, trace_ref, prof, x, turned):
    step = pl.program_id(0)

    @pl.when(step == 0)
    def _():
        prof[...] = jnp.zeros_like(prof)
        for p in range(K):
            turned[...] = jnp.zeros_like(turned)
            turned[0:FULL, :] = prof_ref[p * FULL : (p + 1) * FULL, :].astype(F32)
            prof[:, p, :] = turned[...].T

    for o in range(GROUP):
        at = step * GROUP + o
        r = dot(prof[at][:, 0:137].astype(BF16), jac_ref[o], NT)
        for p in range(K):
            x[p, pl.ds(at, 1), :] = r[p : p + 1, :]

    @pl.when(step == pl.num_programs(0) - 1)
    def _():
        basis = []
        image_q = []
        for j in range(K):
            b = coef_ref[j * K] * img_ref[0]
            q = coef_ref[j * K] * x[0]
            for i in range(1, j + 1):
                b = b + coef_ref[j * K + i] * img_ref[i]
                q = q + coef_ref[j * K + i] * x[i]
            q_ref[j] = q
            basis.append(b)
            image_q.append(q)
        trace_q = jnp.zeros_like(image_q[0])
        trace_w = jnp.zeros_like(image_q[0])
        for j in range(K):
            trace_q = trace_q + basis[j] * image_q[j]
            w = img_ref[K + j]
            rest = test_ref[j]
            for i in range(K):
                w = w - coef_ref[K * K + i * K + j] * image_q[i]
                rest = rest - coef_ref[K * K + i * K + j] * basis[i]
            w_ref[j] = w
            trace_w = trace_w + rest * w
        trace_ref[0] = jnp.sum(trace_q)
        trace_ref[1] = jnp.sum(trace_w)


def outputs(coefs, profiles, test, img, jacobian):
    obs, channels, levels = jacobian.shape
    whole = pl.BlockSpec((K, OBS, channels), lambda i: (0, 0, 0))
    return pl.pallas_call(
        outputs_kernel,
        grid=(obs // GROUP,),
        in_specs=[
            SMEM_SPEC,
            pl.BlockSpec((K * FULL, OBS), lambda i: (0, 0)),
            whole,
            pl.BlockSpec((2 * K, OBS, channels), lambda i: (0, 0, 0)),
            pl.BlockSpec((GROUP, channels, levels), lambda i: (i, 0, 0)),
        ],
        out_specs=[whole, whole, SMEM_SPEC],
        out_shape=[
            jax.ShapeDtypeStruct((K, OBS, channels), F32),
            jax.ShapeDtypeStruct((K, OBS, channels), F32),
            jax.ShapeDtypeStruct((2,), F32),
        ],
        scratch_shapes=[
            pltpu.VMEM((OBS, 8, 256), F32),
            pltpu.VMEM((K, OBS, channels), F32),
            pltpu.VMEM((256, OBS), F32),
        ],
    )(coefs, profiles, test, img, jacobian)


def pick_kernel(tile_ref, code_ref, members_ref, out_ref):
    cells = members_ref.shape[1]
    tile = tile_ref[0].astype(F32)
    slots = lax.broadcasted_iota(jnp.int32, (CAP, OBS), 0).astype(F32)
    lanes = lax.broadcasted_iota(jnp.int32, (CAP, cells), 1).astype(F32)
    members = members_ref[...]
    for d in range(TILES):
        hi = code_ref[d, 0:1, :].astype(F32)
        lo = code_ref[d, 1:2, :].astype(F32)
        slot = code_ref[d, 2:3, :].astype(F32)
        cell = hi * 128.0 + lo - tile * float(cells)
        inside = (cell >= 0.0) & (cell < float(cells))
        here = jnp.where((slots == slot) & inside, cell + 1.0, 0.0)
        at = jnp.sum(here, axis=1, keepdims=True) - 1.0
        chosen = jnp.where(lanes == at, 1.0, 0.0).astype(BF16)
        out_ref[d * CAP : (d + 1) * CAP, :] = dot(chosen, members, NT).astype(BF16)


def pick(tile, codes, members):
    return pl.pallas_call(
        pick_kernel,
        in_specs=[SMEM_SPEC, VMEM_SPEC, VMEM_SPEC],
        out_specs=VMEM_SPEC,
        out_shape=jax.ShapeDtypeStruct((TILES * CAP, members.shape[0]), BF16),
    )(tile, codes, members)


def own_kernel(pos_ref, recv_ref, out_ref):
    rows = lax.broadcasted_iota(jnp.int32, (TILES * CAP, OBS), 0)
    chosen = jnp.where(rows == pos_ref[...], 1.0, 0.0).astype(BF16)
    out_ref[...] = dot(recv_ref[...].T, chosen).astype(BF16)


def own(position, recv):
    return pl.pallas_call(
        own_kernel,
        in_specs=[VMEM_SPEC, VMEM_SPEC],
        out_specs=VMEM_SPEC,
        out_shape=jax.ShapeDtypeStruct((recv.shape[1], OBS), BF16),
    )(position, recv)


def kernel_kernel(col_ref, code_ref, table_ref, out_ref):
    mine = col_ref[...]
    my_x = (mine // CB).astype(F32)
    my_b = mine % CB
    hot = jnp.where(lax.broadcasted_iota(jnp.int32, (OBS, CB), 1) == my_b, 1.0, 0.0).astype(BF16)
    reach = [dot(hot, table_ref[a]).astype(BF16) for a in range(STEPS + 1)]
    rows = lax.broadcasted_iota(jnp.int32, (CB, OBS), 0)
    for d in range(TILES):
        hi = code_ref[d, 0:1, :].astype(jnp.int32)
        lo = code_ref[d, 1:2, :].astype(jnp.int32)
        x = (hi * 4 + lo // CB).astype(F32)
        there = jnp.where(rows == lo % CB, 1.0, 0.0).astype(BF16)
        gap = jnp.abs(my_x - x)
        gap = jnp.minimum(gap, float(NX) - gap)
        total = jnp.zeros((OBS, OBS), F32)
        for a in range(STEPS + 1):
            total = jnp.where(gap == float(a), dot(reach[a], there), total)
        out_ref[:, d * OBS : (d + 1) * OBS] = total.astype(BF16)


def kernel_of(column, codes, table):
    return pl.pallas_call(
        kernel_kernel,
        in_specs=[VMEM_SPEC, VMEM_SPEC, VMEM_SPEC],
        out_specs=VMEM_SPEC,
        out_shape=jax.ShapeDtypeStruct((OBS, TILES * OBS), BF16),
    )(column, codes, table)


def covariance_kernel(probes, scale, all_ref, adj_ref, near_ref, own_ref, vert_ref, out_ref, prod, acc):
    group = all_ref.shape[1] // HALF
    acc[...] = jnp.zeros_like(acc)

    def pair(k, carry):
        for half in range(2):
            d = 2 * k + half
            for p in range(probes):
                adj = adj_ref[d, p * HALF : (p + 1) * HALF, :]
                for m in range(group):
                    at = (m * probes + p) * HALF
                    prod[at : at + HALF, half * OBS : (half + 1) * OBS] = (
                        all_ref[d, m * HALF : (m + 1) * HALF, :] * adj
                    )
        near = near_ref[:, pl.ds(pl.multiple_of(k * 2 * OBS, 2 * OBS), 2 * OBS)]
        acc[...] += dot(prod[...], near, NT)
        return carry

    lax.fori_loop(0, TILES // 2, pair, 0)
    vert = vert_ref[...]
    for p in range(probes):
        total = jnp.zeros((FULL, OBS), F32)
        for m in range(group):
            at = (m * probes + p) * HALF
            mixed = dot(vert, acc[at : at + HALF, :].astype(BF16))
            total = total + own_ref[m * FULL : (m + 1) * FULL, :].astype(F32) * mixed
        out_ref[p * FULL : (p + 1) * FULL, :] = (total * scale).astype(BF16)


def covariance(probes, scale, everyone, adjoints, near, mine, vert):
    rows = everyone.shape[1] * probes
    return pl.pallas_call(
        functools.partial(covariance_kernel, probes, scale),
        in_specs=[VMEM_SPEC] * 5,
        out_specs=VMEM_SPEC,
        out_shape=jax.ShapeDtypeStruct((probes * FULL, OBS), BF16),
        scratch_shapes=[pltpu.VMEM((rows, 2 * OBS), BF16), pltpu.VMEM((rows, OBS), F32)],
    )(everyone, adjoints, near, mine, vert)


def to_everyone(value, axis, peers):
    copies = jnp.broadcast_to(value[None], (peers, *value.shape))
    return lax.all_to_all(copies, axis, 0, 0, tiled=True)


def swap_cores(value, count):
    return lax.ppermute(value, "mem", [(j, j ^ 1) for j in range(count)])


def sum_over_mem(value, core, count):
    half = value.shape[0] // 2
    kept = lax.dynamic_slice_in_dim(value, core * half, half, axis=0)
    sent = lax.dynamic_slice_in_dim(value, (1 - core) * half, half, axis=0)
    kept = (kept.astype(F32) + swap_cores(sent, count).astype(F32)).astype(BF16)
    others = [
        lax.ppermute(kept, "mem", [(j, (j + 2 * k) % count) for j in range(count)])
        for k in range(1, count // 2)
    ]
    total = (kept.astype(F32) + others[1].astype(F32)) + (
        others[0].astype(F32) + others[2].astype(F32)
    )
    total = total.astype(BF16)
    other = swap_cores(total, count)
    first = jnp.where(core == 0, total, other)
    second = jnp.where(core == 0, other, total)
    return jnp.concatenate([first, second], axis=0)


def in_three(value):
    hi = lax.reduce_precision(value, 8, 7)
    mid = lax.reduce_precision(value - hi, 8, 7)
    low = value - hi - mid
    return hi.astype(BF16), mid.astype(BF16), low.astype(BF16)


def on_device(members, vertical, jacobian, sketch_bits, test_bits, obs_column, obs_slot):
    count = lax.axis_size("mem")
    core = lax.axis_index("mem") % 2
    core1 = core.astype(jnp.int32).reshape(1)
    my_tile = lax.axis_index(TILE).astype(jnp.int32)
    local, levels, cells = members.shape
    channels = jacobian.shape[1]
    ensemble = local * count
    size = float(OBS * TILES * channels)
    scale = 1.0 / ((ensemble - 1) * 5.0**STEPS * WALK_SCALE)

    padded = jnp.pad(members, ((0, 0), (0, FULL - levels), (0, 0)))
    kept = lax.dynamic_slice_in_dim(padded, core * HALF, HALF, axis=1)
    sent = lax.dynamic_slice_in_dim(padded, (1 - core) * HALF, HALF, axis=1)
    got = swap_cores(sent, count)
    four = jnp.concatenate(
        [jnp.where(core == 0, kept, got), jnp.where(core == 0, got, kept)], axis=0
    ).reshape(2 * local * HALF, cells)

    signs = jnp.concatenate([2 * sketch_bits - 1, 2 * test_bits - 1], axis=0)
    test = (2 * test_bits - 1).astype(F32)
    v = jnp.pad(jnp.swapaxes(signs, 0, 1).astype(BF16), ((0, 0), (0, 2), (0, 0)))
    adjoints = sign_adjoints(core1, v, jacobian)
    codes = jnp.stack([obs_column // 128, obs_column % 128, obs_slot]).astype(BF16)
    codes = jnp.pad(codes, ((0, 5), (0, 0)))
    first = to_everyone(jnp.concatenate([adjoints, codes], axis=0), TILE, TILES)
    codes = first[:, 2 * K * HALF :, :]

    picked = pick(my_tile.reshape(1), codes, four)
    arrived = lax.all_to_all(picked.reshape(TILES, CAP, -1), TILE, 0, 0, tiled=True)
    position = (obs_column // cells * CAP + obs_slot).reshape(1, OBS)
    mine = own(position, arrived.reshape(TILES * CAP, -1))
    near = kernel_of(obs_column.reshape(OBS, 1), codes, jnp.asarray(walk_table(), BF16))
    partner = swap_cores(mine, count)
    low = jnp.where(core == 0, mine, partner).reshape(2 * local, HALF, OBS)
    high = jnp.where(core == 0, partner, mine).reshape(2 * local, HALF, OBS)
    both = jnp.concatenate([low, high], axis=1).reshape(2 * local * FULL, OBS)
    everyone = to_everyone(mine, TILE, TILES)

    vert = jnp.pad(vertical, ((0, FULL - levels), (0, FULL - levels)))
    vert = lax.dynamic_slice_in_dim(vert, core * HALF, HALF, axis=1)

    part = covariance(2 * K, scale, everyone, first, near, both, vert)
    profiles = sum_over_mem(part, core, count)
    img, back, gram = images(core1, profiles, test, jacobian)

    parts = jnp.stack(in_three(gram))
    parts = jnp.pad(parts, ((0, 5), (0, OBS - parts.shape[1])))
    second = to_everyone(jnp.concatenate([back, parts], axis=0), TILE, TILES)
    gram = second[:, K * HALF : K * HALF + 3, : 2 * K * K].astype(F32).sum(axis=(0, 1))
    part = covariance(K, scale, everyone, second, near, both, vert)
    profiles = sum_over_mem(part, core, count)

    g = [[gram[i * K + j] for j in range(K)] for i in range(K)]
    c = [[gram[K * K + i * K + j] for j in range(K)] for i in range(K)]
    l00 = jnp.sqrt(g[0][0])
    l10, l20 = g[1][0] / l00, g[2][0] / l00
    l11 = jnp.sqrt(g[1][1] - l10 * l10)
    l21 = (g[2][1] - l20 * l10) / l11
    l22 = jnp.sqrt(g[2][2] - l20 * l20 - l21 * l21)
    i00, i11, i22 = 1.0 / l00, 1.0 / l11, 1.0 / l22
    i10 = -l10 * i00 * i11
    i21 = -l21 * i11 * i22
    i20 = -(l20 * i00 + l21 * i10) * i22
    zero = jnp.zeros((), F32)
    root = size**0.5
    inv = [[i00, zero, zero], [i10, i11, zero], [i20, i21, i22]]
    coefs = [root * inv[j][i] for j in range(K) for i in range(K)]
    coefs += [
        sum(inv[i][k] * c[k][j] for k in range(i + 1)) / root for i in range(K) for j in range(K)
    ]
    image_q, image_w, traces = outputs(jnp.stack(coefs), profiles, test, img, jacobian)
    traces = to_everyone(jnp.pad(traces, (0, OBS - 2)).reshape(1, OBS), TILE, TILES)
    traces = traces.sum(axis=(0, 1))
    trace_q, trace_w = traces[0], traces[1]
    trace_mean = trace_q / (size * size) + trace_w / (K * size)
    return (image_q, image_w, trace_mean, trace_q / (K * size))


def solution(mesh):
    finer = Mesh(mesh.devices.reshape(mesh.shape["mem"], 4, 4), ("mem", "tile_0", "tile_1"))
    return jax.shard_map(
        on_device,
        mesh=finer,
        in_specs=(
            P("mem", None, TILE),
            P(),
            P(TILE, None, None),
            P(None, TILE, None),
            P(None, TILE, None),
            P(TILE),
            P(TILE),
        ),
        out_specs=(P(None, TILE, None), P(None, TILE, None), P(), P()),
        check_vma=False,
    )
```

```python
import functools

import jax
import jax.numpy as jnp
import numpy as np
from jax import lax
from jax.experimental import pallas as pl
from jax.experimental.pallas import tpu as pltpu
from jax.sharding import Mesh
from jax.sharding import PartitionSpec as P

CB = 32
NX = 256
K = 3
STEPS = 6
TILE = ("tile_0", "tile_1")
TILES = 16
SLICES = 8
LEVELS = 137
SLICE = 18
FULL = SLICES * SLICE
MEMBERS = 16
CAP = 32
OBS = 128
CHAN = 231
CPAD = 240
BLOCK = 9
BLOCKS = -(-LEVELS // BLOCK)
REST = LEVELS - (BLOCKS - 1) * BLOCK
CODES = 112
FIRST = 120
GRAMS = 56
SECOND = 64


F32 = jnp.float32
BF16 = jnp.bfloat16
VMEM_SPEC = pl.BlockSpec(memory_space=pltpu.VMEM)
SMEM_SPEC = pl.BlockSpec(memory_space=pltpu.SMEM)
NT = (((1,), (1,)), ((), ()))

WALK_SCALE = 1.3338


def walk_table():
    walks = np.zeros((2 * STEPS + 1, 2 * STEPS + 1))
    walks[STEPS, STEPS] = 1
    for _ in range(STEPS):
        grown = walks.copy()
        grown[1:] += walks[:-1]
        grown[:-1] += walks[1:]
        grown[:, 1:] += walks[:, :-1]
        grown[:, :-1] += walks[:, 1:]
        walks = grown

    def count(a, d):
        return walks[STEPS + a, STEPS + d] if d <= STEPS else 0.0

    table = np.zeros((STEPS + 1, CB, CB), np.float32)
    for a in range(STEPS + 1):
        for b in range(CB):
            for c in range(CB):
                table[a, b, c] = (
                    count(a, abs(b - c)) + count(a, b + c + 1) + count(a, 2 * CB - 1 - b - c)
                )
    return table * WALK_SCALE


def dot(a, b, dims=(((1,), (0,)), ((), ()))):
    return lax.dot_general(a, b, dims, preferred_element_type=F32)


def channel_chunks():
    return [(c, min(16, CHAN - c)) for c in range(0, CHAN, 16)]


def jac_rows(jac_ref, level, c, width):
    rows = jac_ref[level, c : c + width, :].astype(F32)
    if width % 8:
        fill = jnp.zeros((8 - width % 8, OBS), F32)
        rows = jnp.concatenate([rows, fill], axis=0)
    return [rows[k : k + 8] for k in range(0, rows.shape[0], 8)]


def back_block(jac_ref, vec_ref, probes, first, valid, put):
    for low in range(0, BLOCK, 3):
        acc = {}
        for c, width in channel_chunks():
            vecs = [
                [vec_ref[p, c + 8 * k : c + 8 * k + 8, :] for k in range(-(-width // 8))]
                for p in range(probes)
            ]
            for level in range(low, low + 3):
                for k, rows in enumerate(jac_rows(jac_ref, level, c, width)):
                    for p in range(probes):
                        term = rows * vecs[p][k]
                        acc[p, level] = acc[p, level] + term if (p, level) in acc else term
        for level in range(low, low + 3):
            for p in range(probes):
                row = jnp.sum(acc[p, level], axis=0, keepdims=True)
                put(p, level, jnp.where(first + level < valid, row, 0.0))


def forward_block(jac_ref, prof_ref, img_ref, probes, first, count):
    weights = [
        [
            jnp.broadcast_to(prof_ref[pl.ds(p * FULL + first + level, 1), :], (8, OBS))
            for level in range(count)
        ]
        for p in range(probes)
    ]
    for c, width in channel_chunks():
        parts = -(-width // 8)
        acc = [
            [img_ref[p, c + 8 * k : c + 8 * k + 8, :] for k in range(parts)] for p in range(probes)
        ]
        for level in range(count):
            for k, rows in enumerate(jac_rows(jac_ref, level, c, width)):
                for p in range(probes):
                    acc[p][k] = acc[p][k] + rows * weights[p][level]
        for p in range(probes):
            for k in range(parts):
                img_ref[p, c + 8 * k : c + 8 * k + 8, :] = acc[p][k]


def forward_step(step, jac_ref, prof_ref, img_ref, probes):
    @pl.when(step < BLOCKS - 1)
    def _():
        forward_block(jac_ref, prof_ref, img_ref, probes, step * BLOCK, BLOCK)

    @pl.when(step == BLOCKS - 1)
    def _():
        forward_block(jac_ref, prof_ref, img_ref, probes, step * BLOCK, REST)


def copies(out_ref, message):
    message = message.astype(BF16)
    for d in range(TILES):
        out_ref[d] = message


def signs_kernel(slice_ref, sketch_ref, test_ref, codes_ref, jac_ref, out_ref, vec, rows):
    step = pl.program_id(0)

    @pl.when(step == 0)
    def _():
        rows[...] = jnp.zeros_like(rows)
        vec[...] = jnp.zeros_like(vec)
        for p in range(K):
            vec[p, 0:CHAN, :] = (2 * sketch_ref[p] - 1).astype(F32)
            vec[K + p, 0:CHAN, :] = (2 * test_ref[p] - 1).astype(F32)
        rows[CODES:FIRST, :] = codes_ref[...]

    def put(p, level, row):
        rows[pl.ds(p * SLICE + step * BLOCK + level, 1), :] = row

    first = slice_ref[0] * SLICE + step * BLOCK
    back_block(jac_ref, vec, 2 * K, first, LEVELS, put)

    @pl.when(step == pl.num_programs(0) - 1)
    def _():
        copies(out_ref, rows[...])


def whole(*shape):
    return pl.BlockSpec(shape, lambda i, *_: (0,) * len(shape))


def sign_adjoints(part, sketch, test, codes, jac):
    return pl.pallas_call(
        signs_kernel,
        grid_spec=pltpu.PrefetchScalarGridSpec(
            num_scalar_prefetch=1,
            grid=(2,),
            in_specs=[
                whole(K, CHAN, OBS),
                whole(K, CHAN, OBS),
                whole(8, OBS),
                pl.BlockSpec((BLOCK, CHAN, OBS), lambda i, s: (s[0] * 2 + i, 0, 0)),
            ],
            out_specs=whole(TILES, FIRST, OBS),
            scratch_shapes=[pltpu.VMEM((2 * K, CPAD, OBS), F32), pltpu.VMEM((FIRST, OBS), F32)],
        ),
        out_shape=jax.ShapeDtypeStruct((TILES, FIRST, OBS), BF16),
        cost_estimate=pl.CostEstimate(flops=10**7, bytes_accessed=2 * 10**6, transcendentals=0),
    )(part, sketch, test, codes, jac)


def images_kernel(part_ref, mine_ref, other_ref, test_ref, jac_ref, img_ref, out_ref, prof, rows):
    step = pl.program_id(0)

    @pl.when(step == 0)
    def _():
        core = part_ref[0] % 2
        rows[...] = jnp.zeros_like(rows)
        img_ref[...] = jnp.zeros_like(img_ref)
        prof[...] = jnp.where(core == 0, mine_ref[...].astype(F32), other_ref[...].astype(F32))

    forward_step(step, jac_ref, prof, img_ref, K)

    @pl.when(step >= BLOCKS)
    def _():
        def put(p, level, row):
            rows[pl.ds(p * SLICE + (step - BLOCKS) * BLOCK + level, 1), :] = row

        first = part_ref[0] * SLICE + (step - BLOCKS) * BLOCK
        back_block(jac_ref, img_ref, K, first, LEVELS, put)

    @pl.when(step == BLOCKS + 1)
    def _():
        lanes = lax.broadcasted_iota(jnp.int32, (1, OBS), 1)
        gram = jnp.zeros((1, OBS), F32)
        for i in range(K):
            for j in range(K):
                if j <= i:
                    value = jnp.sum(img_ref[i] * img_ref[j])
                    gram = jnp.where(lanes == i * K + j, value, gram)
                signs = (2 * test_ref[j] - 1).astype(F32)
                value = jnp.sum(img_ref[i, 0:CHAN, :] * signs)
                gram = jnp.where(lanes == K * K + i * K + j, value, gram)
        high = gram.astype(BF16).astype(F32)
        mid = (gram - high).astype(BF16).astype(F32)
        rows[GRAMS : GRAMS + 1, :] = high
        rows[GRAMS + 1 : GRAMS + 2, :] = mid
        rows[GRAMS + 2 : GRAMS + 3, :] = gram - high - mid
        copies(out_ref, rows[...])


def images(part, mine, other, test, jac):
    return pl.pallas_call(
        images_kernel,
        grid_spec=pltpu.PrefetchScalarGridSpec(
            num_scalar_prefetch=1,
            grid=(BLOCKS + 2,),
            in_specs=[
                whole(K * FULL, OBS),
                whole(K * FULL, OBS),
                whole(K, CHAN, OBS),
                pl.BlockSpec(
                    (BLOCK, CHAN, OBS),
                    lambda i, s: (jnp.where(i < BLOCKS, i, s[0] * 2 + i - BLOCKS), 0, 0),
                ),
            ],
            out_specs=[whole(K, CPAD, OBS), whole(TILES, SECOND, OBS)],
            scratch_shapes=[pltpu.VMEM((K * FULL, OBS), F32), pltpu.VMEM((SECOND, OBS), F32)],
        ),
        out_shape=[
            jax.ShapeDtypeStruct((K, CPAD, OBS), F32),
            jax.ShapeDtypeStruct((TILES, SECOND, OBS), BF16),
        ],
        cost_estimate=pl.CostEstimate(flops=4 * 10**7, bytes_accessed=10**7, transcendentals=0),
    )(part, mine, other, test, jac)


def test_images_kernel(part_ref, mine_ref, other_ref, jac_ref, img_ref, prof):
    step = pl.program_id(0)

    @pl.when(step == 0)
    def _():
        core = part_ref[0] % 2
        img_ref[...] = jnp.zeros_like(img_ref)
        prof[...] = jnp.where(core == 0, other_ref[...].astype(F32), mine_ref[...].astype(F32))

    forward_step(step, jac_ref, prof, img_ref, K)


def test_images(part, mine, other, jac):
    return pl.pallas_call(
        test_images_kernel,
        grid_spec=pltpu.PrefetchScalarGridSpec(
            num_scalar_prefetch=1,
            grid=(BLOCKS,),
            in_specs=[
                whole(K * FULL, OBS),
                whole(K * FULL, OBS),
                pl.BlockSpec((BLOCK, CHAN, OBS), lambda i, s: (i, 0, 0)),
            ],
            out_specs=whole(K, CPAD, OBS),
            scratch_shapes=[pltpu.VMEM((K * FULL, OBS), F32)],
        ),
        out_shape=jax.ShapeDtypeStruct((K, CPAD, OBS), F32),
        cost_estimate=pl.CostEstimate(flops=4 * 10**7, bytes_accessed=10**7, transcendentals=0),
    )(part, mine, other, jac)


def outputs_kernel(
    size, part_ref, mine_ref, other_ref, second_ref, test_ref, y_ref, z_ref, jac_ref,
    q_ref, w_ref, trace_ref, prof, x,
):
    step = pl.program_id(0)
    half = K * FULL // 2

    @pl.when(step == 0)
    def _():
        core = part_ref[0] % 2
        mine, other = mine_ref[...].astype(F32), other_ref[...].astype(F32)
        x[...] = jnp.zeros_like(x)
        prof[0:half, :] = jnp.where(core == 0, mine, other)
        prof[half:, :] = jnp.where(core == 0, other, mine)

    forward_step(step, jac_ref, prof, x, K)

    @pl.when(step == BLOCKS - 1)
    def _():
        total = jnp.zeros((1, OBS), F32)
        for d in range(TILES):
            got = second_ref[d, GRAMS : GRAMS + 8, :].astype(F32)
            total = total + jnp.sum(got, axis=0, keepdims=True)
        lanes = lax.broadcasted_iota(jnp.int32, (1, OBS), 1)

        def entry(k):
            return jnp.sum(jnp.where(lanes == k, total, 0.0), axis=1, keepdims=True)

        g = [[entry(i * K + j) for j in range(i + 1)] for i in range(K)]
        c = [[entry(K * K + i * K + j) for j in range(K)] for i in range(K)]
        l00 = jnp.sqrt(g[0][0])
        l10, l20 = g[1][0] / l00, g[2][0] / l00
        l11 = jnp.sqrt(g[1][1] - l10 * l10)
        l21 = (g[2][1] - l20 * l10) / l11
        l22 = jnp.sqrt(g[2][2] - l20 * l20 - l21 * l21)
        i00, i11, i22 = 1.0 / l00, 1.0 / l11, 1.0 / l22
        i10 = -l10 * i00 * i11
        i21 = -l21 * i11 * i22
        i20 = -(l20 * i00 + l21 * i10) * i22
        inv = [[i00], [i10, i11], [i20, i21, i22]]
        root = size**0.5
        basis, image_q = [], []
        for j in range(K):
            b = q = None
            for i in range(j + 1):
                by, qx = root * inv[j][i] * y_ref[i, 0:CHAN, :], root * inv[j][i] * x[i, 0:CHAN, :]
                b, q = (by, qx) if b is None else (b + by, q + qx)
            q_ref[j] = q
            basis.append(b)
            image_q.append(q)
        trace_q = trace_w = None
        for j in range(K):
            w = z_ref[j, 0:CHAN, :]
            rest = (2 * test_ref[j] - 1).astype(F32)
            for i in range(K):
                share = sum(inv[i][k] * c[k][j] for k in range(i + 1)) / root
                w = w - share * image_q[i]
                rest = rest - share * basis[i]
            w_ref[j] = w
            tq, tw = basis[j] * image_q[j], rest * w
            trace_q, trace_w = (tq, tw) if trace_q is None else (trace_q + tq, trace_w + tw)
        row = jnp.where(lanes == 0, jnp.sum(trace_q), jnp.sum(trace_w))
        for d in range(TILES):
            trace_ref[d] = jnp.broadcast_to(row, (8, OBS))


def outputs(size, part, mine, other, second, test, y, z, jac):
    return pl.pallas_call(
        functools.partial(outputs_kernel, size),
        grid_spec=pltpu.PrefetchScalarGridSpec(
            num_scalar_prefetch=1,
            grid=(BLOCKS,),
            in_specs=[
                whole(K * FULL // 2, OBS),
                whole(K * FULL // 2, OBS),
                whole(TILES, SECOND, OBS),
                whole(K, CHAN, OBS),
                whole(K, CPAD, OBS),
                whole(K, CPAD, OBS),
                pl.BlockSpec((BLOCK, CHAN, OBS), lambda i, s: (i, 0, 0)),
            ],
            out_specs=[whole(K, CHAN, OBS), whole(K, CHAN, OBS), whole(TILES, 8, OBS)],
            scratch_shapes=[pltpu.VMEM((K * FULL, OBS), F32), pltpu.VMEM((K, CPAD, OBS), F32)],
        ),
        out_shape=[
            jax.ShapeDtypeStruct((K, CHAN, OBS), F32),
            jax.ShapeDtypeStruct((K, CHAN, OBS), F32),
            jax.ShapeDtypeStruct((TILES, 8, OBS), F32),
        ],
        cost_estimate=pl.CostEstimate(flops=4 * 10**7, bytes_accessed=10**7, transcendentals=0),
    )(part, mine, other, second, test, y, z, jac)


def pick_kernel(tile_ref, first_ref, members_ref, out_ref):
    cells = members_ref.shape[1]
    tile = tile_ref[0].astype(F32)
    slots = lax.broadcasted_iota(jnp.int32, (CAP, OBS), 0).astype(F32)
    lanes = lax.broadcasted_iota(jnp.int32, (CAP, cells), 1).astype(F32)
    members = members_ref[...]
    for d in range(TILES):
        codes = first_ref[d, CODES:FIRST, :].astype(F32)
        cell = codes[0:1] * 128.0 + codes[1:2] - tile * float(cells)
        inside = (cell >= 0.0) & (cell < float(cells))
        here = jnp.where((slots == codes[2:3]) & inside, cell + 1.0, 0.0)
        at = jnp.sum(here, axis=1, keepdims=True) - 1.0
        chosen = jnp.where(lanes == at, 1.0, 0.0).astype(BF16)
        out_ref[d * CAP : (d + 1) * CAP, :] = dot(chosen, members, NT).astype(BF16)


def pick(tile, first, members):
    return pl.pallas_call(
        pick_kernel,
        in_specs=[SMEM_SPEC, VMEM_SPEC, VMEM_SPEC],
        out_specs=VMEM_SPEC,
        out_shape=jax.ShapeDtypeStruct((TILES * CAP, members.shape[0]), BF16),
    )(tile, first, members)


def own_kernel(pos_ref, recv_ref, out_ref, all_ref):
    rows = lax.broadcasted_iota(jnp.int32, (TILES * CAP, OBS), 0)
    chosen = jnp.where(rows == pos_ref[...], 1.0, 0.0).astype(BF16)
    mine = dot(recv_ref[...].T, chosen)
    out_ref[...] = mine.astype(BF16)
    copies(all_ref, mine)


def own(position, recv):
    rows = recv.shape[1]
    return pl.pallas_call(
        own_kernel,
        in_specs=[VMEM_SPEC, VMEM_SPEC],
        out_specs=[VMEM_SPEC, VMEM_SPEC],
        out_shape=[
            jax.ShapeDtypeStruct((rows, OBS), BF16),
            jax.ShapeDtypeStruct((TILES, rows, OBS), BF16),
        ],
    )(position, recv)


def near_kernel(col_ref, first_ref, table_ref, out_ref):
    mine = col_ref[...]
    my_x = (mine // CB).astype(F32)
    my_b = mine % CB
    hot = jnp.where(lax.broadcasted_iota(jnp.int32, (OBS, CB), 1) == my_b, 1.0, 0.0).astype(BF16)
    reach = [dot(hot, table_ref[a]).astype(BF16) for a in range(STEPS + 1)]
    rows = lax.broadcasted_iota(jnp.int32, (CB, OBS), 0)
    for d in range(TILES):
        codes = first_ref[d, CODES:FIRST, :].astype(F32).astype(jnp.int32)
        hi, lo = codes[0:1], codes[1:2]
        x = (hi * 4 + lo // CB).astype(F32)
        there = jnp.where(rows == lo % CB, 1.0, 0.0).astype(BF16)
        gap = jnp.abs(my_x - x)
        gap = jnp.minimum(gap, float(NX) - gap)
        total = jnp.zeros((OBS, OBS), F32)
        for a in range(STEPS + 1):
            total = jnp.where(gap == float(a), dot(reach[a], there), total)
        out_ref[:, d * OBS : (d + 1) * OBS] = total.astype(BF16)


def near_of(column, first, table):
    return pl.pallas_call(
        near_kernel,
        in_specs=[VMEM_SPEC, VMEM_SPEC, VMEM_SPEC],
        out_specs=VMEM_SPEC,
        out_shape=jax.ShapeDtypeStruct((OBS, TILES * OBS), BF16),
        cost_estimate=pl.CostEstimate(flops=2 * 10**7, bytes_accessed=4 * 10**6, transcendentals=0),
    )(column, first, table)


def covariance_kernel(
    probes, scale, part_ref, all_ref, adj_ref, near_ref, own_ref, vert_ref, keep_ref, send_ref,
    prod, acc, adj, mem, out,
):
    rows = SLICE * MEMBERS
    mem[...] = own_ref[...].astype(F32)

    def pair(k, carry):
        for half in range(2):
            d = 2 * k + half
            adj[...] = adj_ref[d].astype(F32)
            for level in range(SLICE):
                values = all_ref[d, level * MEMBERS : (level + 1) * MEMBERS, :]
                for p in range(probes):
                    at = p * SLICE + level
                    row = jnp.broadcast_to(adj[at : at + 1, :], (MEMBERS, OBS)).astype(BF16)
                    prod[at * MEMBERS : (at + 1) * MEMBERS, half * OBS : (half + 1) * OBS] = (
                        values * row
                    )
        near = near_ref[:, pl.ds(pl.multiple_of(k * 2 * OBS, 2 * OBS), 2 * OBS)]
        acc[...] += dot(prod[...], near, NT)
        return carry

    acc[...] = jnp.zeros_like(acc)
    lax.fori_loop(0, TILES // 2, pair, 0)
    vert = vert_ref[...]
    for p in range(probes):
        total = None
        for m in range(MEMBERS):
            smooth = acc[pl.ds(p * rows + m, SLICE, stride=MEMBERS), :].astype(BF16)
            term = mem[pl.ds(m, FULL, stride=MEMBERS), :] * dot(vert, smooth)
            total = term if total is None else total + term
        out[p * FULL : (p + 1) * FULL, :] = total * scale
    half = probes * FULL // 2
    core = part_ref[0] % 2
    low, high = out[0:half, :], out[half:, :]
    keep_ref[...] = jnp.where(core == 0, low, high).astype(BF16)
    send_ref[...] = jnp.where(core == 0, high, low).astype(BF16)


def covariance(probes, scale, part, everyone, adjoints, near, mine, vert):
    rows = SLICE * MEMBERS
    half = jax.ShapeDtypeStruct((probes * FULL // 2, OBS), BF16)
    return pl.pallas_call(
        functools.partial(covariance_kernel, probes, scale),
        in_specs=[SMEM_SPEC] + [VMEM_SPEC] * 5,
        out_specs=[VMEM_SPEC, VMEM_SPEC],
        out_shape=[half, half],
        scratch_shapes=[
            pltpu.VMEM((probes * rows, 2 * OBS), BF16),
            pltpu.VMEM((probes * rows, OBS), F32),
            pltpu.VMEM((adjoints.shape[1], OBS), F32),
            pltpu.VMEM((FULL * MEMBERS, OBS), F32),
            pltpu.VMEM((probes * FULL, OBS), F32),
        ],
    )(part, everyone, adjoints, near, mine, vert)


def exchange(value, axis):
    return lax.all_to_all(value, axis, 0, 0, tiled=True)


def swap_cores(value):
    return lax.ppermute(value, "mem", [(j, j ^ 1) for j in range(SLICES)])


def from_other_chips(value):
    return [
        lax.ppermute(value, "mem", [(j, (j + 2 * k) % SLICES) for j in range(SLICES)])
        for k in range(1, SLICES // 2)
    ]


def sum_over_mem(keep, send):
    kept = (keep.astype(F32) + swap_cores(send).astype(F32)).astype(BF16)
    others = from_other_chips(kept)
    total = (kept.astype(F32) + others[1].astype(F32)) + (
        others[0].astype(F32) + others[2].astype(F32)
    )
    total = total.astype(BF16)
    return total, swap_cores(total)


def on_device(members, vertical, jacobian, sketch_bits, test_bits, obs_column, obs_slot):
    slice_id = lax.axis_index("mem").astype(jnp.int32)
    part = slice_id.reshape(1)
    my_tile = lax.axis_index(TILE).astype(jnp.int32)
    local, levels, cells = members.shape
    size = float(OBS * TILES * CHAN)
    scale = 1.0 / ((MEMBERS - 1) * 5.0**STEPS * WALK_SCALE)

    padded = jnp.pad(jnp.swapaxes(members, 0, 1), ((0, FULL - levels), (0, 0), (0, 0)))
    sliced = exchange(padded.reshape(SLICES, SLICE * local, cells), "mem")
    sliced = jnp.swapaxes(sliced.reshape(SLICES, SLICE, local, cells), 0, 1)
    sliced = sliced.reshape(SLICE * MEMBERS, cells)

    jac = jnp.transpose(jacobian, (2, 1, 0))
    sketch = jnp.swapaxes(sketch_bits, 1, 2)
    test = jnp.swapaxes(test_bits, 1, 2)
    codes = jnp.stack([obs_column // 128, obs_column % 128, obs_slot]).astype(F32)
    codes = jnp.pad(codes, ((0, 5), (0, 0)))
    first = exchange(sign_adjoints(part, sketch, test, codes, jac), TILE)

    picked = pick(my_tile.reshape(1), first, sliced)
    arrived = exchange(picked.reshape(TILES, CAP, -1), TILE)
    position = (obs_column // cells * CAP + obs_slot).reshape(1, OBS)
    mine, everyone = own(position, arrived.reshape(TILES * CAP, -1))
    everyone = exchange(everyone, TILE)
    near = near_of(obs_column.reshape(OBS, 1), first, jnp.asarray(walk_table(), BF16))
    both = exchange(jnp.broadcast_to(mine[None], (SLICES, *mine.shape)), "mem")
    both = both.reshape(FULL * MEMBERS, OBS)

    vert = jnp.pad(vertical, ((0, FULL - levels), (0, FULL - levels)))
    vert = lax.dynamic_slice_in_dim(vert, slice_id * SLICE, SLICE, axis=1)

    halves = covariance(2 * K, scale, part, everyone, first, near, both, vert)
    mine_1, other_1 = sum_over_mem(*halves)
    y, second = images(part, mine_1, other_1, test, jac)
    second = exchange(second, TILE)
    z = test_images(part, mine_1, other_1, jac)
    halves = covariance(K, scale, part, everyone, second, near, both, vert)
    mine_2, other_2 = sum_over_mem(*halves)
    image_q, image_w, traces = outputs(size, part, mine_2, other_2, second, test, y, z, jac)
    traces = exchange(traces, TILE)[:, 0, :].sum(axis=0)
    trace_q, trace_w = traces[0], traces[1]
    trace_mean = trace_q / (size * size) + trace_w / (K * size)
    return (
        jnp.swapaxes(image_q, 1, 2),
        jnp.swapaxes(image_w, 1, 2),
        trace_mean,
        trace_q / (K * size),
    )


def solution(mesh):
    finer = Mesh(mesh.devices.reshape(mesh.shape["mem"], 4, 4), ("mem", "tile_0", "tile_1"))
    return jax.shard_map(
        on_device,
        mesh=finer,
        in_specs=(
            P("mem", None, TILE),
            P(),
            P(TILE, None, None),
            P(None, TILE, None),
            P(None, TILE, None),
            P(TILE),
            P(TILE),
        ),
        out_specs=(P(None, TILE, None), P(None, TILE, None), P(), P()),
        check_vma=False,
    )
```

```python
import functools

import jax
import jax.numpy as jnp
import numpy as np
from jax import lax
from jax.experimental import pallas as pl
from jax.experimental.pallas import tpu as pltpu
from jax.sharding import Mesh
from jax.sharding import PartitionSpec as P

CB = 32
NX = 256
K = 3
STEPS = 6
TILE = ("tile_0", "tile_1")
TILES = 16
SLICES = 8
LEVELS = 137
SLICE = 18
FULL = SLICES * SLICE
MEMBERS = 16
CAP = 32
OBS = 128
CHAN = 231
CPAD = 240
BLOCK = 9
BLOCKS = -(-LEVELS // BLOCK)
REST = LEVELS - (BLOCKS - 1) * BLOCK
CODES = 112
FIRST = 120
GRAMS = 56
SECOND = 64


F32 = jnp.float32
BF16 = jnp.bfloat16
VMEM_SPEC = pl.BlockSpec(memory_space=pltpu.VMEM)
SMEM_SPEC = pl.BlockSpec(memory_space=pltpu.SMEM)
NT = (((1,), (1,)), ((), ()))

WALK_SCALE = 1.3338


def walk_table():
    walks = np.zeros((2 * STEPS + 1, 2 * STEPS + 1))
    walks[STEPS, STEPS] = 1
    for _ in range(STEPS):
        grown = walks.copy()
        grown[1:] += walks[:-1]
        grown[:-1] += walks[1:]
        grown[:, 1:] += walks[:, :-1]
        grown[:, :-1] += walks[:, 1:]
        walks = grown

    def count(a, d):
        return walks[STEPS + a, STEPS + d] if d <= STEPS else 0.0

    table = np.zeros((STEPS + 1, CB, CB), np.float32)
    for a in range(STEPS + 1):
        for b in range(CB):
            for c in range(CB):
                table[a, b, c] = (
                    count(a, abs(b - c)) + count(a, b + c + 1) + count(a, 2 * CB - 1 - b - c)
                )
    return table * WALK_SCALE


def dot(a, b, dims=(((1,), (0,)), ((), ()))):
    return lax.dot_general(a, b, dims, preferred_element_type=F32)


def channel_chunks():
    return [(c, min(16, CHAN - c)) for c in range(0, CHAN, 16)]


def jac_rows(jac_ref, level, c, width):
    rows = jac_ref[level, c : c + width, :].astype(F32)
    if width % 8:
        fill = jnp.zeros((8 - width % 8, OBS), F32)
        rows = jnp.concatenate([rows, fill], axis=0)
    return [rows[k : k + 8] for k in range(0, rows.shape[0], 8)]


def back_rows(jac_ref, base, vec_ref, probes, first, put):
    def trio(t, carry):
        levels = [jnp.minimum(first + 3 * t + k, LEVELS - 1) - base for k in range(3)]
        acc = {}
        for c, width in channel_chunks():
            vecs = [
                [vec_ref[p, c + 8 * k : c + 8 * k + 8, :] for k in range(-(-width // 8))]
                for p in range(probes)
            ]
            for n, level in enumerate(levels):
                for k, rows in enumerate(jac_rows(jac_ref, level, c, width)):
                    for p in range(probes):
                        term = rows * vecs[p][k]
                        acc[p, n] = acc[p, n] + term if (p, n) in acc else term
        for n in range(3):
            valid = first + 3 * t + n < LEVELS
            for p in range(probes):
                row = jnp.sum(acc[p, n], axis=0, keepdims=True)
                put(p, 3 * t + n, jnp.where(valid, row, 0.0))
        return carry

    lax.fori_loop(0, SLICE // 3, trio, 0)


def forward_block(jac_ref, prof_ref, img_ref, probes, first, count):
    weights = [
        [
            jnp.broadcast_to(prof_ref[pl.ds(p * FULL + first + level, 1), :], (8, OBS))
            for level in range(count)
        ]
        for p in range(probes)
    ]
    for c, width in channel_chunks():
        parts = -(-width // 8)
        acc = [
            [img_ref[p, c + 8 * k : c + 8 * k + 8, :] for k in range(parts)] for p in range(probes)
        ]
        for level in range(count):
            for k, rows in enumerate(jac_rows(jac_ref, first + level, c, width)):
                for p in range(probes):
                    acc[p][k] = acc[p][k] + rows * weights[p][level]
        for p in range(probes):
            for k in range(parts):
                img_ref[p, c + 8 * k : c + 8 * k + 8, :] = acc[p][k]


def jac_copy(jac_hbm, jac_ref, sems, k, count=BLOCK):
    levels = pl.ds(k * BLOCK, count)
    return pltpu.make_async_copy(jac_hbm.at[levels], jac_ref.at[levels], sems.at[k])


def start_jac(jac_hbm, jac_ref, sems):
    for k in range(BLOCKS):
        jac_copy(jac_hbm, jac_ref, sems, k, BLOCK if k < BLOCKS - 1 else REST).start()


def forward(jac_hbm, jac_ref, sems, prof_ref, img_ref, probes):
    def block(k, carry):
        jac_copy(jac_hbm, jac_ref, sems, k).wait()
        forward_block(jac_ref, prof_ref, img_ref, probes, k * BLOCK, BLOCK)
        return carry

    lax.fori_loop(0, BLOCKS - 1, block, 0)
    jac_copy(jac_hbm, jac_ref, sems, BLOCKS - 1, REST).wait()
    forward_block(jac_ref, prof_ref, img_ref, probes, (BLOCKS - 1) * BLOCK, REST)


JAC_SCRATCH = [pltpu.VMEM((LEVELS, CHAN, OBS), BF16), pltpu.SemaphoreType.DMA((BLOCKS,))]
ANY_SPEC = pl.BlockSpec(memory_space=pl.ANY)
COST = pl.CostEstimate(flops=4 * 10**7, bytes_accessed=10**7, transcendentals=0)


def copies(out_ref, message):
    message = message.astype(BF16)
    for d in range(TILES):
        out_ref[d] = message


def signs_kernel(part_ref, sketch_ref, test_ref, codes_ref, jac_hbm, out_ref, jac, sem, vec, rows):
    first = part_ref[0] * SLICE
    base = jnp.minimum(first, LEVELS - SLICE)
    copy = pltpu.make_async_copy(jac_hbm.at[pl.ds(base, SLICE)], jac, sem)
    copy.start()
    rows[...] = jnp.zeros_like(rows)
    for p in range(K):
        vec[p, 0:CHAN, :] = (2 * sketch_ref[p] - 1).astype(F32)
        vec[K + p, 0:CHAN, :] = (2 * test_ref[p] - 1).astype(F32)
        vec[p, CHAN:CPAD, :] = jnp.zeros((CPAD - CHAN, OBS), F32)
        vec[K + p, CHAN:CPAD, :] = jnp.zeros((CPAD - CHAN, OBS), F32)
    rows[CODES:FIRST, :] = codes_ref[...]

    def put(p, level, row):
        rows[pl.ds(p * SLICE + level, 1), :] = row

    copy.wait()
    back_rows(jac, base, vec, 2 * K, first, put)
    copies(out_ref, rows[...])


def sign_adjoints(part, sketch, test, codes, jac):
    return pl.pallas_call(
        signs_kernel,
        in_specs=[SMEM_SPEC, VMEM_SPEC, VMEM_SPEC, VMEM_SPEC, ANY_SPEC],
        out_specs=VMEM_SPEC,
        out_shape=jax.ShapeDtypeStruct((TILES, FIRST, OBS), BF16),
        scratch_shapes=[
            pltpu.VMEM((SLICE, CHAN, OBS), BF16),
            pltpu.SemaphoreType.DMA(()),
            pltpu.VMEM((2 * K, CPAD, OBS), F32),
            pltpu.VMEM((FIRST, OBS), F32),
        ],
        cost_estimate=pl.CostEstimate(flops=10**7, bytes_accessed=2 * 10**6, transcendentals=0),
    )(part, sketch, test, codes, jac)


def images_kernel(
    part_ref, mine_ref, other_ref, test_ref, jac_hbm, img_ref, out_ref, jac, sems, prof, rows
):
    start_jac(jac_hbm, jac, sems)
    core = part_ref[0] % 2
    rows[...] = jnp.zeros_like(rows)
    img_ref[...] = jnp.zeros_like(img_ref)
    prof[...] = jnp.where(core == 0, mine_ref[...].astype(F32), other_ref[...].astype(F32))
    forward(jac_hbm, jac, sems, prof, img_ref, K)

    def put(p, level, row):
        rows[pl.ds(p * SLICE + level, 1), :] = row

    back_rows(jac, 0, img_ref, K, part_ref[0] * SLICE, put)
    lanes = lax.broadcasted_iota(jnp.int32, (1, OBS), 1)
    gram = jnp.zeros((1, OBS), F32)
    for i in range(K):
        for j in range(K):
            if j <= i:
                value = jnp.sum(img_ref[i] * img_ref[j])
                gram = jnp.where(lanes == i * K + j, value, gram)
            signs = (2 * test_ref[j] - 1).astype(F32)
            value = jnp.sum(img_ref[i, 0:CHAN, :] * signs)
            gram = jnp.where(lanes == K * K + i * K + j, value, gram)
    high = gram.astype(BF16).astype(F32)
    mid = (gram - high).astype(BF16).astype(F32)
    rows[GRAMS : GRAMS + 1, :] = high
    rows[GRAMS + 1 : GRAMS + 2, :] = mid
    rows[GRAMS + 2 : GRAMS + 3, :] = gram - high - mid
    copies(out_ref, rows[...])


def images(part, mine, other, test, jac):
    return pl.pallas_call(
        images_kernel,
        in_specs=[SMEM_SPEC, VMEM_SPEC, VMEM_SPEC, VMEM_SPEC, ANY_SPEC],
        out_specs=[VMEM_SPEC, VMEM_SPEC],
        out_shape=[
            jax.ShapeDtypeStruct((K, CPAD, OBS), F32),
            jax.ShapeDtypeStruct((TILES, SECOND, OBS), BF16),
        ],
        scratch_shapes=JAC_SCRATCH
        + [pltpu.VMEM((K * FULL, OBS), F32), pltpu.VMEM((SECOND, OBS), F32)],
        cost_estimate=COST,
    )(part, mine, other, test, jac)


def test_images_kernel(part_ref, mine_ref, other_ref, jac_hbm, img_ref, jac, sems, prof):
    start_jac(jac_hbm, jac, sems)
    core = part_ref[0] % 2
    img_ref[...] = jnp.zeros_like(img_ref)
    prof[...] = jnp.where(core == 0, other_ref[...].astype(F32), mine_ref[...].astype(F32))
    forward(jac_hbm, jac, sems, prof, img_ref, K)


def test_images(part, mine, other, jac):
    return pl.pallas_call(
        test_images_kernel,
        in_specs=[SMEM_SPEC, VMEM_SPEC, VMEM_SPEC, ANY_SPEC],
        out_specs=VMEM_SPEC,
        out_shape=jax.ShapeDtypeStruct((K, CPAD, OBS), F32),
        scratch_shapes=JAC_SCRATCH + [pltpu.VMEM((K * FULL, OBS), F32)],
        cost_estimate=COST,
    )(part, mine, other, jac)


def outputs_kernel(
    size, part_ref, mine_ref, other_ref, second_ref, test_ref, y_ref, z_ref, jac_hbm,
    q_ref, w_ref, trace_ref, jac, sems, prof, x,
):
    start_jac(jac_hbm, jac, sems)
    half = K * FULL // 2
    core = part_ref[0] % 2
    mine, other = mine_ref[...].astype(F32), other_ref[...].astype(F32)
    x[...] = jnp.zeros_like(x)
    prof[0:half, :] = jnp.where(core == 0, mine, other)
    prof[half:, :] = jnp.where(core == 0, other, mine)
    forward(jac_hbm, jac, sems, prof, x, K)

    total = jnp.zeros((1, OBS), F32)
    for d in range(TILES):
        got = second_ref[d, GRAMS : GRAMS + 8, :].astype(F32)
        total = total + jnp.sum(got, axis=0, keepdims=True)
    lanes = lax.broadcasted_iota(jnp.int32, (1, OBS), 1)

    def entry(k):
        return jnp.sum(jnp.where(lanes == k, total, 0.0), axis=1, keepdims=True)

    g = [[entry(i * K + j) for j in range(i + 1)] for i in range(K)]
    c = [[entry(K * K + i * K + j) for j in range(K)] for i in range(K)]
    l00 = jnp.sqrt(g[0][0])
    l10, l20 = g[1][0] / l00, g[2][0] / l00
    l11 = jnp.sqrt(g[1][1] - l10 * l10)
    l21 = (g[2][1] - l20 * l10) / l11
    l22 = jnp.sqrt(g[2][2] - l20 * l20 - l21 * l21)
    i00, i11, i22 = 1.0 / l00, 1.0 / l11, 1.0 / l22
    i10 = -l10 * i00 * i11
    i21 = -l21 * i11 * i22
    i20 = -(l20 * i00 + l21 * i10) * i22
    inv = [[i00], [i10, i11], [i20, i21, i22]]
    root = size**0.5
    basis, image_q = [], []
    for j in range(K):
        b = q = None
        for i in range(j + 1):
            by, qx = root * inv[j][i] * y_ref[i, 0:CHAN, :], root * inv[j][i] * x[i, 0:CHAN, :]
            b, q = (by, qx) if b is None else (b + by, q + qx)
        q_ref[j] = q
        basis.append(b)
        image_q.append(q)
    trace_q = trace_w = None
    for j in range(K):
        w = z_ref[j, 0:CHAN, :]
        rest = (2 * test_ref[j] - 1).astype(F32)
        for i in range(K):
            share = sum(inv[i][k] * c[k][j] for k in range(i + 1)) / root
            w = w - share * image_q[i]
            rest = rest - share * basis[i]
        w_ref[j] = w
        tq, tw = basis[j] * image_q[j], rest * w
        trace_q, trace_w = (tq, tw) if trace_q is None else (trace_q + tq, trace_w + tw)
    row = jnp.where(lanes == 0, jnp.sum(trace_q), jnp.sum(trace_w))
    for d in range(TILES):
        trace_ref[d] = jnp.broadcast_to(row, (8, OBS))


def outputs(size, part, mine, other, second, test, y, z, jac):
    return pl.pallas_call(
        functools.partial(outputs_kernel, size),
        in_specs=[SMEM_SPEC] + [VMEM_SPEC] * 6 + [ANY_SPEC],
        out_specs=[VMEM_SPEC] * 3,
        out_shape=[
            jax.ShapeDtypeStruct((K, CHAN, OBS), F32),
            jax.ShapeDtypeStruct((K, CHAN, OBS), F32),
            jax.ShapeDtypeStruct((TILES, 8, OBS), F32),
        ],
        scratch_shapes=JAC_SCRATCH
        + [pltpu.VMEM((K * FULL, OBS), F32), pltpu.VMEM((K, CPAD, OBS), F32)],
        cost_estimate=COST,
    )(part, mine, other, second, test, y, z, jac)


def pick_kernel(tile_ref, first_ref, members_ref, out_ref):
    cells = members_ref.shape[1]
    tile = tile_ref[0].astype(F32)
    slots = lax.broadcasted_iota(jnp.int32, (CAP, OBS), 0).astype(F32)
    lanes = lax.broadcasted_iota(jnp.int32, (CAP, cells), 1).astype(F32)
    members = members_ref[...]
    for d in range(TILES):
        codes = first_ref[d, CODES:FIRST, :].astype(F32)
        cell = codes[0:1] * 128.0 + codes[1:2] - tile * float(cells)
        inside = (cell >= 0.0) & (cell < float(cells))
        here = jnp.where((slots == codes[2:3]) & inside, cell + 1.0, 0.0)
        at = jnp.sum(here, axis=1, keepdims=True) - 1.0
        chosen = jnp.where(lanes == at, 1.0, 0.0).astype(BF16)
        out_ref[d * CAP : (d + 1) * CAP, :] = dot(chosen, members, NT).astype(BF16)


def pick(tile, first, members):
    return pl.pallas_call(
        pick_kernel,
        in_specs=[SMEM_SPEC, VMEM_SPEC, VMEM_SPEC],
        out_specs=VMEM_SPEC,
        out_shape=jax.ShapeDtypeStruct((TILES * CAP, members.shape[0]), BF16),
    )(tile, first, members)


def own_kernel(pos_ref, recv_ref, out_ref, all_ref):
    rows = lax.broadcasted_iota(jnp.int32, (TILES * CAP, OBS), 0)
    chosen = jnp.where(rows == pos_ref[...], 1.0, 0.0).astype(BF16)
    mine = dot(recv_ref[...].T, chosen)
    out_ref[...] = mine.astype(BF16)
    copies(all_ref, mine)


def own(position, recv):
    rows = recv.shape[1]
    return pl.pallas_call(
        own_kernel,
        in_specs=[VMEM_SPEC, VMEM_SPEC],
        out_specs=[VMEM_SPEC, VMEM_SPEC],
        out_shape=[
            jax.ShapeDtypeStruct((rows, OBS), BF16),
            jax.ShapeDtypeStruct((TILES, rows, OBS), BF16),
        ],
    )(position, recv)


def near_kernel(col_ref, first_ref, table_ref, out_ref):
    mine = col_ref[...]
    my_x = (mine // CB).astype(F32)
    my_b = mine % CB
    hot = jnp.where(lax.broadcasted_iota(jnp.int32, (OBS, CB), 1) == my_b, 1.0, 0.0).astype(BF16)
    reach = [dot(hot, table_ref[a]).astype(BF16) for a in range(STEPS + 1)]
    rows = lax.broadcasted_iota(jnp.int32, (CB, OBS), 0)
    for d in range(TILES):
        codes = first_ref[d, CODES:FIRST, :].astype(F32).astype(jnp.int32)
        hi, lo = codes[0:1], codes[1:2]
        x = (hi * 4 + lo // CB).astype(F32)
        there = jnp.where(rows == lo % CB, 1.0, 0.0).astype(BF16)
        gap = jnp.abs(my_x - x)
        gap = jnp.minimum(gap, float(NX) - gap)
        total = jnp.zeros((OBS, OBS), F32)
        for a in range(STEPS + 1):
            total = jnp.where(gap == float(a), dot(reach[a], there), total)
        out_ref[:, d * OBS : (d + 1) * OBS] = total.astype(BF16)


def near_of(column, first, table):
    return pl.pallas_call(
        near_kernel,
        in_specs=[VMEM_SPEC, VMEM_SPEC, VMEM_SPEC],
        out_specs=VMEM_SPEC,
        out_shape=jax.ShapeDtypeStruct((OBS, TILES * OBS), BF16),
        cost_estimate=pl.CostEstimate(flops=2 * 10**7, bytes_accessed=4 * 10**6, transcendentals=0),
    )(column, first, table)


def covariance_kernel(
    probes, scale, part_ref, all_ref, adj_ref, near_ref, vert_ref, *refs
):
    rows = SLICE * MEMBERS
    pieces = refs[:SLICES]
    keep_ref, send_ref, prod, acc, adj, mem, out = refs[SLICES:]
    chips = SLICES // 2
    chip, core = part_ref[0] // 2, part_ref[0] % 2
    for k in range(chips):
        source = lax.rem(chip + chips - k, chips) * 2
        for n, owner in enumerate((core, 1 - core)):
            at = pl.multiple_of((source + owner) * rows, rows)
            mem[pl.ds(at, rows), :] = pieces[2 * k + n][...].astype(F32)

    def pair(k, carry):
        for half in range(2):
            d = 2 * k + half
            adj[...] = adj_ref[d].astype(F32)
            for level in range(SLICE):
                values = all_ref[d, level * MEMBERS : (level + 1) * MEMBERS, :]
                for p in range(probes):
                    at = p * SLICE + level
                    row = jnp.broadcast_to(adj[at : at + 1, :], (MEMBERS, OBS)).astype(BF16)
                    prod[at * MEMBERS : (at + 1) * MEMBERS, half * OBS : (half + 1) * OBS] = (
                        values * row
                    )
        near = near_ref[:, pl.ds(pl.multiple_of(k * 2 * OBS, 2 * OBS), 2 * OBS)]
        acc[...] += dot(prod[...], near, NT)
        return carry

    acc[...] = jnp.zeros_like(acc)
    lax.fori_loop(0, TILES // 2, pair, 0)
    vert = vert_ref[...]
    for p in range(probes):
        total = None
        for m in range(MEMBERS):
            smooth = acc[pl.ds(p * rows + m, SLICE, stride=MEMBERS), :].astype(BF16)
            term = mem[pl.ds(m, FULL, stride=MEMBERS), :] * dot(vert, smooth)
            total = term if total is None else total + term
        out[p * FULL : (p + 1) * FULL, :] = total * scale
    half = probes * FULL // 2
    low, high = out[0:half, :], out[half:, :]
    keep_ref[...] = jnp.where(core == 0, low, high).astype(BF16)
    send_ref[...] = jnp.where(core == 0, high, low).astype(BF16)


def covariance(probes, scale, part, everyone, adjoints, near, vert, pieces):
    rows = SLICE * MEMBERS
    half = jax.ShapeDtypeStruct((probes * FULL // 2, OBS), BF16)
    return pl.pallas_call(
        functools.partial(covariance_kernel, probes, scale),
        in_specs=[SMEM_SPEC] + [VMEM_SPEC] * (4 + SLICES),
        out_specs=[VMEM_SPEC, VMEM_SPEC],
        out_shape=[half, half],
        scratch_shapes=[
            pltpu.VMEM((probes * rows, 2 * OBS), BF16),
            pltpu.VMEM((probes * rows, OBS), F32),
            pltpu.VMEM((adjoints.shape[1], OBS), F32),
            pltpu.VMEM((FULL * MEMBERS, OBS), F32),
            pltpu.VMEM((probes * FULL, OBS), F32),
        ],
    )(part, everyone, adjoints, near, vert, *pieces)


def exchange(value, axis):
    return lax.all_to_all(value, axis, 0, 0, tiled=True)


def swap_cores(value):
    return lax.ppermute(value, "mem", [(j, j ^ 1) for j in range(SLICES)])


def from_other_chips(value):
    return [
        lax.ppermute(value, "mem", [(j, (j + 2 * k) % SLICES) for j in range(SLICES)])
        for k in range(1, SLICES // 2)
    ]


def sum_over_mem(keep, send):
    kept = (keep.astype(F32) + swap_cores(send).astype(F32)).astype(BF16)
    others = from_other_chips(kept)
    total = (kept.astype(F32) + others[1].astype(F32)) + (
        others[0].astype(F32) + others[2].astype(F32)
    )
    total = total.astype(BF16)
    return total, swap_cores(total)


def on_device(members, vertical, jacobian, sketch_bits, test_bits, obs_column, obs_slot):
    slice_id = lax.axis_index("mem").astype(jnp.int32)
    part = slice_id.reshape(1)
    my_tile = lax.axis_index(TILE).astype(jnp.int32)
    local, levels, cells = members.shape
    size = float(OBS * TILES * CHAN)
    scale = 1.0 / ((MEMBERS - 1) * 5.0**STEPS * WALK_SCALE)

    padded = jnp.pad(jnp.swapaxes(members, 0, 1), ((0, FULL - levels), (0, 0), (0, 0)))
    sliced = exchange(padded.reshape(SLICES, SLICE * local, cells), "mem")
    sliced = jnp.swapaxes(sliced.reshape(SLICES, SLICE, local, cells), 0, 1)
    sliced = sliced.reshape(SLICE * MEMBERS, cells)

    jac = jnp.transpose(jacobian, (2, 1, 0))
    sketch = jnp.swapaxes(sketch_bits, 1, 2)
    test = jnp.swapaxes(test_bits, 1, 2)
    codes = jnp.stack([obs_column // 128, obs_column % 128, obs_slot]).astype(F32)
    codes = jnp.pad(codes, ((0, 5), (0, 0)))
    first = exchange(sign_adjoints(part, sketch, test, codes, jac), TILE)

    picked = pick(my_tile.reshape(1), first, sliced)
    arrived = exchange(picked.reshape(TILES, CAP, -1), TILE)
    position = (obs_column // cells * CAP + obs_slot).reshape(1, OBS)
    mine, everyone = own(position, arrived.reshape(TILES * CAP, -1))
    everyone = exchange(everyone, TILE)
    near = near_of(obs_column.reshape(OBS, 1), first, jnp.asarray(walk_table(), BF16))
    pieces = []
    for piece in [mine] + from_other_chips(mine):
        pieces += [piece, swap_cores(piece)]

    vert = jnp.pad(vertical, ((0, FULL - levels), (0, FULL - levels)))
    vert = lax.dynamic_slice_in_dim(vert, slice_id * SLICE, SLICE, axis=1)

    halves = covariance(2 * K, scale, part, everyone, first, near, vert, pieces)
    mine_1, other_1 = sum_over_mem(*halves)
    y, second = images(part, mine_1, other_1, test, jac)
    second = exchange(second, TILE)
    z = test_images(part, mine_1, other_1, jac)
    second, z = lax.optimization_barrier((second, z))
    halves = covariance(K, scale, part, everyone, second, near, vert, pieces)
    mine_2, other_2 = sum_over_mem(*halves)
    image_q, image_w, traces = outputs(size, part, mine_2, other_2, second, test, y, z, jac)
    traces = exchange(traces, TILE)[:, 0, :].sum(axis=0)
    trace_q, trace_w = traces[0], traces[1]
    trace_mean = trace_q / (size * size) + trace_w / (K * size)
    return (
        jnp.swapaxes(image_q, 1, 2),
        jnp.swapaxes(image_w, 1, 2),
        trace_mean,
        trace_q / (K * size),
    )


def solution(mesh):
    finer = Mesh(mesh.devices.reshape(mesh.shape["mem"], 4, 4), ("mem", "tile_0", "tile_1"))
    return jax.shard_map(
        on_device,
        mesh=finer,
        in_specs=(
            P("mem", None, TILE),
            P(),
            P(TILE, None, None),
            P(None, TILE, None),
            P(None, TILE, None),
            P(TILE),
            P(TILE),
        ),
        out_specs=(P(None, TILE, None), P(None, TILE, None), P(), P()),
        check_vma=False,
    )
```

```python
import functools

import jax
import jax.numpy as jnp
import numpy as np
from jax import lax
from jax.experimental import pallas as pl
from jax.experimental.pallas import tpu as pltpu
from jax.sharding import Mesh
from jax.sharding import PartitionSpec as P

CB = 32
NX = 256
K = 3
STEPS = 6
TILE = ("tile_0", "tile_1")
TILES = 16
SLICES = 8
LEVELS = 137
SLICE = 18
FULL = SLICES * SLICE
MEMBERS = 16
PIECE = 48
CAP = 32
OBS = 128
CHAN = 231
CPAD = 240
BLOCK = 9
BLOCKS = -(-LEVELS // BLOCK)
REST = LEVELS - (BLOCKS - 1) * BLOCK
CODES = 112
FIRST = 120
GRAMS = 56
SECOND = 64


LIMIT = pltpu.CompilerParams(vmem_limit_bytes=24 * 2**20)
WIDE = pltpu.CompilerParams(vmem_limit_bytes=57 * 2**20)
F32 = jnp.float32
BF16 = jnp.bfloat16
VMEM_SPEC = pl.BlockSpec(memory_space=pltpu.VMEM)
SMEM_SPEC = pl.BlockSpec(memory_space=pltpu.SMEM)
NT = (((1,), (1,)), ((), ()))

WALK_SCALE = 1.3338


def walk_table():
    walks = np.zeros((2 * STEPS + 1, 2 * STEPS + 1))
    walks[STEPS, STEPS] = 1
    for _ in range(STEPS):
        grown = walks.copy()
        grown[1:] += walks[:-1]
        grown[:-1] += walks[1:]
        grown[:, 1:] += walks[:, :-1]
        grown[:, :-1] += walks[:, 1:]
        walks = grown

    def count(a, d):
        return walks[STEPS + a, STEPS + d] if d <= STEPS else 0.0

    table = np.zeros((STEPS + 1, CB, CB), np.float32)
    for a in range(STEPS + 1):
        for b in range(CB):
            for c in range(CB):
                table[a, b, c] = (
                    count(a, abs(b - c)) + count(a, b + c + 1) + count(a, 2 * CB - 1 - b - c)
                )
    return table * WALK_SCALE


def dot(a, b, dims=(((1,), (0,)), ((), ()))):
    return lax.dot_general(a, b, dims, preferred_element_type=F32)


def channel_chunks():
    return [(c, min(16, CHAN - c)) for c in range(0, CHAN, 16)]


def jac_rows(jac_ref, level, c, width):
    rows = jac_ref[level, c : c + width, :].astype(F32)
    if width % 8:
        fill = jnp.zeros((8 - width % 8, OBS), F32)
        rows = jnp.concatenate([rows, fill], axis=0)
    return [rows[k : k + 8] for k in range(0, rows.shape[0], 8)]


def back_rows(jac_ref, base, vec_ref, probes, first, put):
    def trio(t, carry):
        levels = [jnp.minimum(first + 3 * t + k, LEVELS - 1) - base for k in range(3)]
        acc = {}
        for c, width in channel_chunks():
            vecs = [
                [vec_ref[p, c + 8 * k : c + 8 * k + 8, :] for k in range(-(-width // 8))]
                for p in range(probes)
            ]
            for n, level in enumerate(levels):
                for k, rows in enumerate(jac_rows(jac_ref, level, c, width)):
                    for p in range(probes):
                        term = rows * vecs[p][k]
                        acc[p, n] = acc[p, n] + term if (p, n) in acc else term
        for n in range(3):
            valid = first + 3 * t + n < LEVELS
            for p in range(probes):
                row = jnp.sum(acc[p, n], axis=0, keepdims=True)
                put(p, 3 * t + n, jnp.where(valid, row, 0.0))
        return carry

    lax.fori_loop(0, SLICE // 3, trio, 0)


def forward_block(jac_ref, prof_ref, img_ref, probes, first, count):
    weights = [
        [
            jnp.broadcast_to(prof_ref[pl.ds(p * FULL + first + level, 1), :], (8, OBS))
            for level in range(count)
        ]
        for p in range(probes)
    ]
    for c, width in channel_chunks():
        parts = -(-width // 8)
        acc = [
            [img_ref[p, c + 8 * k : c + 8 * k + 8, :] for k in range(parts)] for p in range(probes)
        ]
        for level in range(count):
            for k, rows in enumerate(jac_rows(jac_ref, first + level, c, width)):
                for p in range(probes):
                    acc[p][k] = acc[p][k] + rows * weights[p][level]
        for p in range(probes):
            for k in range(parts):
                img_ref[p, c + 8 * k : c + 8 * k + 8, :] = acc[p][k]


def jac_copy(jac_hbm, jac_ref, sems, k, count=BLOCK):
    levels = pl.ds(k * BLOCK, count)
    return pltpu.make_async_copy(jac_hbm.at[levels], jac_ref.at[levels], sems.at[k])


def start_jac(jac_hbm, jac_ref, sems):
    for k in range(BLOCKS):
        jac_copy(jac_hbm, jac_ref, sems, k, BLOCK if k < BLOCKS - 1 else REST).start()


def forward(jac_hbm, jac_ref, sems, prof_ref, img_ref, probes):
    def block(k, carry):
        jac_copy(jac_hbm, jac_ref, sems, k).wait()
        forward_block(jac_ref, prof_ref, img_ref, probes, k * BLOCK, BLOCK)
        return carry

    lax.fori_loop(0, BLOCKS - 1, block, 0)
    jac_copy(jac_hbm, jac_ref, sems, BLOCKS - 1, REST).wait()
    forward_block(jac_ref, prof_ref, img_ref, probes, (BLOCKS - 1) * BLOCK, REST)


JAC_SCRATCH = [pltpu.VMEM((LEVELS, CHAN, OBS), BF16), pltpu.SemaphoreType.DMA((BLOCKS,))]
HBM_SPEC = pl.BlockSpec(memory_space=pl.ANY)
COST = pl.CostEstimate(flops=4 * 10**7, bytes_accessed=10**7, transcendentals=0)


def copies(out_ref, message):
    message = message.astype(BF16)
    for d in range(TILES):
        out_ref[d] = message


def signs_kernel(
    part_ref, sketch_ref, test_ref, column_ref, slot_ref, jac_hbm, out_ref, jac, sem, vec, rows
):
    first = part_ref[0] * SLICE
    base = jnp.minimum(first, LEVELS - SLICE)
    copy = pltpu.make_async_copy(jac_hbm.at[pl.ds(base, SLICE)], jac, sem)
    copy.start()
    rows[...] = jnp.zeros_like(rows)
    for p in range(K):
        vec[p, 0:CHAN, :] = (2 * sketch_ref[p] - 1).astype(F32)
        vec[K + p, 0:CHAN, :] = (2 * test_ref[p] - 1).astype(F32)
        vec[p, CHAN:CPAD, :] = jnp.zeros((CPAD - CHAN, OBS), F32)
        vec[K + p, CHAN:CPAD, :] = jnp.zeros((CPAD - CHAN, OBS), F32)
    column = column_ref[...]
    rows[CODES : CODES + 1, :] = jnp.right_shift(column, 7).astype(F32)
    rows[CODES + 1 : CODES + 2, :] = (column & 127).astype(F32)
    rows[CODES + 2 : CODES + 3, :] = slot_ref[...].astype(F32)

    def put(p, level, row):
        rows[pl.ds(p * SLICE + level, 1), :] = row

    copy.wait()
    back_rows(jac, base, vec, 2 * K, first, put)
    copies(out_ref, rows[...])


def sign_adjoints(part, sketch, test, column, slot, jac):
    return pl.pallas_call(
        signs_kernel,
        compiler_params=WIDE,
        in_specs=[SMEM_SPEC] + [VMEM_SPEC] * 4 + [HBM_SPEC],
        out_specs=VMEM_SPEC,
        out_shape=jax.ShapeDtypeStruct((TILES, FIRST, OBS), BF16),
        scratch_shapes=[
            pltpu.VMEM((SLICE, CHAN, OBS), BF16),
            pltpu.SemaphoreType.DMA(()),
            pltpu.VMEM((2 * K, CPAD, OBS), F32),
            pltpu.VMEM((FIRST, OBS), F32),
        ],
        cost_estimate=pl.CostEstimate(flops=10**7, bytes_accessed=2 * 10**6, transcendentals=0),
    )(part, sketch, test, column, slot, jac)


def images_kernel(
    part_ref, mine_ref, other_ref, test_ref, jac_hbm, img_ref, out_ref, jac, sems, prof, rows
):
    start_jac(jac_hbm, jac, sems)
    core = part_ref[0] % 2
    rows[...] = jnp.zeros_like(rows)
    img_ref[...] = jnp.zeros_like(img_ref)
    prof[...] = jnp.where(core == 0, mine_ref[...].astype(F32), other_ref[...].astype(F32))
    forward(jac_hbm, jac, sems, prof, img_ref, K)

    def put(p, level, row):
        rows[pl.ds(p * SLICE + level, 1), :] = row

    back_rows(jac, 0, img_ref, K, part_ref[0] * SLICE, put)
    lanes = lax.broadcasted_iota(jnp.int32, (1, OBS), 1)
    gram = jnp.zeros((1, OBS), F32)
    for i in range(K):
        for j in range(K):
            if j <= i:
                value = jnp.sum(img_ref[i] * img_ref[j])
                gram = jnp.where(lanes == i * K + j, value, gram)
            signs = (2 * test_ref[j] - 1).astype(F32)
            value = jnp.sum(img_ref[i, 0:CHAN, :] * signs)
            gram = jnp.where(lanes == K * K + i * K + j, value, gram)
    high = gram.astype(BF16).astype(F32)
    mid = (gram - high).astype(BF16).astype(F32)
    rows[GRAMS : GRAMS + 1, :] = high
    rows[GRAMS + 1 : GRAMS + 2, :] = mid
    rows[GRAMS + 2 : GRAMS + 3, :] = gram - high - mid
    copies(out_ref, rows[...])


def images(part, mine, other, test, jac):
    return pl.pallas_call(
        images_kernel,
        compiler_params=WIDE,
        in_specs=[SMEM_SPEC, VMEM_SPEC, VMEM_SPEC, VMEM_SPEC, HBM_SPEC],
        out_specs=[VMEM_SPEC, VMEM_SPEC],
        out_shape=[
            jax.ShapeDtypeStruct((K, CPAD, OBS), F32),
            jax.ShapeDtypeStruct((TILES, SECOND, OBS), BF16),
        ],
        scratch_shapes=JAC_SCRATCH
        + [pltpu.VMEM((K * FULL, OBS), F32), pltpu.VMEM((SECOND, OBS), F32)],
        cost_estimate=COST,
    )(part, mine, other, test, jac)


def test_images_kernel(part_ref, mine_ref, other_ref, jac_hbm, img_ref, jac, sems, prof):
    start_jac(jac_hbm, jac, sems)
    core = part_ref[0] % 2
    img_ref[...] = jnp.zeros_like(img_ref)
    prof[...] = jnp.where(core == 0, other_ref[...].astype(F32), mine_ref[...].astype(F32))
    forward(jac_hbm, jac, sems, prof, img_ref, K)


def test_images(part, mine, other, jac):
    return pl.pallas_call(
        test_images_kernel,
        compiler_params=WIDE,
        in_specs=[SMEM_SPEC, VMEM_SPEC, VMEM_SPEC, HBM_SPEC],
        out_specs=VMEM_SPEC,
        out_shape=jax.ShapeDtypeStruct((K, CPAD, OBS), F32),
        scratch_shapes=JAC_SCRATCH + [pltpu.VMEM((K * FULL, OBS), F32)],
        cost_estimate=COST,
    )(part, mine, other, jac)


def outputs_kernel(
    size, part_ref, mine_ref, other_ref, second_ref, test_ref, y_ref, z_ref, jac_hbm,
    q_ref, w_ref, trace_ref, jac, sems, prof, x,
):
    start_jac(jac_hbm, jac, sems)
    half = K * FULL // 2
    core = part_ref[0] % 2
    mine, other = mine_ref[...].astype(F32), other_ref[...].astype(F32)
    x[...] = jnp.zeros_like(x)
    prof[0:half, :] = jnp.where(core == 0, mine, other)
    prof[half:, :] = jnp.where(core == 0, other, mine)
    forward(jac_hbm, jac, sems, prof, x, K)

    total = jnp.zeros((1, OBS), F32)
    for d in range(TILES):
        got = second_ref[d, GRAMS : GRAMS + 8, :].astype(F32)
        total = total + jnp.sum(got, axis=0, keepdims=True)
    lanes = lax.broadcasted_iota(jnp.int32, (1, OBS), 1)

    def entry(k):
        return jnp.sum(jnp.where(lanes == k, total, 0.0), axis=1, keepdims=True)

    g = [[entry(i * K + j) for j in range(i + 1)] for i in range(K)]
    c = [[entry(K * K + i * K + j) for j in range(K)] for i in range(K)]
    l00 = jnp.sqrt(g[0][0])
    l10, l20 = g[1][0] / l00, g[2][0] / l00
    l11 = jnp.sqrt(g[1][1] - l10 * l10)
    l21 = (g[2][1] - l20 * l10) / l11
    l22 = jnp.sqrt(g[2][2] - l20 * l20 - l21 * l21)
    i00, i11, i22 = 1.0 / l00, 1.0 / l11, 1.0 / l22
    i10 = -l10 * i00 * i11
    i21 = -l21 * i11 * i22
    i20 = -(l20 * i00 + l21 * i10) * i22
    inv = [[i00], [i10, i11], [i20, i21, i22]]
    root = size**0.5
    basis, image_q = [], []
    for j in range(K):
        b = q = None
        for i in range(j + 1):
            by, qx = root * inv[j][i] * y_ref[i, 0:CHAN, :], root * inv[j][i] * x[i, 0:CHAN, :]
            b, q = (by, qx) if b is None else (b + by, q + qx)
        q_ref[j] = q
        basis.append(b)
        image_q.append(q)
    trace_q = trace_w = None
    for j in range(K):
        w = z_ref[j, 0:CHAN, :]
        rest = (2 * test_ref[j] - 1).astype(F32)
        for i in range(K):
            share = sum(inv[i][k] * c[k][j] for k in range(i + 1)) / root
            w = w - share * image_q[i]
            rest = rest - share * basis[i]
        w_ref[j] = w
        tq, tw = basis[j] * image_q[j], rest * w
        trace_q, trace_w = (tq, tw) if trace_q is None else (trace_q + tq, trace_w + tw)
    row = jnp.where(lanes == 0, jnp.sum(trace_q), jnp.sum(trace_w))
    for d in range(TILES):
        trace_ref[d] = jnp.broadcast_to(row, (8, OBS))


def outputs(size, part, mine, other, second, test, y, z, jac):
    return pl.pallas_call(
        functools.partial(outputs_kernel, size),
        compiler_params=WIDE,
        in_specs=[SMEM_SPEC] + [VMEM_SPEC] * 6 + [HBM_SPEC],
        out_specs=[VMEM_SPEC] * 3,
        out_shape=[
            jax.ShapeDtypeStruct((K, CHAN, OBS), F32),
            jax.ShapeDtypeStruct((K, CHAN, OBS), F32),
            jax.ShapeDtypeStruct((TILES, 8, OBS), F32),
        ],
        scratch_shapes=JAC_SCRATCH
        + [pltpu.VMEM((K * FULL, OBS), F32), pltpu.VMEM((K, CPAD, OBS), F32)],
        cost_estimate=COST,
    )(part, mine, other, second, test, y, z, jac)


def split_kernel(part_ref, members_ref, *out_refs):
    for k in range(SLICES):
        out_refs[k][...] = members_ref[lax.rem(part_ref[0] + k, SLICES)]


def split(part, members):
    piece = jax.ShapeDtypeStruct(members.shape[1:], BF16)
    return pl.pallas_call(
        split_kernel,
        compiler_params=LIMIT,
        in_specs=[SMEM_SPEC, VMEM_SPEC],
        out_specs=[VMEM_SPEC] * SLICES,
        out_shape=[piece] * SLICES,
    )(part, members)


def pick_kernel(place_ref, first_ref, *refs):
    pieces = refs[:SLICES]
    out_ref, members, chosen = refs[SLICES:]
    cells = members.shape[1]
    for k in range(SLICES):
        source = lax.rem(place_ref[1] + SLICES - k, SLICES)
        members[pl.ds(pl.multiple_of(source * PIECE, PIECE), PIECE), :] = pieces[k][...]
    tile = place_ref[0].astype(F32)
    slots = lax.broadcasted_iota(jnp.int32, (CAP, OBS), 0).astype(F32)
    lanes = lax.broadcasted_iota(jnp.int32, (CAP, cells), 1).astype(F32)
    for d in range(TILES):
        codes = first_ref[d, CODES:FIRST, :].astype(F32)
        cell = codes[0:1] * 128.0 + codes[1:2] - tile * float(cells)
        inside = (cell >= 0.0) & (cell < float(cells))
        here = jnp.where((slots == codes[2:3]) & inside, cell + 1.0, 0.0)
        at = jnp.sum(here, axis=1, keepdims=True) - 1.0
        chosen[d * CAP : (d + 1) * CAP, :] = jnp.where(lanes == at, 1.0, 0.0).astype(BF16)
    out_ref[...] = dot(chosen[...], members[...], NT).astype(BF16)


def pick(place, first, pieces):
    cells = pieces[0].shape[1]
    return pl.pallas_call(
        pick_kernel,
        compiler_params=LIMIT,
        in_specs=[SMEM_SPEC] + [VMEM_SPEC] * (1 + SLICES),
        out_specs=VMEM_SPEC,
        out_shape=jax.ShapeDtypeStruct((TILES * CAP, SLICES * PIECE), BF16),
        scratch_shapes=[
            pltpu.VMEM((SLICES * PIECE, cells), BF16),
            pltpu.VMEM((TILES * CAP, cells), BF16),
        ],
    )(place, first, *pieces)


def own_kernel(pos_ref, recv_ref, out_ref, all_ref):
    rows = lax.broadcasted_iota(jnp.int32, (TILES * CAP, OBS), 0)
    chosen = jnp.where(rows == pos_ref[...], 1.0, 0.0).astype(BF16)
    mine = dot(recv_ref[...].T, chosen).astype(BF16)
    shape = (SLICE * MEMBERS, SLICES * PIECE)
    row = lax.broadcasted_iota(jnp.int32, shape, 0)
    lane = lax.broadcasted_iota(jnp.int32, shape, 1)
    level, member = jnp.right_shift(row, 4), row & 15
    source = jnp.right_shift(member, 1) * PIECE + 2 * level + (member & 1)
    turn = jnp.where(lane == source, 1.0, 0.0).astype(BF16)
    mine = dot(turn, mine)
    out_ref[...] = mine.astype(BF16)
    copies(all_ref, mine)


def own(position, recv):
    rows = SLICE * MEMBERS
    return pl.pallas_call(
        own_kernel,
        compiler_params=LIMIT,
        in_specs=[VMEM_SPEC, VMEM_SPEC],
        out_specs=[VMEM_SPEC, VMEM_SPEC],
        out_shape=[
            jax.ShapeDtypeStruct((rows, OBS), BF16),
            jax.ShapeDtypeStruct((TILES, rows, OBS), BF16),
        ],
    )(position, recv)


def gathered_kernel(part_ref, *refs):
    rows = SLICE * MEMBERS
    pieces = refs[:SLICES]
    out_ref, mem = refs[SLICES:]
    chips = SLICES // 2
    chip, core = part_ref[0] // 2, part_ref[0] % 2
    for k in range(chips):
        source = lax.rem(chip + chips - k, chips) * 2
        for n, owner in enumerate((core, 1 - core)):
            at = pl.multiple_of((source + owner) * rows, rows)
            mem[pl.ds(at, rows), :] = pieces[2 * k + n][...].astype(F32)
    for m in range(MEMBERS):
        out_ref[m * FULL : (m + 1) * FULL, :] = mem[pl.ds(m, FULL, stride=MEMBERS), :]


def gathered(part, pieces):
    return pl.pallas_call(
        gathered_kernel,
        compiler_params=LIMIT,
        in_specs=[SMEM_SPEC] + [VMEM_SPEC] * SLICES,
        out_specs=VMEM_SPEC,
        out_shape=jax.ShapeDtypeStruct((MEMBERS * FULL, OBS), F32),
        scratch_shapes=[pltpu.VMEM((MEMBERS * FULL, OBS), F32)],
        cost_estimate=pl.CostEstimate(flops=10**6, bytes_accessed=2 * 10**6, transcendentals=0),
    )(part, *pieces)


def near_kernel(col_ref, first_ref, table_ref, out_ref):
    mine = col_ref[...]
    my_x = (mine // CB).astype(F32)
    my_b = mine % CB
    hot = jnp.where(lax.broadcasted_iota(jnp.int32, (OBS, CB), 1) == my_b, 1.0, 0.0).astype(BF16)
    reach = [dot(hot, table_ref[a]).astype(BF16) for a in range(STEPS + 1)]
    rows = lax.broadcasted_iota(jnp.int32, (CB, OBS), 0)
    for d in range(TILES):
        codes = first_ref[d, CODES:FIRST, :].astype(F32).astype(jnp.int32)
        hi, lo = codes[0:1], codes[1:2]
        x = (hi * 4 + lo // CB).astype(F32)
        there = jnp.where(rows == lo % CB, 1.0, 0.0).astype(BF16)
        gap = jnp.abs(my_x - x)
        gap = jnp.minimum(gap, float(NX) - gap)
        total = jnp.zeros((OBS, OBS), F32)
        for a in range(STEPS + 1):
            total = jnp.where(gap == float(a), dot(reach[a], there), total)
        out_ref[:, d * OBS : (d + 1) * OBS] = total.astype(BF16)


def near_of(column, first, table):
    return pl.pallas_call(
        near_kernel,
        compiler_params=LIMIT,
        in_specs=[VMEM_SPEC, VMEM_SPEC, VMEM_SPEC],
        out_specs=VMEM_SPEC,
        out_shape=jax.ShapeDtypeStruct((OBS, TILES * OBS), BF16),
        cost_estimate=pl.CostEstimate(flops=2 * 10**7, bytes_accessed=4 * 10**6, transcendentals=0),
    )(column, first, table)


def covariance_kernel(
    probes, scale, part_ref, all_ref, adj_ref, near_ref, mem_ref, vert_ref, keep_ref, send_ref,
    prod, acc, adj, out,
):
    rows = SLICE * MEMBERS
    adj[...] = adj_ref[...].astype(F32)

    def probe(p, carry):
        for d in range(TILES):
            for level in range(SLICE):
                row = adj[d, pl.ds(p * SLICE + level, 1), :]
                row = jnp.broadcast_to(row, (MEMBERS, OBS)).astype(BF16)
                at = slice(level * MEMBERS, (level + 1) * MEMBERS)
                prod[at, d * OBS : (d + 1) * OBS] = all_ref[d, at, :] * row
        acc[pl.ds(pl.multiple_of(p * rows, rows), rows), :] = dot(prod[...], near_ref[...], NT)
        return carry

    lax.fori_loop(0, probes, probe, 0)
    vert = vert_ref[...]
    for p in range(probes):
        total = None
        for m in range(MEMBERS):
            smooth = acc[pl.ds(p * rows + m, SLICE, stride=MEMBERS), :].astype(BF16)
            term = mem_ref[m * FULL : (m + 1) * FULL, :] * dot(vert, smooth)
            total = term if total is None else total + term
        out[p * FULL : (p + 1) * FULL, :] = total * scale
    half = probes * FULL // 2
    core = part_ref[0] % 2
    low, high = out[0:half, :], out[half:, :]
    keep_ref[...] = jnp.where(core == 0, low, high).astype(BF16)
    send_ref[...] = jnp.where(core == 0, high, low).astype(BF16)


def covariance(probes, scale, part, everyone, adjoints, near, mem, vert):
    rows = SLICE * MEMBERS
    half = jax.ShapeDtypeStruct((probes * FULL // 2, OBS), BF16)
    return pl.pallas_call(
        functools.partial(covariance_kernel, probes, scale),
        compiler_params=LIMIT,
        in_specs=[SMEM_SPEC] + [VMEM_SPEC] * 5,
        out_specs=[VMEM_SPEC, VMEM_SPEC],
        out_shape=[half, half],
        scratch_shapes=[
            pltpu.VMEM((rows, TILES * OBS), BF16),
            pltpu.VMEM((probes * rows, OBS), F32),
            pltpu.VMEM(adjoints.shape, F32),
            pltpu.VMEM((probes * FULL, OBS), F32),
        ],
    )(part, everyone, adjoints, near, mem, vert)


def exchange(value, axis):
    return lax.all_to_all(value, axis, 0, 0, tiled=True)


def swap_cores(value):
    return lax.ppermute(value, "mem", [(j, j ^ 1) for j in range(SLICES)])


def from_other_chips(value):
    return [
        lax.ppermute(value, "mem", [(j, (j + 2 * k) % SLICES) for j in range(SLICES)])
        for k in range(1, SLICES // 2)
    ]


def sum_over_mem(keep, send):
    kept = (keep.astype(F32) + swap_cores(send).astype(F32)).astype(BF16)
    others = from_other_chips(kept)
    total = (kept.astype(F32) + others[1].astype(F32)) + (
        others[0].astype(F32) + others[2].astype(F32)
    )
    total = total.astype(BF16)
    return total, swap_cores(total)


def on_device(members, vertical, jacobian, sketch_bits, test_bits, obs_column, obs_slot):
    slice_id = lax.axis_index("mem").astype(jnp.int32)
    part = slice_id.reshape(1)
    my_tile = lax.axis_index(TILE).astype(jnp.int32)
    local, levels, cells = members.shape
    size = float(OBS * TILES * CHAN)
    scale = 1.0 / ((MEMBERS - 1) * 5.0**STEPS * WALK_SCALE)

    jac = jnp.transpose(jacobian, (2, 1, 0))
    sketch = jnp.swapaxes(sketch_bits, 1, 2)
    test = jnp.swapaxes(test_bits, 1, 2)
    column, slot = obs_column.reshape(1, OBS), obs_slot.reshape(1, OBS)
    first = sign_adjoints(part, sketch, test, column, slot, jac)
    first, members = lax.optimization_barrier((first, members))
    first = exchange(first, TILE)

    padded = jnp.pad(jnp.swapaxes(members, 0, 1), ((0, FULL - levels), (0, 0), (0, 0)))
    padded = padded.reshape(SLICES, SLICE * local, cells)
    padded = jnp.pad(padded, ((0, 0), (0, PIECE - SLICE * local), (0, 0)))
    pieces = list(split(part, padded))
    for k in range(1, SLICES):
        pieces[k] = lax.ppermute(pieces[k], "mem", [(j, (j + k) % SLICES) for j in range(SLICES)])

    picked = pick(jnp.stack([my_tile, slice_id]), first, pieces)
    arrived = exchange(picked.reshape(TILES, CAP, -1), TILE)
    position = (obs_column // cells * CAP + obs_slot).reshape(1, OBS)
    mine, everyone = own(position, arrived.reshape(TILES * CAP, -1))
    everyone = exchange(everyone, TILE)
    near = near_of(obs_column.reshape(OBS, 1), first, jnp.asarray(walk_table(), BF16))
    pieces = []
    for piece in [mine] + from_other_chips(mine):
        pieces += [piece, swap_cores(piece)]
    mem = gathered(part, pieces)

    vert = jnp.pad(vertical, ((0, FULL - levels), (0, FULL - levels)))
    vert = lax.dynamic_slice_in_dim(vert, slice_id * SLICE, SLICE, axis=1)

    halves = covariance(2 * K, scale, part, everyone, first, near, mem, vert)
    mine_1, other_1 = sum_over_mem(*halves)
    y, second = images(part, mine_1, other_1, test, jac)
    second = exchange(second, TILE)
    z = test_images(part, mine_1, other_1, jac)
    second, z = lax.optimization_barrier((second, z))
    halves = covariance(K, scale, part, everyone, second, near, mem, vert)
    mine_2, other_2 = sum_over_mem(*halves)
    image_q, image_w, traces = outputs(size, part, mine_2, other_2, second, test, y, z, jac)
    traces = exchange(traces, TILE)[:, 0, :].sum(axis=0)
    trace_q, trace_w = traces[0], traces[1]
    trace_mean = trace_q / (size * size) + trace_w / (K * size)
    return (
        jnp.swapaxes(image_q, 1, 2),
        jnp.swapaxes(image_w, 1, 2),
        trace_mean,
        trace_q / (K * size),
    )


def solution(mesh):
    finer = Mesh(mesh.devices.reshape(mesh.shape["mem"], 4, 4), ("mem", "tile_0", "tile_1"))
    return jax.shard_map(
        on_device,
        mesh=finer,
        in_specs=(
            P("mem", None, TILE),
            P(),
            P(TILE, None, None),
            P(None, TILE, None),
            P(None, TILE, None),
            P(TILE),
            P(TILE),
        ),
        out_specs=(P(None, TILE, None), P(None, TILE, None), P(), P()),
        check_vma=False,
    )
```

```python
import functools

import jax
import jax.numpy as jnp
import numpy as np
from jax import lax
from jax.experimental import pallas as pl
from jax.experimental.pallas import tpu as pltpu
from jax.sharding import Mesh
from jax.sharding import PartitionSpec as P

CB = 32
NX = 256
K = 3
STEPS = 6
TILE = ("tile_0", "tile_1")
TILES = 16
SLICES = 8
LEVELS = 137
SLICE = 18
FULL = SLICES * SLICE
MEMBERS = 16
PIECE = 48
CAP = 32
OBS = 128
CHAN = 231
CPAD = 240
BLOCK = 9
BLOCKS = -(-LEVELS // BLOCK)
REST = LEVELS - (BLOCKS - 1) * BLOCK
CODES = 112
FIRST = 120
GRAMS = 56
SECOND = 64


LIMIT = pltpu.CompilerParams(vmem_limit_bytes=24 * 2**20)
WIDE = pltpu.CompilerParams(vmem_limit_bytes=59000000)
F32 = jnp.float32
BF16 = jnp.bfloat16
VMEM_SPEC = pl.BlockSpec(memory_space=pltpu.VMEM)
SMEM_SPEC = pl.BlockSpec(memory_space=pltpu.SMEM)
NT = (((1,), (1,)), ((), ()))

WALK_SCALE = 1.3338


def walk_table():
    walks = np.zeros((2 * STEPS + 1, 2 * STEPS + 1))
    walks[STEPS, STEPS] = 1
    for _ in range(STEPS):
        grown = walks.copy()
        grown[1:] += walks[:-1]
        grown[:-1] += walks[1:]
        grown[:, 1:] += walks[:, :-1]
        grown[:, :-1] += walks[:, 1:]
        walks = grown

    def count(a, d):
        return walks[STEPS + a, STEPS + d] if d <= STEPS else 0.0

    table = np.zeros((STEPS + 1, CB, CB), np.float32)
    for a in range(STEPS + 1):
        for b in range(CB):
            for c in range(CB):
                table[a, b, c] = (
                    count(a, abs(b - c)) + count(a, b + c + 1) + count(a, 2 * CB - 1 - b - c)
                )
    return table * WALK_SCALE


def dot(a, b, dims=(((1,), (0,)), ((), ()))):
    return lax.dot_general(a, b, dims, preferred_element_type=F32)


def channel_chunks():
    return [(c, min(16, CHAN - c)) for c in range(0, CHAN, 16)]


def jac_rows(jac_ref, level, c, width):
    rows = jac_ref[level, c : c + width, :].astype(F32)
    if width % 8:
        fill = jnp.zeros((8 - width % 8, OBS), F32)
        rows = jnp.concatenate([rows, fill], axis=0)
    return [rows[k : k + 8] for k in range(0, rows.shape[0], 8)]


def back_rows(jac_ref, base, vec_ref, probes, first, put):
    def trio(t, carry):
        levels = [jnp.minimum(first + 3 * t + k, LEVELS - 1) - base for k in range(3)]
        acc = {}
        for c, width in channel_chunks():
            vecs = [
                [vec_ref[p, c + 8 * k : c + 8 * k + 8, :] for k in range(-(-width // 8))]
                for p in range(probes)
            ]
            for n, level in enumerate(levels):
                for k, rows in enumerate(jac_rows(jac_ref, level, c, width)):
                    for p in range(probes):
                        term = rows * vecs[p][k]
                        acc[p, n] = acc[p, n] + term if (p, n) in acc else term
        for n in range(3):
            valid = first + 3 * t + n < LEVELS
            for p in range(probes):
                row = jnp.sum(acc[p, n], axis=0, keepdims=True)
                put(p, 3 * t + n, jnp.where(valid, row, 0.0))
        return carry

    lax.fori_loop(0, SLICE // 3, trio, 0)


def forward_block(jac_ref, prof_ref, img_ref, probes, first, count):
    weights = [
        [
            jnp.broadcast_to(prof_ref[pl.ds(p * FULL + first + level, 1), :], (8, OBS))
            for level in range(count)
        ]
        for p in range(probes)
    ]
    for c, width in channel_chunks():
        parts = -(-width // 8)
        acc = [
            [img_ref[p, c + 8 * k : c + 8 * k + 8, :] for k in range(parts)] for p in range(probes)
        ]
        for level in range(count):
            for k, rows in enumerate(jac_rows(jac_ref, first + level, c, width)):
                for p in range(probes):
                    acc[p][k] = acc[p][k] + rows * weights[p][level]
        for p in range(probes):
            for k in range(parts):
                img_ref[p, c + 8 * k : c + 8 * k + 8, :] = acc[p][k]


def jac_copy(jac_hbm, jac_ref, sems, k, count=BLOCK):
    levels = pl.ds(k * BLOCK, count)
    return pltpu.make_async_copy(jac_hbm.at[levels], jac_ref.at[levels], sems.at[k])


def start_jac(jac_hbm, jac_ref, sems):
    for k in range(BLOCKS):
        jac_copy(jac_hbm, jac_ref, sems, k, BLOCK if k < BLOCKS - 1 else REST).start()


def forward(jac_hbm, jac_ref, sems, prof_ref, img_ref, probes):
    def block(k, carry):
        jac_copy(jac_hbm, jac_ref, sems, k).wait()
        forward_block(jac_ref, prof_ref, img_ref, probes, k * BLOCK, BLOCK)
        return carry

    lax.fori_loop(0, BLOCKS - 1, block, 0)
    jac_copy(jac_hbm, jac_ref, sems, BLOCKS - 1, REST).wait()
    forward_block(jac_ref, prof_ref, img_ref, probes, (BLOCKS - 1) * BLOCK, REST)


JAC_SCRATCH = [pltpu.VMEM((LEVELS, CHAN, OBS), BF16), pltpu.SemaphoreType.DMA((BLOCKS,))]
HBM_SPEC = pl.BlockSpec(memory_space=pl.ANY)
COST = pl.CostEstimate(flops=4 * 10**7, bytes_accessed=10**7, transcendentals=0)


def copies(out_ref, message):
    message = message.astype(BF16)
    for d in range(TILES):
        out_ref[d] = message


def signs_kernel(
    part_ref, sketch_ref, test_ref, column_ref, slot_ref, jac_hbm, out_ref, jac, sem, vec, rows
):
    first = part_ref[0] * SLICE
    base = jnp.minimum(first, LEVELS - SLICE)
    copy = pltpu.make_async_copy(jac_hbm.at[pl.ds(base, SLICE)], jac, sem)
    copy.start()
    rows[...] = jnp.zeros_like(rows)
    for p in range(K):
        vec[p, 0:CHAN, :] = (2 * sketch_ref[p] - 1).astype(F32)
        vec[K + p, 0:CHAN, :] = (2 * test_ref[p] - 1).astype(F32)
        vec[p, CHAN:CPAD, :] = jnp.zeros((CPAD - CHAN, OBS), F32)
        vec[K + p, CHAN:CPAD, :] = jnp.zeros((CPAD - CHAN, OBS), F32)
    column = column_ref[...]
    rows[CODES : CODES + 1, :] = jnp.right_shift(column, 7).astype(F32)
    rows[CODES + 1 : CODES + 2, :] = (column & 127).astype(F32)
    rows[CODES + 2 : CODES + 3, :] = slot_ref[...].astype(F32)

    def put(p, level, row):
        rows[pl.ds(p * SLICE + level, 1), :] = row

    copy.wait()
    back_rows(jac, base, vec, 2 * K, first, put)
    copies(out_ref, rows[...])


def sign_adjoints(part, sketch, test, column, slot, jac):
    return pl.pallas_call(
        signs_kernel,
        compiler_params=WIDE,
        in_specs=[SMEM_SPEC] + [VMEM_SPEC] * 4 + [HBM_SPEC],
        out_specs=VMEM_SPEC,
        out_shape=jax.ShapeDtypeStruct((TILES, FIRST, OBS), BF16),
        scratch_shapes=[
            pltpu.VMEM((SLICE, CHAN, OBS), BF16),
            pltpu.SemaphoreType.DMA(()),
            pltpu.VMEM((2 * K, CPAD, OBS), F32),
            pltpu.VMEM((FIRST, OBS), F32),
        ],
        cost_estimate=pl.CostEstimate(flops=10**7, bytes_accessed=2 * 10**6, transcendentals=0),
    )(part, sketch, test, column, slot, jac)


def images_kernel(
    part_ref, mine_ref, other_ref, test_ref, jac_hbm, img_ref, out_ref, jac, sems, prof, rows
):
    start_jac(jac_hbm, jac, sems)
    core = part_ref[0] % 2
    rows[...] = jnp.zeros_like(rows)
    img_ref[...] = jnp.zeros_like(img_ref)
    prof[...] = jnp.where(core == 0, mine_ref[...].astype(F32), other_ref[...].astype(F32))
    forward(jac_hbm, jac, sems, prof, img_ref, K)

    def put(p, level, row):
        rows[pl.ds(p * SLICE + level, 1), :] = row

    back_rows(jac, 0, img_ref, K, part_ref[0] * SLICE, put)
    lanes = lax.broadcasted_iota(jnp.int32, (1, OBS), 1)
    gram = jnp.zeros((1, OBS), F32)
    for i in range(K):
        for j in range(K):
            if j <= i:
                value = jnp.sum(img_ref[i] * img_ref[j])
                gram = jnp.where(lanes == i * K + j, value, gram)
            signs = (2 * test_ref[j] - 1).astype(F32)
            value = jnp.sum(img_ref[i, 0:CHAN, :] * signs)
            gram = jnp.where(lanes == K * K + i * K + j, value, gram)
    high = gram.astype(BF16).astype(F32)
    mid = (gram - high).astype(BF16).astype(F32)
    rows[GRAMS : GRAMS + 1, :] = high
    rows[GRAMS + 1 : GRAMS + 2, :] = mid
    rows[GRAMS + 2 : GRAMS + 3, :] = gram - high - mid
    copies(out_ref, rows[...])


def images(part, mine, other, test, jac):
    return pl.pallas_call(
        images_kernel,
        compiler_params=WIDE,
        in_specs=[SMEM_SPEC, VMEM_SPEC, VMEM_SPEC, VMEM_SPEC, HBM_SPEC],
        out_specs=[VMEM_SPEC, VMEM_SPEC],
        out_shape=[
            jax.ShapeDtypeStruct((K, CPAD, OBS), F32),
            jax.ShapeDtypeStruct((TILES, SECOND, OBS), BF16),
        ],
        scratch_shapes=JAC_SCRATCH
        + [pltpu.VMEM((K * FULL, OBS), F32), pltpu.VMEM((SECOND, OBS), F32)],
        cost_estimate=COST,
    )(part, mine, other, test, jac)


def test_images_kernel(part_ref, mine_ref, other_ref, jac_hbm, img_ref, jac, sems, prof):
    start_jac(jac_hbm, jac, sems)
    core = part_ref[0] % 2
    img_ref[...] = jnp.zeros_like(img_ref)
    prof[...] = jnp.where(core == 0, other_ref[...].astype(F32), mine_ref[...].astype(F32))
    forward(jac_hbm, jac, sems, prof, img_ref, K)


def test_images(part, mine, other, jac):
    return pl.pallas_call(
        test_images_kernel,
        compiler_params=WIDE,
        in_specs=[SMEM_SPEC, VMEM_SPEC, VMEM_SPEC, HBM_SPEC],
        out_specs=VMEM_SPEC,
        out_shape=jax.ShapeDtypeStruct((K, CPAD, OBS), F32),
        scratch_shapes=JAC_SCRATCH + [pltpu.VMEM((K * FULL, OBS), F32)],
        cost_estimate=COST,
    )(part, mine, other, jac)


def outputs_kernel(
    size, part_ref, mine_ref, other_ref, second_ref, test_ref, y_ref, z_ref, jac_hbm,
    q_ref, w_ref, trace_ref, jac, sems, prof, x,
):
    start_jac(jac_hbm, jac, sems)
    half = K * FULL // 2
    core = part_ref[0] % 2
    mine, other = mine_ref[...].astype(F32), other_ref[...].astype(F32)
    x[...] = jnp.zeros_like(x)
    prof[0:half, :] = jnp.where(core == 0, mine, other)
    prof[half:, :] = jnp.where(core == 0, other, mine)
    forward(jac_hbm, jac, sems, prof, x, K)

    total = jnp.zeros((1, OBS), F32)
    for d in range(TILES):
        got = second_ref[d, GRAMS : GRAMS + 8, :].astype(F32)
        total = total + jnp.sum(got, axis=0, keepdims=True)
    lanes = lax.broadcasted_iota(jnp.int32, (1, OBS), 1)

    def entry(k):
        return jnp.sum(jnp.where(lanes == k, total, 0.0), axis=1, keepdims=True)

    g = [[entry(i * K + j) for j in range(i + 1)] for i in range(K)]
    c = [[entry(K * K + i * K + j) for j in range(K)] for i in range(K)]
    l00 = jnp.sqrt(g[0][0])
    l10, l20 = g[1][0] / l00, g[2][0] / l00
    l11 = jnp.sqrt(g[1][1] - l10 * l10)
    l21 = (g[2][1] - l20 * l10) / l11
    l22 = jnp.sqrt(g[2][2] - l20 * l20 - l21 * l21)
    i00, i11, i22 = 1.0 / l00, 1.0 / l11, 1.0 / l22
    i10 = -l10 * i00 * i11
    i21 = -l21 * i11 * i22
    i20 = -(l20 * i00 + l21 * i10) * i22
    inv = [[i00], [i10, i11], [i20, i21, i22]]
    root = size**0.5
    basis, image_q = [], []
    for j in range(K):
        b = q = None
        for i in range(j + 1):
            by, qx = root * inv[j][i] * y_ref[i, 0:CHAN, :], root * inv[j][i] * x[i, 0:CHAN, :]
            b, q = (by, qx) if b is None else (b + by, q + qx)
        q_ref[j] = q
        basis.append(b)
        image_q.append(q)
    trace_q = trace_w = None
    for j in range(K):
        w = z_ref[j, 0:CHAN, :]
        rest = (2 * test_ref[j] - 1).astype(F32)
        for i in range(K):
            share = sum(inv[i][k] * c[k][j] for k in range(i + 1)) / root
            w = w - share * image_q[i]
            rest = rest - share * basis[i]
        w_ref[j] = w
        tq, tw = basis[j] * image_q[j], rest * w
        trace_q, trace_w = (tq, tw) if trace_q is None else (trace_q + tq, trace_w + tw)
    row = jnp.where(lanes == 0, jnp.sum(trace_q), jnp.sum(trace_w))
    for d in range(TILES):
        trace_ref[d] = jnp.broadcast_to(row, (8, OBS))


def outputs(size, part, mine, other, second, test, y, z, jac):
    return pl.pallas_call(
        functools.partial(outputs_kernel, size),
        compiler_params=WIDE,
        in_specs=[SMEM_SPEC] + [VMEM_SPEC] * 6 + [HBM_SPEC],
        out_specs=[VMEM_SPEC] * 3,
        out_shape=[
            jax.ShapeDtypeStruct((K, CHAN, OBS), F32),
            jax.ShapeDtypeStruct((K, CHAN, OBS), F32),
            jax.ShapeDtypeStruct((TILES, 8, OBS), F32),
        ],
        scratch_shapes=JAC_SCRATCH
        + [pltpu.VMEM((K * FULL, OBS), F32), pltpu.VMEM((K, CPAD, OBS), F32)],
        cost_estimate=COST,
    )(part, mine, other, second, test, y, z, jac)


CHIPS = SLICES // 2


def parity_kernel(part_ref, members_ref, keep_ref, send_ref):
    core = part_ref[0] % 2
    for chip in range(CHIPS):
        keep_ref[chip] = members_ref[2 * chip + core]
        send_ref[chip] = members_ref[2 * chip + 1 - core]


def by_parity(part, members):
    half = jax.ShapeDtypeStruct((CHIPS, *members.shape[1:]), BF16)
    return pl.pallas_call(
        parity_kernel,
        compiler_params=LIMIT,
        in_specs=[SMEM_SPEC, VMEM_SPEC],
        out_specs=[VMEM_SPEC, VMEM_SPEC],
        out_shape=[half, half],
    )(part, members)


def split_kernel(part_ref, keep_ref, got_ref, *out_refs):
    for k in range(CHIPS):
        chip = lax.rem(part_ref[0] // 2 + k, CHIPS)
        out_refs[k][0:PIECE, :] = keep_ref[chip]
        out_refs[k][PIECE:, :] = got_ref[chip]


def split(part, keep, got):
    pair = jax.ShapeDtypeStruct((2 * PIECE, keep.shape[2]), BF16)
    return pl.pallas_call(
        split_kernel,
        compiler_params=LIMIT,
        in_specs=[SMEM_SPEC, VMEM_SPEC, VMEM_SPEC],
        out_specs=[VMEM_SPEC] * CHIPS,
        out_shape=[pair] * CHIPS,
    )(part, keep, got)


def pick_kernel(place_ref, first_ref, *refs):
    pairs = refs[:CHIPS]
    out_ref, members, chosen = refs[CHIPS:]
    cells = members.shape[1]
    core = place_ref[1] % 2
    for k in range(CHIPS):
        source = lax.rem(place_ref[1] // 2 + CHIPS - k, CHIPS) * 2
        for n, owner in enumerate((core, 1 - core)):
            at = pl.multiple_of((source + owner) * PIECE, PIECE)
            members[pl.ds(at, PIECE), :] = pairs[k][n * PIECE : (n + 1) * PIECE, :]
    tile = place_ref[0].astype(F32)
    slots = lax.broadcasted_iota(jnp.int32, (CAP, OBS), 0).astype(F32)
    lanes = lax.broadcasted_iota(jnp.int32, (CAP, cells), 1).astype(F32)
    for d in range(TILES):
        codes = first_ref[d, CODES:FIRST, :].astype(F32)
        cell = codes[0:1] * 128.0 + codes[1:2] - tile * float(cells)
        inside = (cell >= 0.0) & (cell < float(cells))
        here = jnp.where((slots == codes[2:3]) & inside, cell + 1.0, 0.0)
        at = jnp.sum(here, axis=1, keepdims=True) - 1.0
        chosen[d * CAP : (d + 1) * CAP, :] = jnp.where(lanes == at, 1.0, 0.0).astype(BF16)
    out_ref[...] = dot(chosen[...], members[...], NT).astype(BF16)


def pick(place, first, pieces):
    cells = pieces[0].shape[1]
    return pl.pallas_call(
        pick_kernel,
        compiler_params=LIMIT,
        in_specs=[SMEM_SPEC] + [VMEM_SPEC] * (1 + CHIPS),
        out_specs=VMEM_SPEC,
        out_shape=jax.ShapeDtypeStruct((TILES * CAP, SLICES * PIECE), BF16),
        scratch_shapes=[
            pltpu.VMEM((SLICES * PIECE, cells), BF16),
            pltpu.VMEM((TILES * CAP, cells), BF16),
        ],
    )(place, first, *pieces)


def own_kernel(pos_ref, recv_ref, out_ref, all_ref):
    rows = lax.broadcasted_iota(jnp.int32, (TILES * CAP, OBS), 0)
    chosen = jnp.where(rows == pos_ref[...], 1.0, 0.0).astype(BF16)
    mine = dot(recv_ref[...].T, chosen).astype(BF16)
    shape = (SLICE * MEMBERS, SLICES * PIECE)
    row = lax.broadcasted_iota(jnp.int32, shape, 0)
    lane = lax.broadcasted_iota(jnp.int32, shape, 1)
    level, member = jnp.right_shift(row, 4), row & 15
    source = jnp.right_shift(member, 1) * PIECE + 2 * level + (member & 1)
    turn = jnp.where(lane == source, 1.0, 0.0).astype(BF16)
    mine = dot(turn, mine)
    out_ref[...] = mine.astype(BF16)
    copies(all_ref, mine)


def own(position, recv):
    rows = SLICE * MEMBERS
    return pl.pallas_call(
        own_kernel,
        compiler_params=LIMIT,
        in_specs=[VMEM_SPEC, VMEM_SPEC],
        out_specs=[VMEM_SPEC, VMEM_SPEC],
        out_shape=[
            jax.ShapeDtypeStruct((rows, OBS), BF16),
            jax.ShapeDtypeStruct((TILES, rows, OBS), BF16),
        ],
    )(position, recv)


def pair_kernel(mine_ref, got_ref, out_ref):
    rows = mine_ref.shape[0]
    out_ref[0:rows, :] = mine_ref[...]
    out_ref[rows:, :] = got_ref[...]


def paired(mine, got):
    return pl.pallas_call(
        pair_kernel,
        compiler_params=LIMIT,
        in_specs=[VMEM_SPEC, VMEM_SPEC],
        out_specs=VMEM_SPEC,
        out_shape=jax.ShapeDtypeStruct((2 * mine.shape[0], OBS), BF16),
    )(mine, got)


def gathered_kernel(part_ref, *refs):
    rows = SLICE * MEMBERS
    pairs = refs[:CHIPS]
    out_ref, mem = refs[CHIPS:]
    chip, core = part_ref[0] // 2, part_ref[0] % 2
    for k in range(CHIPS):
        source = lax.rem(chip + CHIPS - k, CHIPS) * 2
        for n, owner in enumerate((core, 1 - core)):
            at = pl.multiple_of((source + owner) * rows, rows)
            mem[pl.ds(at, rows), :] = pairs[k][n * rows : (n + 1) * rows, :].astype(F32)
    for m in range(MEMBERS):
        out_ref[m * FULL : (m + 1) * FULL, :] = mem[pl.ds(m, FULL, stride=MEMBERS), :]


def gathered(part, pairs):
    return pl.pallas_call(
        gathered_kernel,
        compiler_params=LIMIT,
        in_specs=[SMEM_SPEC] + [VMEM_SPEC] * CHIPS,
        out_specs=VMEM_SPEC,
        out_shape=jax.ShapeDtypeStruct((MEMBERS * FULL, OBS), F32),
        scratch_shapes=[pltpu.VMEM((MEMBERS * FULL, OBS), F32)],
        cost_estimate=pl.CostEstimate(flops=10**6, bytes_accessed=2 * 10**6, transcendentals=0),
    )(part, *pairs)


def near_kernel(col_ref, first_ref, table_ref, out_ref):
    mine = col_ref[...]
    my_x = (mine // CB).astype(F32)
    my_b = mine % CB
    hot = jnp.where(lax.broadcasted_iota(jnp.int32, (OBS, CB), 1) == my_b, 1.0, 0.0).astype(BF16)
    reach = [dot(hot, table_ref[a]).astype(BF16) for a in range(STEPS + 1)]
    rows = lax.broadcasted_iota(jnp.int32, (CB, OBS), 0)
    for d in range(TILES):
        codes = first_ref[d, CODES:FIRST, :].astype(F32).astype(jnp.int32)
        hi, lo = codes[0:1], codes[1:2]
        x = (hi * 4 + lo // CB).astype(F32)
        there = jnp.where(rows == lo % CB, 1.0, 0.0).astype(BF16)
        gap = jnp.abs(my_x - x)
        gap = jnp.minimum(gap, float(NX) - gap)
        total = jnp.zeros((OBS, OBS), F32)
        for a in range(STEPS + 1):
            total = jnp.where(gap == float(a), dot(reach[a], there), total)
        out_ref[:, d * OBS : (d + 1) * OBS] = total.astype(BF16)


def near_of(column, first, table):
    return pl.pallas_call(
        near_kernel,
        compiler_params=LIMIT,
        in_specs=[VMEM_SPEC, VMEM_SPEC, VMEM_SPEC],
        out_specs=VMEM_SPEC,
        out_shape=jax.ShapeDtypeStruct((OBS, TILES * OBS), BF16),
        cost_estimate=pl.CostEstimate(flops=2 * 10**7, bytes_accessed=4 * 10**6, transcendentals=0),
    )(column, first, table)


def covariance_kernel(
    probes, scale, part_ref, all_ref, adj_ref, near_ref, mem_ref, vert_ref, keep_ref, send_ref,
    prod, acc, adj, out,
):
    rows = SLICE * MEMBERS
    adj[...] = adj_ref[...].astype(F32)

    def probe(p, carry):
        for d in range(TILES):
            for level in range(SLICE):
                row = adj[d, pl.ds(p * SLICE + level, 1), :]
                row = jnp.broadcast_to(row, (MEMBERS, OBS)).astype(BF16)
                at = slice(level * MEMBERS, (level + 1) * MEMBERS)
                prod[at, d * OBS : (d + 1) * OBS] = all_ref[d, at, :] * row
        acc[pl.ds(pl.multiple_of(p * rows, rows), rows), :] = dot(prod[...], near_ref[...], NT)
        return carry

    lax.fori_loop(0, probes, probe, 0)
    vert = vert_ref[...]
    for p in range(probes):
        total = None
        for m in range(MEMBERS):
            smooth = acc[pl.ds(p * rows + m, SLICE, stride=MEMBERS), :].astype(BF16)
            term = mem_ref[m * FULL : (m + 1) * FULL, :] * dot(vert, smooth)
            total = term if total is None else total + term
        out[p * FULL : (p + 1) * FULL, :] = total * scale
    half = probes * FULL // 2
    core = part_ref[0] % 2
    low, high = out[0:half, :], out[half:, :]
    keep_ref[...] = jnp.where(core == 0, low, high).astype(BF16)
    send_ref[...] = jnp.where(core == 0, high, low).astype(BF16)


def covariance(probes, scale, part, everyone, adjoints, near, mem, vert):
    rows = SLICE * MEMBERS
    half = jax.ShapeDtypeStruct((probes * FULL // 2, OBS), BF16)
    return pl.pallas_call(
        functools.partial(covariance_kernel, probes, scale),
        compiler_params=LIMIT,
        in_specs=[SMEM_SPEC] + [VMEM_SPEC] * 5,
        out_specs=[VMEM_SPEC, VMEM_SPEC],
        out_shape=[half, half],
        scratch_shapes=[
            pltpu.VMEM((rows, TILES * OBS), BF16),
            pltpu.VMEM((probes * rows, OBS), F32),
            pltpu.VMEM(adjoints.shape, F32),
            pltpu.VMEM((probes * FULL, OBS), F32),
        ],
    )(part, everyone, adjoints, near, mem, vert)


def exchange(value, axis):
    return lax.all_to_all(value, axis, 0, 0, tiled=True)


def swap_cores(value):
    return lax.ppermute(value, "mem", [(j, j ^ 1) for j in range(SLICES)])


def to_other_chip(value, k):
    return lax.ppermute(value, "mem", [(j, (j + 2 * k) % SLICES) for j in range(SLICES)])


def from_other_chips(value):
    return [to_other_chip(value, k) for k in range(1, CHIPS)]


def sum_over_mem(keep, send):
    kept = (keep.astype(F32) + swap_cores(send).astype(F32)).astype(BF16)
    others = from_other_chips(kept)
    total = (kept.astype(F32) + others[1].astype(F32)) + (
        others[0].astype(F32) + others[2].astype(F32)
    )
    total = total.astype(BF16)
    return total, swap_cores(total)


def on_device(members, vertical, jacobian, sketch_bits, test_bits, obs_column, obs_slot):
    slice_id = lax.axis_index("mem").astype(jnp.int32)
    part = slice_id.reshape(1)
    my_tile = lax.axis_index(TILE).astype(jnp.int32)
    local, levels, cells = members.shape
    size = float(OBS * TILES * CHAN)
    scale = 1.0 / ((MEMBERS - 1) * 5.0**STEPS * WALK_SCALE)

    jac = jnp.transpose(jacobian, (2, 1, 0))
    sketch = jnp.swapaxes(sketch_bits, 1, 2)
    test = jnp.swapaxes(test_bits, 1, 2)
    column, slot = obs_column.reshape(1, OBS), obs_slot.reshape(1, OBS)
    first = sign_adjoints(part, sketch, test, column, slot, jac)
    first, members = lax.optimization_barrier((first, members))
    first = exchange(first, TILE)

    padded = jnp.pad(jnp.swapaxes(members, 0, 1), ((0, FULL - levels), (0, 0), (0, 0)))
    padded = padded.reshape(SLICES, SLICE * local, cells)
    padded = jnp.pad(padded, ((0, 0), (0, PIECE - SLICE * local), (0, 0)))
    keep, send = by_parity(part, padded)
    pairs = list(split(part, keep, swap_cores(send)))
    for k in range(1, CHIPS):
        pairs[k] = to_other_chip(pairs[k], k)

    picked = pick(jnp.stack([my_tile, slice_id]), first, pairs)
    arrived = exchange(picked.reshape(TILES, CAP, -1), TILE)
    position = (obs_column // cells * CAP + obs_slot).reshape(1, OBS)
    mine, everyone = own(position, arrived.reshape(TILES * CAP, -1))
    everyone = exchange(everyone, TILE)
    near = near_of(obs_column.reshape(OBS, 1), first, jnp.asarray(walk_table(), BF16))
    pair = paired(mine, swap_cores(mine))
    mem = gathered(part, [pair] + from_other_chips(pair))

    vert = jnp.pad(vertical, ((0, FULL - levels), (0, FULL - levels)))
    vert = lax.dynamic_slice_in_dim(vert, slice_id * SLICE, SLICE, axis=1)

    halves = covariance(2 * K, scale, part, everyone, first, near, mem, vert)
    mine_1, other_1 = sum_over_mem(*halves)
    y, second = images(part, mine_1, other_1, test, jac)
    second = exchange(second, TILE)
    z = test_images(part, mine_1, other_1, jac)
    second, z = lax.optimization_barrier((second, z))
    halves = covariance(K, scale, part, everyone, second, near, mem, vert)
    mine_2, other_2 = sum_over_mem(*halves)
    image_q, image_w, traces = outputs(size, part, mine_2, other_2, second, test, y, z, jac)
    traces = exchange(traces, TILE)[:, 0, :].sum(axis=0)
    trace_q, trace_w = traces[0], traces[1]
    trace_mean = trace_q / (size * size) + trace_w / (K * size)
    return (
        jnp.swapaxes(image_q, 1, 2),
        jnp.swapaxes(image_w, 1, 2),
        trace_mean,
        trace_q / (K * size),
    )


def solution(mesh):
    finer = Mesh(mesh.devices.reshape(mesh.shape["mem"], 4, 4), ("mem", "tile_0", "tile_1"))
    return jax.shard_map(
        on_device,
        mesh=finer,
        in_specs=(
            P("mem", None, TILE),
            P(),
            P(TILE, None, None),
            P(None, TILE, None),
            P(None, TILE, None),
            P(TILE),
            P(TILE),
        ),
        out_specs=(P(None, TILE, None), P(None, TILE, None), P(), P()),
        check_vma=False,
    )
```

```python
import functools

import jax
import jax.numpy as jnp
import numpy as np
from jax import lax
from jax.experimental import pallas as pl
from jax.experimental.pallas import tpu as pltpu
from jax.sharding import Mesh
from jax.sharding import PartitionSpec as P

CB = 32
NX = 256
K = 3
STEPS = 6
TILE = ("tile_0", "tile_1")
TILES = 16
SLICES = 8
LEVELS = 137
SLICE = 18
FULL = SLICES * SLICE
MEMBERS = 16
PIECE = 48
CAP = 32
OBS = 128
CHAN = 231
CPAD = 240
BLOCK = 9
BLOCKS = -(-LEVELS // BLOCK)
REST = LEVELS - (BLOCKS - 1) * BLOCK
CODES = 112
FIRST = 120
GRAMS = 56
SECOND = 64


LIMIT = pltpu.CompilerParams(vmem_limit_bytes=24 * 2**20)
WIDE = pltpu.CompilerParams(vmem_limit_bytes=59000000)
F32 = jnp.float32
BF16 = jnp.bfloat16
VMEM_SPEC = pl.BlockSpec(memory_space=pltpu.VMEM)
SMEM_SPEC = pl.BlockSpec(memory_space=pltpu.SMEM)
NT = (((1,), (1,)), ((), ()))

WALK_SCALE = 1.3338


def walk_table():
    walks = np.zeros((2 * STEPS + 1, 2 * STEPS + 1))
    walks[STEPS, STEPS] = 1
    for _ in range(STEPS):
        grown = walks.copy()
        grown[1:] += walks[:-1]
        grown[:-1] += walks[1:]
        grown[:, 1:] += walks[:, :-1]
        grown[:, :-1] += walks[:, 1:]
        walks = grown

    def count(a, d):
        return walks[STEPS + a, STEPS + d] if d <= STEPS else 0.0

    table = np.zeros((STEPS + 1, CB, CB), np.float32)
    for a in range(STEPS + 1):
        for b in range(CB):
            for c in range(CB):
                table[a, b, c] = (
                    count(a, abs(b - c)) + count(a, b + c + 1) + count(a, 2 * CB - 1 - b - c)
                )
    return table * WALK_SCALE


def dot(a, b, dims=(((1,), (0,)), ((), ()))):
    return lax.dot_general(a, b, dims, preferred_element_type=F32)


def channel_chunks():
    return [(c, min(16, CHAN - c)) for c in range(0, CHAN, 16)]


def jac_rows(jac_ref, level, c, width):
    rows = jac_ref[level, c : c + width, :].astype(F32)
    if width % 8:
        fill = jnp.zeros((8 - width % 8, OBS), F32)
        rows = jnp.concatenate([rows, fill], axis=0)
    return [rows[k : k + 8] for k in range(0, rows.shape[0], 8)]


def back_rows(jac_ref, base, vec_ref, probes, first, put):
    def trio(t, carry):
        levels = [jnp.minimum(first + 3 * t + k, LEVELS - 1) - base for k in range(3)]
        acc = {}
        for c, width in channel_chunks():
            vecs = [
                [vec_ref[p, c + 8 * k : c + 8 * k + 8, :] for k in range(-(-width // 8))]
                for p in range(probes)
            ]
            for n, level in enumerate(levels):
                for k, rows in enumerate(jac_rows(jac_ref, level, c, width)):
                    for p in range(probes):
                        term = rows * vecs[p][k]
                        acc[p, n] = acc[p, n] + term if (p, n) in acc else term
        for n in range(3):
            valid = first + 3 * t + n < LEVELS
            for p in range(probes):
                row = jnp.sum(acc[p, n], axis=0, keepdims=True)
                put(p, 3 * t + n, jnp.where(valid, row, 0.0))
        return carry

    lax.fori_loop(0, SLICE // 3, trio, 0)


def forward_block(jac_ref, prof_ref, img_ref, probes, first, count):
    weights = [
        [
            jnp.broadcast_to(prof_ref[pl.ds(p * FULL + first + level, 1), :], (8, OBS))
            for level in range(count)
        ]
        for p in range(probes)
    ]
    for c, width in channel_chunks():
        parts = -(-width // 8)
        acc = [
            [img_ref[p, c + 8 * k : c + 8 * k + 8, :] for k in range(parts)] for p in range(probes)
        ]
        for level in range(count):
            for k, rows in enumerate(jac_rows(jac_ref, first + level, c, width)):
                for p in range(probes):
                    acc[p][k] = acc[p][k] + rows * weights[p][level]
        for p in range(probes):
            for k in range(parts):
                img_ref[p, c + 8 * k : c + 8 * k + 8, :] = acc[p][k]


def jac_copy(jac_hbm, jac_ref, sems, k, count=BLOCK):
    levels = pl.ds(k * BLOCK, count)
    return pltpu.make_async_copy(jac_hbm.at[levels], jac_ref.at[levels], sems.at[k])


def start_jac(jac_hbm, jac_ref, sems):
    for k in range(BLOCKS):
        jac_copy(jac_hbm, jac_ref, sems, k, BLOCK if k < BLOCKS - 1 else REST).start()


def forward(jac_hbm, jac_ref, sems, prof_ref, img_ref, probes):
    def block(k, carry):
        jac_copy(jac_hbm, jac_ref, sems, k).wait()
        forward_block(jac_ref, prof_ref, img_ref, probes, k * BLOCK, BLOCK)
        return carry

    lax.fori_loop(0, BLOCKS - 1, block, 0)
    jac_copy(jac_hbm, jac_ref, sems, BLOCKS - 1, REST).wait()
    forward_block(jac_ref, prof_ref, img_ref, probes, (BLOCKS - 1) * BLOCK, REST)


JAC_SCRATCH = [pltpu.VMEM((LEVELS, CHAN, OBS), BF16), pltpu.SemaphoreType.DMA((BLOCKS,))]
HBM_SPEC = pl.BlockSpec(memory_space=pl.ANY)
COST = pl.CostEstimate(flops=4 * 10**7, bytes_accessed=10**7, transcendentals=0)


def copies(out_ref, message):
    message = message.astype(BF16)
    for d in range(TILES):
        out_ref[d] = message


def signs_kernel(
    part_ref, sketch_ref, test_ref, column_ref, slot_ref, jac_hbm, out_ref, jac, sem, vec, rows
):
    first = part_ref[0] * SLICE
    base = jnp.minimum(first, LEVELS - SLICE)
    copy = pltpu.make_async_copy(jac_hbm.at[pl.ds(base, SLICE)], jac, sem)
    copy.start()
    rows[...] = jnp.zeros_like(rows)
    for p in range(K):
        vec[p, 0:CHAN, :] = (2 * sketch_ref[p] - 1).astype(F32)
        vec[K + p, 0:CHAN, :] = (2 * test_ref[p] - 1).astype(F32)
        vec[p, CHAN:CPAD, :] = jnp.zeros((CPAD - CHAN, OBS), F32)
        vec[K + p, CHAN:CPAD, :] = jnp.zeros((CPAD - CHAN, OBS), F32)
    column = column_ref[...]
    rows[CODES : CODES + 1, :] = jnp.right_shift(column, 7).astype(F32)
    rows[CODES + 1 : CODES + 2, :] = (column & 127).astype(F32)
    rows[CODES + 2 : CODES + 3, :] = slot_ref[...].astype(F32)

    def put(p, level, row):
        rows[pl.ds(p * SLICE + level, 1), :] = row

    copy.wait()
    back_rows(jac, base, vec, 2 * K, first, put)
    copies(out_ref, rows[...])


def sign_adjoints(part, sketch, test, column, slot, jac):
    return pl.pallas_call(
        signs_kernel,
        compiler_params=WIDE,
        in_specs=[SMEM_SPEC] + [VMEM_SPEC] * 4 + [HBM_SPEC],
        out_specs=VMEM_SPEC,
        out_shape=jax.ShapeDtypeStruct((TILES, FIRST, OBS), BF16),
        scratch_shapes=[
            pltpu.VMEM((SLICE, CHAN, OBS), BF16),
            pltpu.SemaphoreType.DMA(()),
            pltpu.VMEM((2 * K, CPAD, OBS), F32),
            pltpu.VMEM((FIRST, OBS), F32),
        ],
        cost_estimate=pl.CostEstimate(flops=10**7, bytes_accessed=2 * 10**6, transcendentals=0),
    )(part, sketch, test, column, slot, jac)


def images_kernel(
    part_ref, mine_ref, other_ref, test_ref, jac_hbm, img_ref, out_ref, jac, sems, prof, rows
):
    start_jac(jac_hbm, jac, sems)
    core = part_ref[0] % 2
    rows[...] = jnp.zeros_like(rows)
    img_ref[...] = jnp.zeros_like(img_ref)
    prof[...] = jnp.where(core == 0, mine_ref[...].astype(F32), other_ref[...].astype(F32))
    forward(jac_hbm, jac, sems, prof, img_ref, K)

    def put(p, level, row):
        rows[pl.ds(p * SLICE + level, 1), :] = row

    back_rows(jac, 0, img_ref, K, part_ref[0] * SLICE, put)
    lanes = lax.broadcasted_iota(jnp.int32, (1, OBS), 1)
    gram = jnp.zeros((1, OBS), F32)
    for i in range(K):
        for j in range(K):
            if j <= i:
                value = jnp.sum(img_ref[i] * img_ref[j])
                gram = jnp.where(lanes == i * K + j, value, gram)
            signs = (2 * test_ref[j] - 1).astype(F32)
            value = jnp.sum(img_ref[i, 0:CHAN, :] * signs)
            gram = jnp.where(lanes == K * K + i * K + j, value, gram)
    high = gram.astype(BF16).astype(F32)
    mid = (gram - high).astype(BF16).astype(F32)
    rows[GRAMS : GRAMS + 1, :] = high
    rows[GRAMS + 1 : GRAMS + 2, :] = mid
    rows[GRAMS + 2 : GRAMS + 3, :] = gram - high - mid
    copies(out_ref, rows[...])


def images(part, mine, other, test, jac):
    return pl.pallas_call(
        images_kernel,
        compiler_params=WIDE,
        in_specs=[SMEM_SPEC, VMEM_SPEC, VMEM_SPEC, VMEM_SPEC, HBM_SPEC],
        out_specs=[VMEM_SPEC, VMEM_SPEC],
        out_shape=[
            jax.ShapeDtypeStruct((K, CPAD, OBS), F32),
            jax.ShapeDtypeStruct((TILES, SECOND, OBS), BF16),
        ],
        scratch_shapes=JAC_SCRATCH
        + [pltpu.VMEM((K * FULL, OBS), F32), pltpu.VMEM((SECOND, OBS), F32)],
        cost_estimate=COST,
    )(part, mine, other, test, jac)


def test_images_kernel(part_ref, mine_ref, other_ref, jac_hbm, img_ref, jac, sems, prof):
    start_jac(jac_hbm, jac, sems)
    core = part_ref[0] % 2
    img_ref[...] = jnp.zeros_like(img_ref)
    prof[...] = jnp.where(core == 0, other_ref[...].astype(F32), mine_ref[...].astype(F32))
    forward(jac_hbm, jac, sems, prof, img_ref, K)


def test_images(part, mine, other, jac):
    return pl.pallas_call(
        test_images_kernel,
        compiler_params=WIDE,
        in_specs=[SMEM_SPEC, VMEM_SPEC, VMEM_SPEC, HBM_SPEC],
        out_specs=VMEM_SPEC,
        out_shape=jax.ShapeDtypeStruct((K, CPAD, OBS), F32),
        scratch_shapes=JAC_SCRATCH + [pltpu.VMEM((K * FULL, OBS), F32)],
        cost_estimate=COST,
    )(part, mine, other, jac)


def outputs_kernel(
    size, part_ref, mine_ref, other_ref, second_ref, test_ref, y_ref, z_ref, jac_hbm,
    q_ref, w_ref, trace_ref, jac, sems, prof, x,
):
    start_jac(jac_hbm, jac, sems)
    half = K * FULL // 2
    core = part_ref[0] % 2
    mine, other = mine_ref[...].astype(F32), other_ref[...].astype(F32)
    x[...] = jnp.zeros_like(x)
    prof[0:half, :] = jnp.where(core == 0, mine, other)
    prof[half:, :] = jnp.where(core == 0, other, mine)
    forward(jac_hbm, jac, sems, prof, x, K)

    total = jnp.zeros((1, OBS), F32)
    for d in range(TILES):
        got = second_ref[d, GRAMS : GRAMS + 8, :].astype(F32)
        total = total + jnp.sum(got, axis=0, keepdims=True)
    lanes = lax.broadcasted_iota(jnp.int32, (1, OBS), 1)

    def entry(k):
        return jnp.sum(jnp.where(lanes == k, total, 0.0), axis=1, keepdims=True)

    g = [[entry(i * K + j) for j in range(i + 1)] for i in range(K)]
    c = [[entry(K * K + i * K + j) for j in range(K)] for i in range(K)]
    l00 = jnp.sqrt(g[0][0])
    l10, l20 = g[1][0] / l00, g[2][0] / l00
    l11 = jnp.sqrt(g[1][1] - l10 * l10)
    l21 = (g[2][1] - l20 * l10) / l11
    l22 = jnp.sqrt(g[2][2] - l20 * l20 - l21 * l21)
    i00, i11, i22 = 1.0 / l00, 1.0 / l11, 1.0 / l22
    i10 = -l10 * i00 * i11
    i21 = -l21 * i11 * i22
    i20 = -(l20 * i00 + l21 * i10) * i22
    inv = [[i00], [i10, i11], [i20, i21, i22]]
    root = size**0.5
    basis, image_q = [], []
    for j in range(K):
        b = q = None
        for i in range(j + 1):
            by, qx = root * inv[j][i] * y_ref[i, 0:CHAN, :], root * inv[j][i] * x[i, 0:CHAN, :]
            b, q = (by, qx) if b is None else (b + by, q + qx)
        q_ref[j] = q
        basis.append(b)
        image_q.append(q)
    trace_q = trace_w = None
    for j in range(K):
        w = z_ref[j, 0:CHAN, :]
        rest = (2 * test_ref[j] - 1).astype(F32)
        for i in range(K):
            share = sum(inv[i][k] * c[k][j] for k in range(i + 1)) / root
            w = w - share * image_q[i]
            rest = rest - share * basis[i]
        w_ref[j] = w
        tq, tw = basis[j] * image_q[j], rest * w
        trace_q, trace_w = (tq, tw) if trace_q is None else (trace_q + tq, trace_w + tw)
    row = jnp.where(lanes == 0, jnp.sum(trace_q), jnp.sum(trace_w))
    for d in range(TILES):
        trace_ref[d] = jnp.broadcast_to(row, (8, OBS))


def outputs(size, part, mine, other, second, test, y, z, jac):
    return pl.pallas_call(
        functools.partial(outputs_kernel, size),
        compiler_params=LIMIT,
        in_specs=[SMEM_SPEC] + [VMEM_SPEC] * 6 + [HBM_SPEC],
        out_specs=[VMEM_SPEC] * 3,
        out_shape=[
            jax.ShapeDtypeStruct((K, CHAN, OBS), F32),
            jax.ShapeDtypeStruct((K, CHAN, OBS), F32),
            jax.ShapeDtypeStruct((TILES, 8, OBS), F32),
        ],
        scratch_shapes=JAC_SCRATCH
        + [pltpu.VMEM((K * FULL, OBS), F32), pltpu.VMEM((K, CPAD, OBS), F32)],
        cost_estimate=COST,
    )(part, mine, other, second, test, y, z, jac)


CHIPS = SLICES // 2


def parity_kernel(part_ref, members_ref, keep_ref, send_ref):
    core = part_ref[0] % 2
    for chip in range(CHIPS):
        keep_ref[chip] = members_ref[2 * chip + core]
        send_ref[chip] = members_ref[2 * chip + 1 - core]


def by_parity(part, members):
    half = jax.ShapeDtypeStruct((CHIPS, *members.shape[1:]), BF16)
    return pl.pallas_call(
        parity_kernel,
        compiler_params=LIMIT,
        in_specs=[SMEM_SPEC, VMEM_SPEC],
        out_specs=[VMEM_SPEC, VMEM_SPEC],
        out_shape=[half, half],
    )(part, members)


def split_kernel(part_ref, keep_ref, got_ref, *out_refs):
    for k in range(CHIPS):
        chip = lax.rem(part_ref[0] // 2 + k, CHIPS)
        out_refs[k][0:PIECE, :] = keep_ref[chip]
        out_refs[k][PIECE:, :] = got_ref[chip]


def split(part, keep, got):
    pair = jax.ShapeDtypeStruct((2 * PIECE, keep.shape[2]), BF16)
    return pl.pallas_call(
        split_kernel,
        compiler_params=LIMIT,
        in_specs=[SMEM_SPEC, VMEM_SPEC, VMEM_SPEC],
        out_specs=[VMEM_SPEC] * CHIPS,
        out_shape=[pair] * CHIPS,
    )(part, keep, got)


def pick_kernel(place_ref, first_ref, *refs):
    pairs = refs[:CHIPS]
    out_ref, members, chosen = refs[CHIPS:]
    cells = members.shape[1]
    core = place_ref[1] % 2
    for k in range(CHIPS):
        source = lax.rem(place_ref[1] // 2 + CHIPS - k, CHIPS) * 2
        for n, owner in enumerate((core, 1 - core)):
            at = pl.multiple_of((source + owner) * PIECE, PIECE)
            members[pl.ds(at, PIECE), :] = pairs[k][n * PIECE : (n + 1) * PIECE, :]
    tile = place_ref[0].astype(F32)
    slots = lax.broadcasted_iota(jnp.int32, (CAP, OBS), 0).astype(F32)
    lanes = lax.broadcasted_iota(jnp.int32, (CAP, cells), 1).astype(F32)
    for d in range(TILES):
        codes = first_ref[d, CODES:FIRST, :].astype(F32)
        cell = codes[0:1] * 128.0 + codes[1:2] - tile * float(cells)
        inside = (cell >= 0.0) & (cell < float(cells))
        here = jnp.where((slots == codes[2:3]) & inside, cell + 1.0, 0.0)
        at = jnp.sum(here, axis=1, keepdims=True) - 1.0
        chosen[d * CAP : (d + 1) * CAP, :] = jnp.where(lanes == at, 1.0, 0.0).astype(BF16)
    out_ref[...] = dot(chosen[...], members[...], NT).astype(BF16)


def pick(place, first, pieces):
    cells = pieces[0].shape[1]
    return pl.pallas_call(
        pick_kernel,
        compiler_params=LIMIT,
        in_specs=[SMEM_SPEC] + [VMEM_SPEC] * (1 + CHIPS),
        out_specs=VMEM_SPEC,
        out_shape=jax.ShapeDtypeStruct((TILES * CAP, SLICES * PIECE), BF16),
        scratch_shapes=[
            pltpu.VMEM((SLICES * PIECE, cells), BF16),
            pltpu.VMEM((TILES * CAP, cells), BF16),
        ],
    )(place, first, *pieces)


def own_kernel(pos_ref, recv_ref, out_ref, all_ref):
    rows = lax.broadcasted_iota(jnp.int32, (TILES * CAP, OBS), 0)
    chosen = jnp.where(rows == pos_ref[...], 1.0, 0.0).astype(BF16)
    mine = dot(recv_ref[...].T, chosen).astype(BF16)
    shape = (SLICE * MEMBERS, SLICES * PIECE)
    row = lax.broadcasted_iota(jnp.int32, shape, 0)
    lane = lax.broadcasted_iota(jnp.int32, shape, 1)
    level, member = jnp.right_shift(row, 4), row & 15
    source = jnp.right_shift(member, 1) * PIECE + 2 * level + (member & 1)
    turn = jnp.where(lane == source, 1.0, 0.0).astype(BF16)
    mine = dot(turn, mine)
    out_ref[...] = mine.astype(BF16)
    copies(all_ref, mine)


def own(position, recv):
    rows = SLICE * MEMBERS
    return pl.pallas_call(
        own_kernel,
        compiler_params=LIMIT,
        in_specs=[VMEM_SPEC, VMEM_SPEC],
        out_specs=[VMEM_SPEC, VMEM_SPEC],
        out_shape=[
            jax.ShapeDtypeStruct((rows, OBS), BF16),
            jax.ShapeDtypeStruct((TILES, rows, OBS), BF16),
        ],
    )(position, recv)


def pair_kernel(mine_ref, got_ref, out_ref):
    rows = mine_ref.shape[0]
    out_ref[0:rows, :] = mine_ref[...]
    out_ref[rows:, :] = got_ref[...]


def paired(mine, got):
    return pl.pallas_call(
        pair_kernel,
        compiler_params=LIMIT,
        in_specs=[VMEM_SPEC, VMEM_SPEC],
        out_specs=VMEM_SPEC,
        out_shape=jax.ShapeDtypeStruct((2 * mine.shape[0], OBS), BF16),
    )(mine, got)


def gathered_kernel(part_ref, *refs):
    rows = SLICE * MEMBERS
    pairs = refs[:CHIPS]
    out_ref, mem = refs[CHIPS:]
    chip, core = part_ref[0] // 2, part_ref[0] % 2
    for k in range(CHIPS):
        source = lax.rem(chip + CHIPS - k, CHIPS) * 2
        for n, owner in enumerate((core, 1 - core)):
            at = pl.multiple_of((source + owner) * rows, rows)
            mem[pl.ds(at, rows), :] = pairs[k][n * rows : (n + 1) * rows, :].astype(F32)
    for m in range(MEMBERS):
        out_ref[m * FULL : (m + 1) * FULL, :] = mem[pl.ds(m, FULL, stride=MEMBERS), :]


def gathered(part, pairs):
    return pl.pallas_call(
        gathered_kernel,
        compiler_params=LIMIT,
        in_specs=[SMEM_SPEC] + [VMEM_SPEC] * CHIPS,
        out_specs=VMEM_SPEC,
        out_shape=jax.ShapeDtypeStruct((MEMBERS * FULL, OBS), F32),
        scratch_shapes=[pltpu.VMEM((MEMBERS * FULL, OBS), F32)],
        cost_estimate=pl.CostEstimate(flops=10**6, bytes_accessed=2 * 10**6, transcendentals=0),
    )(part, *pairs)


def near_kernel(col_ref, first_ref, table_ref, out_ref):
    mine = col_ref[...]
    my_x = (mine // CB).astype(F32)
    my_b = mine % CB
    hot = jnp.where(lax.broadcasted_iota(jnp.int32, (OBS, CB), 1) == my_b, 1.0, 0.0).astype(BF16)
    reach = [dot(hot, table_ref[a]).astype(BF16) for a in range(STEPS + 1)]
    rows = lax.broadcasted_iota(jnp.int32, (CB, OBS), 0)
    for d in range(TILES):
        codes = first_ref[d, CODES:FIRST, :].astype(F32).astype(jnp.int32)
        hi, lo = codes[0:1], codes[1:2]
        x = (hi * 4 + lo // CB).astype(F32)
        there = jnp.where(rows == lo % CB, 1.0, 0.0).astype(BF16)
        gap = jnp.abs(my_x - x)
        gap = jnp.minimum(gap, float(NX) - gap)
        total = jnp.zeros((OBS, OBS), F32)
        for a in range(STEPS + 1):
            total = jnp.where(gap == float(a), dot(reach[a], there), total)
        out_ref[:, d * OBS : (d + 1) * OBS] = total.astype(BF16)


def near_of(column, first, table):
    return pl.pallas_call(
        near_kernel,
        compiler_params=LIMIT,
        in_specs=[VMEM_SPEC, VMEM_SPEC, VMEM_SPEC],
        out_specs=VMEM_SPEC,
        out_shape=jax.ShapeDtypeStruct((OBS, TILES * OBS), BF16),
        cost_estimate=pl.CostEstimate(flops=2 * 10**7, bytes_accessed=4 * 10**6, transcendentals=0),
    )(column, first, table)


def covariance_kernel(
    probes, scale, part_ref, all_ref, adj_ref, near_ref, mem_ref, vert_ref, keep_ref, send_ref,
    prod, acc, adj, out,
):
    rows = SLICE * MEMBERS
    adj[...] = adj_ref[...].astype(F32)

    def probe(p, carry):
        for d in range(TILES):
            for level in range(SLICE):
                row = adj[d, pl.ds(p * SLICE + level, 1), :]
                row = jnp.broadcast_to(row, (MEMBERS, OBS)).astype(BF16)
                at = slice(level * MEMBERS, (level + 1) * MEMBERS)
                prod[at, d * OBS : (d + 1) * OBS] = all_ref[d, at, :] * row
        acc[pl.ds(pl.multiple_of(p * rows, rows), rows), :] = dot(prod[...], near_ref[...], NT)
        return carry

    lax.fori_loop(0, probes, probe, 0)
    vert = vert_ref[...]
    for p in range(probes):
        total = None
        for m in range(MEMBERS):
            smooth = acc[pl.ds(p * rows + m, SLICE, stride=MEMBERS), :].astype(BF16)
            term = mem_ref[m * FULL : (m + 1) * FULL, :] * dot(vert, smooth)
            total = term if total is None else total + term
        out[p * FULL : (p + 1) * FULL, :] = total * scale
    half = probes * FULL // 2
    core = part_ref[0] % 2
    low, high = out[0:half, :], out[half:, :]
    keep_ref[...] = jnp.where(core == 0, low, high).astype(BF16)
    send_ref[...] = jnp.where(core == 0, high, low).astype(BF16)


def covariance(probes, scale, part, everyone, adjoints, near, mem, vert):
    rows = SLICE * MEMBERS
    half = jax.ShapeDtypeStruct((probes * FULL // 2, OBS), BF16)
    return pl.pallas_call(
        functools.partial(covariance_kernel, probes, scale),
        compiler_params=LIMIT,
        in_specs=[SMEM_SPEC] + [VMEM_SPEC] * 5,
        out_specs=[VMEM_SPEC, VMEM_SPEC],
        out_shape=[half, half],
        scratch_shapes=[
            pltpu.VMEM((rows, TILES * OBS), BF16),
            pltpu.VMEM((probes * rows, OBS), F32),
            pltpu.VMEM(adjoints.shape, F32),
            pltpu.VMEM((probes * FULL, OBS), F32),
        ],
    )(part, everyone, adjoints, near, mem, vert)


def exchange(value, axis):
    return lax.all_to_all(value, axis, 0, 0, tiled=True)


def swap_cores(value):
    return lax.ppermute(value, "mem", [(j, j ^ 1) for j in range(SLICES)])


def to_other_chip(value, k):
    return lax.ppermute(value, "mem", [(j, (j + 2 * k) % SLICES) for j in range(SLICES)])


def from_other_chips(value):
    return [to_other_chip(value, k) for k in range(1, CHIPS)]


def sum_over_mem(keep, send):
    kept = (keep.astype(F32) + swap_cores(send).astype(F32)).astype(BF16)
    others = from_other_chips(kept)
    total = (kept.astype(F32) + others[1].astype(F32)) + (
        others[0].astype(F32) + others[2].astype(F32)
    )
    total = total.astype(BF16)
    return total, swap_cores(total)


def on_device(members, vertical, jacobian, sketch_bits, test_bits, obs_column, obs_slot):
    slice_id = lax.axis_index("mem").astype(jnp.int32)
    part = slice_id.reshape(1)
    my_tile = lax.axis_index(TILE).astype(jnp.int32)
    local, levels, cells = members.shape
    size = float(OBS * TILES * CHAN)
    scale = 1.0 / ((MEMBERS - 1) * 5.0**STEPS * WALK_SCALE)

    jac = pltpu.with_memory_space_constraint(jnp.transpose(jacobian, (2, 1, 0)), pltpu.HBM)
    sketch = jnp.swapaxes(sketch_bits, 1, 2)
    test = jnp.swapaxes(test_bits, 1, 2)
    column, slot = obs_column.reshape(1, OBS), obs_slot.reshape(1, OBS)
    first = sign_adjoints(part, sketch, test, column, slot, jac)
    first, members = lax.optimization_barrier((first, members))
    first = exchange(first, TILE)

    padded = jnp.pad(jnp.swapaxes(members, 0, 1), ((0, FULL - levels), (0, 0), (0, 0)))
    padded = padded.reshape(SLICES, SLICE * local, cells)
    padded = jnp.pad(padded, ((0, 0), (0, PIECE - SLICE * local), (0, 0)))
    keep, send = by_parity(part, padded)
    pairs = list(split(part, keep, swap_cores(send)))
    for k in range(1, CHIPS):
        pairs[k] = to_other_chip(pairs[k], k)

    picked = pick(jnp.stack([my_tile, slice_id]), first, pairs)
    arrived = exchange(picked.reshape(TILES, CAP, -1), TILE)
    near = near_of(obs_column.reshape(OBS, 1), first, jnp.asarray(walk_table(), BF16))
    vert = jnp.pad(vertical, ((0, FULL - levels), (0, FULL - levels)))
    vert = lax.dynamic_slice_in_dim(vert, slice_id * SLICE, SLICE, axis=1)
    arrived, near, vert = lax.optimization_barrier((arrived, near, vert))
    position = (obs_column // cells * CAP + obs_slot).reshape(1, OBS)
    mine, everyone = own(position, arrived.reshape(TILES * CAP, -1))
    everyone = exchange(everyone, TILE)
    pair = paired(mine, swap_cores(mine))
    mem = gathered(part, [pair] + from_other_chips(pair))

    halves = covariance(2 * K, scale, part, everyone, first, near, mem, vert)
    mine_1, other_1 = sum_over_mem(*halves)
    y, second = images(part, mine_1, other_1, test, jac)
    second = exchange(second, TILE)
    z = test_images(part, mine_1, other_1, jac)
    second, z = lax.optimization_barrier((second, z))
    halves = covariance(K, scale, part, everyone, second, near, mem, vert)
    mine_2, other_2 = sum_over_mem(*halves)
    image_q, image_w, traces = outputs(size, part, mine_2, other_2, second, test, y, z, jac)
    traces = exchange(traces, TILE)[:, 0, :].sum(axis=0)
    trace_q, trace_w = traces[0], traces[1]
    trace_mean = trace_q / (size * size) + trace_w / (K * size)
    return (
        jnp.swapaxes(image_q, 1, 2),
        jnp.swapaxes(image_w, 1, 2),
        trace_mean,
        trace_q / (K * size),
    )


def solution(mesh):
    finer = Mesh(mesh.devices.reshape(mesh.shape["mem"], 4, 4), ("mem", "tile_0", "tile_1"))
    return jax.shard_map(
        on_device,
        mesh=finer,
        in_specs=(
            P("mem", None, TILE),
            P(),
            P(TILE, None, None),
            P(None, TILE, None),
            P(None, TILE, None),
            P(TILE),
            P(TILE),
        ),
        out_specs=(P(None, TILE, None), P(None, TILE, None), P(), P()),
        check_vma=False,
    )
```

```python
import functools

import jax
import jax.numpy as jnp
import numpy as np
from jax import lax
from jax.experimental import pallas as pl
from jax.experimental.pallas import tpu as pltpu
from jax.sharding import Mesh
from jax.sharding import PartitionSpec as P

CB = 32
NX = 256
K = 3
STEPS = 6
TILE = ("tile_0", "tile_1")
TILES = 16
SLICES = 8
LEVELS = 137
SLICE = 18
FULL = SLICES * SLICE
MEMBERS = 16
PIECE = 48
CAP = 32
OBS = 128
CHAN = 231
CPAD = 240
BLOCK = 9
BLOCKS = -(-LEVELS // BLOCK)
REST = LEVELS - (BLOCKS - 1) * BLOCK
CODES = 112
FIRST = 120
GRAMS = 56
SECOND = 64


LIMIT = pltpu.CompilerParams(vmem_limit_bytes=24 * 2**20)
WIDE = pltpu.CompilerParams(vmem_limit_bytes=59000000)
F32 = jnp.float32
BF16 = jnp.bfloat16
VMEM_SPEC = pl.BlockSpec(memory_space=pltpu.VMEM)
SMEM_SPEC = pl.BlockSpec(memory_space=pltpu.SMEM)
NT = (((1,), (1,)), ((), ()))

WALK_SCALE = 1.3338


def walk_table():
    walks = np.zeros((2 * STEPS + 1, 2 * STEPS + 1))
    walks[STEPS, STEPS] = 1
    for _ in range(STEPS):
        grown = walks.copy()
        grown[1:] += walks[:-1]
        grown[:-1] += walks[1:]
        grown[:, 1:] += walks[:, :-1]
        grown[:, :-1] += walks[:, 1:]
        walks = grown

    def count(a, d):
        return walks[STEPS + a, STEPS + d] if d <= STEPS else 0.0

    table = np.zeros((STEPS + 1, CB, CB), np.float32)
    for a in range(STEPS + 1):
        for b in range(CB):
            for c in range(CB):
                table[a, b, c] = (
                    count(a, abs(b - c)) + count(a, b + c + 1) + count(a, 2 * CB - 1 - b - c)
                )
    return table * WALK_SCALE


def dot(a, b, dims=(((1,), (0,)), ((), ()))):
    return lax.dot_general(a, b, dims, preferred_element_type=F32)


def channel_chunks():
    return [(c, min(16, CHAN - c)) for c in range(0, CHAN, 16)]


def jac_rows(jac_ref, level, c, width):
    rows = jac_ref[level, c : c + width, :].astype(F32)
    if width % 8:
        fill = jnp.zeros((8 - width % 8, OBS), F32)
        rows = jnp.concatenate([rows, fill], axis=0)
    return [rows[k : k + 8] for k in range(0, rows.shape[0], 8)]


def back_rows(jac_ref, base, vec_ref, probes, first, put):
    def trio(t, carry):
        levels = [jnp.minimum(first + 3 * t + k, LEVELS - 1) - base for k in range(3)]
        acc = {}
        for c, width in channel_chunks():
            vecs = [
                [vec_ref[p, c + 8 * k : c + 8 * k + 8, :] for k in range(-(-width // 8))]
                for p in range(probes)
            ]
            for n, level in enumerate(levels):
                for k, rows in enumerate(jac_rows(jac_ref, level, c, width)):
                    for p in range(probes):
                        term = rows * vecs[p][k]
                        acc[p, n] = acc[p, n] + term if (p, n) in acc else term
        for n in range(3):
            valid = first + 3 * t + n < LEVELS
            for p in range(probes):
                row = jnp.sum(acc[p, n], axis=0, keepdims=True)
                put(p, 3 * t + n, jnp.where(valid, row, 0.0))
        return carry

    lax.fori_loop(0, SLICE // 3, trio, 0)


def forward_block(jac_ref, prof_ref, img_ref, probes, first, count):
    weights = [
        [
            jnp.broadcast_to(prof_ref[pl.ds(p * FULL + first + level, 1), :], (8, OBS))
            for level in range(count)
        ]
        for p in range(probes)
    ]
    for c, width in channel_chunks():
        parts = -(-width // 8)
        acc = [
            [img_ref[p, c + 8 * k : c + 8 * k + 8, :] for k in range(parts)] for p in range(probes)
        ]
        for level in range(count):
            for k, rows in enumerate(jac_rows(jac_ref, first + level, c, width)):
                for p in range(probes):
                    acc[p][k] = acc[p][k] + rows * weights[p][level]
        for p in range(probes):
            for k in range(parts):
                img_ref[p, c + 8 * k : c + 8 * k + 8, :] = acc[p][k]


def jac_copy(jac_hbm, jac_ref, sems, k, count=BLOCK):
    levels = pl.ds(k * BLOCK, count)
    return pltpu.make_async_copy(jac_hbm.at[levels], jac_ref.at[levels], sems.at[k])


def start_jac(jac_hbm, jac_ref, sems):
    for k in range(BLOCKS):
        jac_copy(jac_hbm, jac_ref, sems, k, BLOCK if k < BLOCKS - 1 else REST).start()


def forward(jac_hbm, jac_ref, sems, prof_ref, img_ref, probes):
    def block(k, carry):
        jac_copy(jac_hbm, jac_ref, sems, k).wait()
        forward_block(jac_ref, prof_ref, img_ref, probes, k * BLOCK, BLOCK)
        return carry

    lax.fori_loop(0, BLOCKS - 1, block, 0)
    jac_copy(jac_hbm, jac_ref, sems, BLOCKS - 1, REST).wait()
    forward_block(jac_ref, prof_ref, img_ref, probes, (BLOCKS - 1) * BLOCK, REST)


JAC_SCRATCH = [pltpu.VMEM((LEVELS, CHAN, OBS), BF16), pltpu.SemaphoreType.DMA((BLOCKS,))]
HBM_SPEC = pl.BlockSpec(memory_space=pl.ANY)
COST = pl.CostEstimate(flops=4 * 10**7, bytes_accessed=10**7, transcendentals=0)


def copies(out_ref, message):
    message = message.astype(BF16)
    for d in range(TILES):
        out_ref[d] = message


def signs_kernel(
    part_ref, sketch_ref, test_ref, column_ref, slot_ref, jac_hbm, out_ref, jac, sem, vec, rows
):
    first = part_ref[0] * SLICE
    base = jnp.minimum(first, LEVELS - SLICE)
    copy = pltpu.make_async_copy(jac_hbm.at[pl.ds(base, SLICE)], jac, sem)
    copy.start()
    rows[...] = jnp.zeros_like(rows)
    for p in range(K):
        vec[p, 0:CHAN, :] = (2 * sketch_ref[p] - 1).astype(F32)
        vec[K + p, 0:CHAN, :] = (2 * test_ref[p] - 1).astype(F32)
        vec[p, CHAN:CPAD, :] = jnp.zeros((CPAD - CHAN, OBS), F32)
        vec[K + p, CHAN:CPAD, :] = jnp.zeros((CPAD - CHAN, OBS), F32)
    column = column_ref[...]
    rows[CODES : CODES + 1, :] = jnp.right_shift(column, 7).astype(F32)
    rows[CODES + 1 : CODES + 2, :] = (column & 127).astype(F32)
    rows[CODES + 2 : CODES + 3, :] = slot_ref[...].astype(F32)

    def put(p, level, row):
        rows[pl.ds(p * SLICE + level, 1), :] = row

    copy.wait()
    back_rows(jac, base, vec, 2 * K, first, put)
    copies(out_ref, rows[...])


def sign_adjoints(part, sketch, test, column, slot, jac):
    return pl.pallas_call(
        signs_kernel,
        compiler_params=WIDE,
        in_specs=[SMEM_SPEC] + [VMEM_SPEC] * 4 + [HBM_SPEC],
        out_specs=VMEM_SPEC,
        out_shape=jax.ShapeDtypeStruct((TILES, FIRST, OBS), BF16),
        scratch_shapes=[
            pltpu.VMEM((SLICE, CHAN, OBS), BF16),
            pltpu.SemaphoreType.DMA(()),
            pltpu.VMEM((2 * K, CPAD, OBS), F32),
            pltpu.VMEM((FIRST, OBS), F32),
        ],
        cost_estimate=pl.CostEstimate(flops=10**7, bytes_accessed=2 * 10**6, transcendentals=0),
    )(part, sketch, test, column, slot, jac)


def images_kernel(
    part_ref, mine_ref, other_ref, test_ref, jac_hbm, img_ref, out_ref, jac, sems, prof, rows
):
    start_jac(jac_hbm, jac, sems)
    core = part_ref[0] % 2
    rows[...] = jnp.zeros_like(rows)
    img_ref[...] = jnp.zeros_like(img_ref)
    prof[...] = jnp.where(core == 0, mine_ref[...].astype(F32), other_ref[...].astype(F32))
    forward(jac_hbm, jac, sems, prof, img_ref, K)

    def put(p, level, row):
        rows[pl.ds(p * SLICE + level, 1), :] = row

    back_rows(jac, 0, img_ref, K, part_ref[0] * SLICE, put)
    lanes = lax.broadcasted_iota(jnp.int32, (1, OBS), 1)
    gram = jnp.zeros((1, OBS), F32)
    for i in range(K):
        for j in range(K):
            if j <= i:
                value = jnp.sum(img_ref[i] * img_ref[j])
                gram = jnp.where(lanes == i * K + j, value, gram)
            signs = (2 * test_ref[j] - 1).astype(F32)
            value = jnp.sum(img_ref[i, 0:CHAN, :] * signs)
            gram = jnp.where(lanes == K * K + i * K + j, value, gram)
    high = gram.astype(BF16).astype(F32)
    mid = (gram - high).astype(BF16).astype(F32)
    rows[GRAMS : GRAMS + 1, :] = high
    rows[GRAMS + 1 : GRAMS + 2, :] = mid
    rows[GRAMS + 2 : GRAMS + 3, :] = gram - high - mid
    copies(out_ref, rows[...])


def images(part, mine, other, test, jac):
    return pl.pallas_call(
        images_kernel,
        compiler_params=WIDE,
        in_specs=[SMEM_SPEC, VMEM_SPEC, VMEM_SPEC, VMEM_SPEC, HBM_SPEC],
        out_specs=[VMEM_SPEC, VMEM_SPEC],
        out_shape=[
            jax.ShapeDtypeStruct((K, CPAD, OBS), F32),
            jax.ShapeDtypeStruct((TILES, SECOND, OBS), BF16),
        ],
        scratch_shapes=JAC_SCRATCH
        + [pltpu.VMEM((K * FULL, OBS), F32), pltpu.VMEM((SECOND, OBS), F32)],
        cost_estimate=COST,
    )(part, mine, other, test, jac)


def test_images_kernel(part_ref, mine_ref, other_ref, jac_hbm, img_ref, jac, sems, prof):
    start_jac(jac_hbm, jac, sems)
    core = part_ref[0] % 2
    img_ref[...] = jnp.zeros_like(img_ref)
    prof[...] = jnp.where(core == 0, other_ref[...].astype(F32), mine_ref[...].astype(F32))
    forward(jac_hbm, jac, sems, prof, img_ref, K)


def test_images(part, mine, other, jac):
    return pl.pallas_call(
        test_images_kernel,
        compiler_params=WIDE,
        in_specs=[SMEM_SPEC, VMEM_SPEC, VMEM_SPEC, HBM_SPEC],
        out_specs=VMEM_SPEC,
        out_shape=jax.ShapeDtypeStruct((K, CPAD, OBS), F32),
        scratch_shapes=JAC_SCRATCH + [pltpu.VMEM((K * FULL, OBS), F32)],
        cost_estimate=COST,
    )(part, mine, other, jac)


def coefficients(gram_ref, size):
    total = jnp.zeros((1, OBS), F32)
    for d in range(TILES):
        total = total + jnp.sum(gram_ref[d].astype(F32), axis=0, keepdims=True)
    entry = functools.partial(lane_of, total)
    g = [[entry(i * K + j) for j in range(i + 1)] for i in range(K)]
    c = [[entry(K * K + i * K + j) for j in range(K)] for i in range(K)]
    l00 = jnp.sqrt(g[0][0])
    l10, l20 = g[1][0] / l00, g[2][0] / l00
    l11 = jnp.sqrt(g[1][1] - l10 * l10)
    l21 = (g[2][1] - l20 * l10) / l11
    l22 = jnp.sqrt(g[2][2] - l20 * l20 - l21 * l21)
    i00, i11, i22 = 1.0 / l00, 1.0 / l11, 1.0 / l22
    i10 = -l10 * i00 * i11
    i21 = -l21 * i11 * i22
    i20 = -(l20 * i00 + l21 * i10) * i22
    inv = [[i00], [i10, i11], [i20, i21, i22]]
    root = size**0.5
    lower = [[root * value for value in row] for row in inv]
    share = [
        [sum(inv[i][k] * c[k][j] for k in range(i + 1)) / root for j in range(K)] for i in range(K)
    ]
    return lower, share


def lane_of(row, k):
    lanes = lax.broadcasted_iota(jnp.int32, row.shape, 1)
    return jnp.sum(jnp.where(lanes == k, row, 0.0), axis=1, keepdims=True)


def row_of(values):
    lanes = lax.broadcasted_iota(jnp.int32, (1, OBS), 1)
    row = jnp.zeros((1, OBS), F32)
    for k, value in enumerate(values):
        row = jnp.where(lanes == k, value, row)
    return row


def second_profiles(core, mine_ref, other_ref, prof):
    half = K * FULL // 2
    mine, other = mine_ref[...].astype(F32), other_ref[...].astype(F32)
    prof[0:half, :] = jnp.where(core == 0, mine, other)
    prof[half:, :] = jnp.where(core == 0, other, mine)


def inner_kernel(
    place_ref, mine_1_ref, other_1_ref, mine_2_ref, other_2_ref, first_ref, second_ref, out_ref,
    test_prof, prof,
):
    tile, part = place_ref[0], place_ref[1]
    core = part % 2
    second_profiles(core, mine_2_ref, other_2_ref, prof)
    test_prof[...] = jnp.where(
        core == 0, other_1_ref[...].astype(F32), mine_1_ref[...].astype(F32)
    )
    sign = first_ref[tile].astype(F32)
    image = second_ref[tile].astype(F32)
    signs = [sign[(K + j) * SLICE : (K + j + 1) * SLICE] for j in range(K)]
    images = [image[k * SLICE : (k + 1) * SLICE] for k in range(K)]
    tests = [test_prof[pl.ds(j * FULL + part * SLICE, SLICE), :] for j in range(K)]
    profs = [prof[pl.ds(j * FULL + part * SLICE, SLICE), :] for j in range(K)]
    values = [jnp.sum(images[k] * profs[j]) for k in range(K) for j in range(K)]
    values += [jnp.sum(tests[j] * images[k]) for j in range(K) for k in range(K)]
    values += [jnp.sum(signs[j] * tests[j]) for j in range(K)]
    out_ref[...] = jnp.broadcast_to(row_of(values), out_ref.shape)


def inner_products(place, profiles_1, profiles_2, first, second):
    devices = SLICES * TILES
    return pl.pallas_call(
        inner_kernel,
        compiler_params=LIMIT,
        in_specs=[SMEM_SPEC] + [VMEM_SPEC] * 6,
        out_specs=VMEM_SPEC,
        out_shape=jax.ShapeDtypeStruct((devices, OBS), F32),
        scratch_shapes=[pltpu.VMEM((K * FULL, OBS), F32), pltpu.VMEM((K * FULL, OBS), F32)],
    )(place, *profiles_1, *profiles_2, first, second)


def outputs_kernel(
    size, part_ref, mine_ref, other_ref, gram_ref, z_ref, jac_hbm, q_ref, w_ref, coef_ref,
    jac, sems, prof, x,
):
    start_jac(jac_hbm, jac, sems)
    x[...] = jnp.zeros_like(x)
    second_profiles(part_ref[0] % 2, mine_ref, other_ref, prof)
    lower, share = coefficients(gram_ref, size)
    coef_ref[...] = row_of([v for row in lower for v in row] + [v for row in share for v in row])
    forward(jac_hbm, jac, sems, prof, x, K)
    image_q = []
    for j in range(K):
        q = None
        for i in range(j + 1):
            qx = lower[j][i] * x[i, 0:CHAN, :]
            q = qx if q is None else q + qx
        q_ref[j] = q
        image_q.append(q)
    for j in range(K):
        w = z_ref[j, 0:CHAN, :]
        for i in range(K):
            w = w - share[i][j] * image_q[i]
        w_ref[j] = w


def outputs(size, part, mine, other, grams, z, jac):
    return pl.pallas_call(
        functools.partial(outputs_kernel, size),
        compiler_params=WIDE,
        in_specs=[SMEM_SPEC] + [VMEM_SPEC] * 4 + [HBM_SPEC],
        out_specs=[VMEM_SPEC] * 3,
        out_shape=[
            jax.ShapeDtypeStruct((K, CHAN, OBS), F32),
            jax.ShapeDtypeStruct((K, CHAN, OBS), F32),
            jax.ShapeDtypeStruct((1, OBS), F32),
        ],
        scratch_shapes=JAC_SCRATCH
        + [pltpu.VMEM((K * FULL, OBS), F32), pltpu.VMEM((K, CPAD, OBS), F32)],
        cost_estimate=COST,
    )(part, mine, other, grams, z, jac)


def traces_kernel(size, parts_ref, coef_ref, out_ref):
    total = functools.partial(lane_of, jnp.sum(parts_ref[...], axis=0, keepdims=True))
    coef = functools.partial(lane_of, coef_ref[...])
    lower = [[coef(j * (j + 1) // 2 + i) for i in range(j + 1)] for j in range(K)]
    share = [[coef(2 * K + i * K + j) for j in range(K)] for i in range(K)]
    yx = [[total(k * K + j) for j in range(K)] for k in range(K)]
    zy = [[total(K * K + j * K + k) for k in range(K)] for j in range(K)]
    tz = [total(2 * K * K + j) for j in range(K)]
    quad = [
        [
            sum(
                lower[i][a] * lower[k][b] * yx[a][b]
                for a in range(i + 1)
                for b in range(k + 1)
            )
            for k in range(K)
        ]
        for i in range(K)
    ]
    cross = [
        [sum(lower[i][b] * zy[j][b] for b in range(i + 1)) for j in range(K)] for i in range(K)
    ]
    trace_q = quad[0][0] + quad[1][1] + quad[2][2]
    trace_w = 0.0
    for j in range(K):
        trace_w = trace_w + tz[j]
        for i in range(K):
            trace_w = trace_w - 2.0 * share[i][j] * cross[i][j]
            for k in range(K):
                trace_w = trace_w + share[i][j] * share[k][j] * quad[i][k]
    mean = trace_q / (size * size) + trace_w / (K * size)
    out_ref[...] = row_of([mean, trace_q / (K * size)])


def traces(size, parts, coefs):
    return pl.pallas_call(
        functools.partial(traces_kernel, size),
        compiler_params=LIMIT,
        in_specs=[VMEM_SPEC, VMEM_SPEC],
        out_specs=VMEM_SPEC,
        out_shape=jax.ShapeDtypeStruct((1, OBS), F32),
    )(parts, coefs)


CHIPS = SLICES // 2


def parity_kernel(part_ref, members_ref, keep_ref, send_ref):
    core = part_ref[0] % 2
    for chip in range(CHIPS):
        keep_ref[chip] = members_ref[2 * chip + core]
        send_ref[chip] = members_ref[2 * chip + 1 - core]


def by_parity(part, members):
    half = jax.ShapeDtypeStruct((CHIPS, *members.shape[1:]), BF16)
    return pl.pallas_call(
        parity_kernel,
        compiler_params=LIMIT,
        in_specs=[SMEM_SPEC, VMEM_SPEC],
        out_specs=[VMEM_SPEC, VMEM_SPEC],
        out_shape=[half, half],
    )(part, members)


def split_kernel(part_ref, keep_ref, got_ref, *out_refs):
    for k in range(CHIPS):
        chip = lax.rem(part_ref[0] // 2 + k, CHIPS)
        out_refs[k][0:PIECE, :] = keep_ref[chip]
        out_refs[k][PIECE:, :] = got_ref[chip]


def split(part, keep, got):
    pair = jax.ShapeDtypeStruct((2 * PIECE, keep.shape[2]), BF16)
    return pl.pallas_call(
        split_kernel,
        compiler_params=LIMIT,
        in_specs=[SMEM_SPEC, VMEM_SPEC, VMEM_SPEC],
        out_specs=[VMEM_SPEC] * CHIPS,
        out_shape=[pair] * CHIPS,
    )(part, keep, got)


def pick_kernel(place_ref, first_ref, *refs):
    pairs = refs[:CHIPS]
    out_ref, members, chosen = refs[CHIPS:]
    cells = members.shape[1]
    core = place_ref[1] % 2
    for k in range(CHIPS):
        source = lax.rem(place_ref[1] // 2 + CHIPS - k, CHIPS) * 2
        for n, owner in enumerate((core, 1 - core)):
            at = pl.multiple_of((source + owner) * PIECE, PIECE)
            members[pl.ds(at, PIECE), :] = pairs[k][n * PIECE : (n + 1) * PIECE, :]
    tile = place_ref[0].astype(F32)
    slots = lax.broadcasted_iota(jnp.int32, (CAP, OBS), 0).astype(F32)
    lanes = lax.broadcasted_iota(jnp.int32, (CAP, cells), 1).astype(F32)
    for d in range(TILES):
        codes = first_ref[d, CODES:FIRST, :].astype(F32)
        cell = codes[0:1] * 128.0 + codes[1:2] - tile * float(cells)
        inside = (cell >= 0.0) & (cell < float(cells))
        here = jnp.where((slots == codes[2:3]) & inside, cell + 1.0, 0.0)
        at = jnp.sum(here, axis=1, keepdims=True) - 1.0
        chosen[d * CAP : (d + 1) * CAP, :] = jnp.where(lanes == at, 1.0, 0.0).astype(BF16)
    out_ref[...] = dot(chosen[...], members[...], NT).astype(BF16)


def pick(place, first, pieces):
    cells = pieces[0].shape[1]
    return pl.pallas_call(
        pick_kernel,
        compiler_params=LIMIT,
        in_specs=[SMEM_SPEC] + [VMEM_SPEC] * (1 + CHIPS),
        out_specs=VMEM_SPEC,
        out_shape=jax.ShapeDtypeStruct((TILES * CAP, SLICES * PIECE), BF16),
        scratch_shapes=[
            pltpu.VMEM((SLICES * PIECE, cells), BF16),
            pltpu.VMEM((TILES * CAP, cells), BF16),
        ],
    )(place, first, *pieces)


def own_kernel(pos_ref, recv_ref, out_ref, all_ref):
    rows = lax.broadcasted_iota(jnp.int32, (TILES * CAP, OBS), 0)
    chosen = jnp.where(rows == pos_ref[...], 1.0, 0.0).astype(BF16)
    mine = dot(recv_ref[...].T, chosen).astype(BF16)
    shape = (SLICE * MEMBERS, SLICES * PIECE)
    row = lax.broadcasted_iota(jnp.int32, shape, 0)
    lane = lax.broadcasted_iota(jnp.int32, shape, 1)
    level, member = jnp.right_shift(row, 4), row & 15
    source = jnp.right_shift(member, 1) * PIECE + 2 * level + (member & 1)
    turn = jnp.where(lane == source, 1.0, 0.0).astype(BF16)
    mine = dot(turn, mine)
    out_ref[...] = mine.astype(BF16)
    copies(all_ref, mine)


def own(position, recv):
    rows = SLICE * MEMBERS
    return pl.pallas_call(
        own_kernel,
        compiler_params=LIMIT,
        in_specs=[VMEM_SPEC, VMEM_SPEC],
        out_specs=[VMEM_SPEC, VMEM_SPEC],
        out_shape=[
            jax.ShapeDtypeStruct((rows, OBS), BF16),
            jax.ShapeDtypeStruct((TILES, rows, OBS), BF16),
        ],
    )(position, recv)


def pair_kernel(mine_ref, got_ref, out_ref):
    rows = mine_ref.shape[0]
    out_ref[0:rows, :] = mine_ref[...]
    out_ref[rows:, :] = got_ref[...]


def paired(mine, got):
    return pl.pallas_call(
        pair_kernel,
        compiler_params=LIMIT,
        in_specs=[VMEM_SPEC, VMEM_SPEC],
        out_specs=VMEM_SPEC,
        out_shape=jax.ShapeDtypeStruct((2 * mine.shape[0], OBS), BF16),
    )(mine, got)


def gathered_kernel(part_ref, *refs):
    rows = SLICE * MEMBERS
    pairs = refs[:CHIPS]
    out_ref, mem = refs[CHIPS:]
    chip, core = part_ref[0] // 2, part_ref[0] % 2
    for k in range(CHIPS):
        source = lax.rem(chip + CHIPS - k, CHIPS) * 2
        for n, owner in enumerate((core, 1 - core)):
            at = pl.multiple_of((source + owner) * rows, rows)
            mem[pl.ds(at, rows), :] = pairs[k][n * rows : (n + 1) * rows, :].astype(F32)
    for m in range(MEMBERS):
        out_ref[m * FULL : (m + 1) * FULL, :] = mem[pl.ds(m, FULL, stride=MEMBERS), :]


def gathered(part, pairs):
    return pl.pallas_call(
        gathered_kernel,
        compiler_params=LIMIT,
        in_specs=[SMEM_SPEC] + [VMEM_SPEC] * CHIPS,
        out_specs=VMEM_SPEC,
        out_shape=jax.ShapeDtypeStruct((MEMBERS * FULL, OBS), F32),
        scratch_shapes=[pltpu.VMEM((MEMBERS * FULL, OBS), F32)],
        cost_estimate=pl.CostEstimate(flops=10**6, bytes_accessed=2 * 10**6, transcendentals=0),
    )(part, *pairs)


def near_kernel(col_ref, first_ref, table_ref, out_ref):
    mine = col_ref[...]
    my_x = (mine // CB).astype(F32)
    my_b = mine % CB
    hot = jnp.where(lax.broadcasted_iota(jnp.int32, (OBS, CB), 1) == my_b, 1.0, 0.0).astype(BF16)
    reach = [dot(hot, table_ref[a]).astype(BF16) for a in range(STEPS + 1)]
    rows = lax.broadcasted_iota(jnp.int32, (CB, OBS), 0)
    for d in range(TILES):
        codes = first_ref[d, CODES:FIRST, :].astype(F32).astype(jnp.int32)
        hi, lo = codes[0:1], codes[1:2]
        x = (hi * 4 + lo // CB).astype(F32)
        there = jnp.where(rows == lo % CB, 1.0, 0.0).astype(BF16)
        gap = jnp.abs(my_x - x)
        gap = jnp.minimum(gap, float(NX) - gap)
        total = jnp.zeros((OBS, OBS), F32)
        for a in range(STEPS + 1):
            total = jnp.where(gap == float(a), dot(reach[a], there), total)
        out_ref[:, d * OBS : (d + 1) * OBS] = total.astype(BF16)


def near_of(column, first, table):
    return pl.pallas_call(
        near_kernel,
        compiler_params=LIMIT,
        in_specs=[VMEM_SPEC, VMEM_SPEC, VMEM_SPEC],
        out_specs=VMEM_SPEC,
        out_shape=jax.ShapeDtypeStruct((OBS, TILES * OBS), BF16),
        cost_estimate=pl.CostEstimate(flops=2 * 10**7, bytes_accessed=4 * 10**6, transcendentals=0),
    )(column, first, table)


def covariance_kernel(
    probes, scale, part_ref, all_ref, adj_ref, near_ref, mem_ref, vert_ref, keep_ref, send_ref,
    prod, acc, adj, out,
):
    rows = SLICE * MEMBERS
    adj[...] = adj_ref[...].astype(F32)

    def probe(p, carry):
        for d in range(TILES):
            for level in range(SLICE):
                row = adj[d, pl.ds(p * SLICE + level, 1), :]
                row = jnp.broadcast_to(row, (MEMBERS, OBS)).astype(BF16)
                at = slice(level * MEMBERS, (level + 1) * MEMBERS)
                prod[at, d * OBS : (d + 1) * OBS] = all_ref[d, at, :] * row
        acc[pl.ds(pl.multiple_of(p * rows, rows), rows), :] = dot(prod[...], near_ref[...], NT)
        return carry

    lax.fori_loop(0, probes, probe, 0)
    vert = vert_ref[...]
    for p in range(probes):
        total = None
        for m in range(MEMBERS):
            smooth = acc[pl.ds(p * rows + m, SLICE, stride=MEMBERS), :].astype(BF16)
            term = mem_ref[m * FULL : (m + 1) * FULL, :] * dot(vert, smooth)
            total = term if total is None else total + term
        out[p * FULL : (p + 1) * FULL, :] = total * scale
    half = probes * FULL // 2
    core = part_ref[0] % 2
    low, high = out[0:half, :], out[half:, :]
    keep_ref[...] = jnp.where(core == 0, low, high).astype(BF16)
    send_ref[...] = jnp.where(core == 0, high, low).astype(BF16)


def covariance(probes, scale, part, everyone, adjoints, near, mem, vert):
    rows = SLICE * MEMBERS
    half = jax.ShapeDtypeStruct((probes * FULL // 2, OBS), BF16)
    return pl.pallas_call(
        functools.partial(covariance_kernel, probes, scale),
        compiler_params=LIMIT,
        in_specs=[SMEM_SPEC] + [VMEM_SPEC] * 5,
        out_specs=[VMEM_SPEC, VMEM_SPEC],
        out_shape=[half, half],
        scratch_shapes=[
            pltpu.VMEM((rows, TILES * OBS), BF16),
            pltpu.VMEM((probes * rows, OBS), F32),
            pltpu.VMEM(adjoints.shape, F32),
            pltpu.VMEM((probes * FULL, OBS), F32),
        ],
    )(part, everyone, adjoints, near, mem, vert)


def exchange(value, axis):
    return lax.all_to_all(value, axis, 0, 0, tiled=True)


def swap_cores(value):
    return lax.ppermute(value, "mem", [(j, j ^ 1) for j in range(SLICES)])


def to_other_chip(value, k):
    return lax.ppermute(value, "mem", [(j, (j + 2 * k) % SLICES) for j in range(SLICES)])


def from_other_chips(value):
    return [to_other_chip(value, k) for k in range(1, CHIPS)]


def sum_over_mem(keep, send):
    kept = (keep.astype(F32) + swap_cores(send).astype(F32)).astype(BF16)
    others = from_other_chips(kept)
    total = (kept.astype(F32) + others[1].astype(F32)) + (
        others[0].astype(F32) + others[2].astype(F32)
    )
    total = total.astype(BF16)
    return total, swap_cores(total)


def on_device(members, vertical, jacobian, sketch_bits, test_bits, obs_column, obs_slot):
    slice_id = lax.axis_index("mem").astype(jnp.int32)
    part = slice_id.reshape(1)
    my_tile = lax.axis_index(TILE).astype(jnp.int32)
    local, levels, cells = members.shape
    size = float(OBS * TILES * CHAN)
    scale = 1.0 / ((MEMBERS - 1) * 5.0**STEPS * WALK_SCALE)

    jac = jnp.transpose(jacobian, (2, 1, 0))
    sketch = jnp.swapaxes(sketch_bits, 1, 2)
    test = jnp.swapaxes(test_bits, 1, 2)
    column, slot = obs_column.reshape(1, OBS), obs_slot.reshape(1, OBS)
    first = sign_adjoints(part, sketch, test, column, slot, jac)
    first, members = lax.optimization_barrier((first, members))
    first = exchange(first, TILE)

    padded = jnp.pad(jnp.swapaxes(members, 0, 1), ((0, FULL - levels), (0, 0), (0, 0)))
    padded = padded.reshape(SLICES, SLICE * local, cells)
    padded = jnp.pad(padded, ((0, 0), (0, PIECE - SLICE * local), (0, 0)))
    keep, send = by_parity(part, padded)
    pairs = list(split(part, keep, swap_cores(send)))
    for k in range(1, CHIPS):
        pairs[k] = to_other_chip(pairs[k], k)

    place = jnp.stack([my_tile, slice_id])
    picked = pick(place, first, pairs)
    arrived = exchange(picked.reshape(TILES, CAP, -1), TILE)
    near = near_of(obs_column.reshape(OBS, 1), first, jnp.asarray(walk_table(), BF16))
    vert = jnp.pad(vertical, ((0, FULL - levels), (0, FULL - levels)))
    vert = lax.dynamic_slice_in_dim(vert, slice_id * SLICE, SLICE, axis=1)
    arrived, near, vert = lax.optimization_barrier((arrived, near, vert))
    position = (obs_column // cells * CAP + obs_slot).reshape(1, OBS)
    mine, everyone = own(position, arrived.reshape(TILES * CAP, -1))
    everyone = exchange(everyone, TILE)
    pair = paired(mine, swap_cores(mine))
    mem = gathered(part, [pair] + from_other_chips(pair))

    halves = covariance(2 * K, scale, part, everyone, first, near, mem, vert)
    mine_1, other_1 = sum_over_mem(*halves)
    y, second = images(part, mine_1, other_1, test, jac)
    second = exchange(second, TILE)
    z = test_images(part, mine_1, other_1, jac)
    second, z = lax.optimization_barrier((second, z))
    halves = covariance(K, scale, part, everyone, second, near, mem, vert)
    mine_2, other_2 = sum_over_mem(*halves)
    parts = inner_products(place, (mine_1, other_1), (mine_2, other_2), first, second)
    parts = exchange(parts.reshape(-1, 1, OBS), ("mem", *TILE))
    image_q, image_w, coefs = outputs(size, part, mine_2, other_2, second[:, GRAMS:], z, jac)
    result = traces(size, parts.reshape(-1, OBS), coefs)
    return (jnp.swapaxes(image_q, 1, 2), jnp.swapaxes(image_w, 1, 2), result[0, 0], result[0, 1])


def solution(mesh):
    finer = Mesh(mesh.devices.reshape(mesh.shape["mem"], 4, 4), ("mem", "tile_0", "tile_1"))
    return jax.shard_map(
        on_device,
        mesh=finer,
        in_specs=(
            P("mem", None, TILE),
            P(),
            P(TILE, None, None),
            P(None, TILE, None),
            P(None, TILE, None),
            P(TILE),
            P(TILE),
        ),
        out_specs=(P(None, TILE, None), P(None, TILE, None), P(), P()),
        check_vma=False,
    )
```

```python
import functools

import jax
import jax.numpy as jnp
import numpy as np
from jax import lax
from jax.experimental import pallas as pl
from jax.experimental.pallas import tpu as pltpu
from jax.sharding import Mesh
from jax.sharding import PartitionSpec as P

CB = 32
NX = 256
K = 3
STEPS = 6
TILE = ("tile_0", "tile_1")
TILES = 16
SLICES = 8
LEVELS = 137
SLICE = 18
FULL = SLICES * SLICE
MEMBERS = 16
PIECE = 48
CAP = 32
OBS = 128
CHAN = 231
CPAD = 240
BLOCK = 9
BLOCKS = -(-LEVELS // BLOCK)
REST = LEVELS - (BLOCKS - 1) * BLOCK
CODES = 112
FIRST = 120
GRAMS = 56
SECOND = 64


LIMIT = pltpu.CompilerParams(vmem_limit_bytes=24 * 2**20)
WIDE = pltpu.CompilerParams(vmem_limit_bytes=59000000)
F32 = jnp.float32
BF16 = jnp.bfloat16
VMEM_SPEC = pl.BlockSpec(memory_space=pltpu.VMEM)
SMEM_SPEC = pl.BlockSpec(memory_space=pltpu.SMEM)
NT = (((1,), (1,)), ((), ()))

WALK_SCALE = 1.3338


def walk_table():
    walks = np.zeros((2 * STEPS + 1, 2 * STEPS + 1))
    walks[STEPS, STEPS] = 1
    for _ in range(STEPS):
        grown = walks.copy()
        grown[1:] += walks[:-1]
        grown[:-1] += walks[1:]
        grown[:, 1:] += walks[:, :-1]
        grown[:, :-1] += walks[:, 1:]
        walks = grown

    def count(a, d):
        return walks[STEPS + a, STEPS + d] if d <= STEPS else 0.0

    table = np.zeros((STEPS + 1, CB, CB), np.float32)
    for a in range(STEPS + 1):
        for b in range(CB):
            for c in range(CB):
                table[a, b, c] = (
                    count(a, abs(b - c)) + count(a, b + c + 1) + count(a, 2 * CB - 1 - b - c)
                )
    return table * WALK_SCALE


def dot(a, b, dims=(((1,), (0,)), ((), ()))):
    return lax.dot_general(a, b, dims, preferred_element_type=F32)


def channel_chunks():
    return [(c, min(16, CHAN - c)) for c in range(0, CHAN, 16)]


def jac_rows(jac_ref, level, c, width):
    rows = jac_ref[level, c : c + width, :].astype(F32)
    if width % 8:
        fill = jnp.zeros((8 - width % 8, OBS), F32)
        rows = jnp.concatenate([rows, fill], axis=0)
    return [rows[k : k + 8] for k in range(0, rows.shape[0], 8)]


def back_rows(jac_ref, base, vec_ref, probes, first, put):
    def trio(t, carry):
        levels = [jnp.minimum(first + 3 * t + k, LEVELS - 1) - base for k in range(3)]
        acc = {}
        for c, width in channel_chunks():
            vecs = [
                [vec_ref[p, c + 8 * k : c + 8 * k + 8, :] for k in range(-(-width // 8))]
                for p in range(probes)
            ]
            for n, level in enumerate(levels):
                for k, rows in enumerate(jac_rows(jac_ref, level, c, width)):
                    for p in range(probes):
                        term = rows * vecs[p][k]
                        acc[p, n] = acc[p, n] + term if (p, n) in acc else term
        for n in range(3):
            valid = first + 3 * t + n < LEVELS
            for p in range(probes):
                row = jnp.sum(acc[p, n], axis=0, keepdims=True)
                put(p, 3 * t + n, jnp.where(valid, row, 0.0))
        return carry

    lax.fori_loop(0, SLICE // 3, trio, 0)


def forward_block(jac_ref, prof_ref, img_ref, probes, first, count):
    weights = [
        [
            jnp.broadcast_to(prof_ref[pl.ds(p * FULL + first + level, 1), :], (8, OBS))
            for level in range(count)
        ]
        for p in range(probes)
    ]
    for c, width in channel_chunks():
        parts = -(-width // 8)
        acc = [
            [img_ref[p, c + 8 * k : c + 8 * k + 8, :] for k in range(parts)] for p in range(probes)
        ]
        for level in range(count):
            for k, rows in enumerate(jac_rows(jac_ref, first + level, c, width)):
                for p in range(probes):
                    acc[p][k] = acc[p][k] + rows * weights[p][level]
        for p in range(probes):
            for k in range(parts):
                img_ref[p, c + 8 * k : c + 8 * k + 8, :] = acc[p][k]


def jac_copy(jac_hbm, jac_ref, sems, k, count=BLOCK):
    levels = pl.ds(k * BLOCK, count)
    return pltpu.make_async_copy(jac_hbm.at[levels], jac_ref.at[levels], sems.at[k])


def start_jac(jac_hbm, jac_ref, sems):
    for k in range(BLOCKS):
        jac_copy(jac_hbm, jac_ref, sems, k, BLOCK if k < BLOCKS - 1 else REST).start()


def forward(jac_hbm, jac_ref, sems, prof_ref, img_ref, probes):
    def block(k, carry):
        jac_copy(jac_hbm, jac_ref, sems, k).wait()
        forward_block(jac_ref, prof_ref, img_ref, probes, k * BLOCK, BLOCK)
        return carry

    lax.fori_loop(0, BLOCKS - 1, block, 0)
    jac_copy(jac_hbm, jac_ref, sems, BLOCKS - 1, REST).wait()
    forward_block(jac_ref, prof_ref, img_ref, probes, (BLOCKS - 1) * BLOCK, REST)


JAC_SCRATCH = [pltpu.VMEM((LEVELS, CHAN, OBS), BF16), pltpu.SemaphoreType.DMA((BLOCKS,))]
HBM_SPEC = pl.BlockSpec(memory_space=pl.ANY)
COST = pl.CostEstimate(flops=4 * 10**7, bytes_accessed=10**7, transcendentals=0)


def copies(out_ref, message):
    message = message.astype(BF16)
    for d in range(TILES):
        out_ref[d] = message


def signs_kernel(
    part_ref, sketch_ref, test_ref, column_ref, slot_ref, jac_hbm, out_ref, rows, jac, sem, vec
):
    first = part_ref[0] * SLICE
    base = jnp.minimum(first, LEVELS - SLICE)
    copy = pltpu.make_async_copy(jac_hbm.at[pl.ds(base, SLICE)], jac, sem)
    copy.start()
    rows[...] = jnp.zeros_like(rows)
    for p in range(K):
        vec[p, 0:CHAN, :] = (2 * sketch_ref[p] - 1).astype(F32)
        vec[K + p, 0:CHAN, :] = (2 * test_ref[p] - 1).astype(F32)
        vec[p, CHAN:CPAD, :] = jnp.zeros((CPAD - CHAN, OBS), F32)
        vec[K + p, CHAN:CPAD, :] = jnp.zeros((CPAD - CHAN, OBS), F32)
    column = column_ref[...]
    rows[CODES : CODES + 1, :] = jnp.right_shift(column, 7).astype(F32)
    rows[CODES + 1 : CODES + 2, :] = (column & 127).astype(F32)
    rows[CODES + 2 : CODES + 3, :] = slot_ref[...].astype(F32)

    def put(p, level, row):
        rows[pl.ds(p * SLICE + level, 1), :] = row

    copy.wait()
    back_rows(jac, base, vec, 2 * K, first, put)
    copies(out_ref, rows[...])


def sign_adjoints(part, sketch, test, column, slot, jac):
    return pl.pallas_call(
        signs_kernel,
        compiler_params=WIDE,
        in_specs=[SMEM_SPEC] + [VMEM_SPEC] * 4 + [HBM_SPEC],
        out_specs=[VMEM_SPEC, VMEM_SPEC],
        out_shape=[
            jax.ShapeDtypeStruct((TILES, FIRST, OBS), BF16),
            jax.ShapeDtypeStruct((FIRST, OBS), F32),
        ],
        scratch_shapes=[
            pltpu.VMEM((SLICE, CHAN, OBS), BF16),
            pltpu.SemaphoreType.DMA(()),
            pltpu.VMEM((2 * K, CPAD, OBS), F32),
        ],
        cost_estimate=pl.CostEstimate(flops=10**7, bytes_accessed=2 * 10**6, transcendentals=0),
    )(part, sketch, test, column, slot, jac)


def images_kernel(
    part_ref, mine_ref, other_ref, test_ref, jac_hbm, out_ref, rows, jac, sems, prof, img_ref
):
    start_jac(jac_hbm, jac, sems)
    core = part_ref[0] % 2
    rows[...] = jnp.zeros_like(rows)
    img_ref[...] = jnp.zeros_like(img_ref)
    prof[...] = jnp.where(core == 0, mine_ref[...].astype(F32), other_ref[...].astype(F32))
    forward(jac_hbm, jac, sems, prof, img_ref, K)

    def put(p, level, row):
        rows[pl.ds(p * SLICE + level, 1), :] = row

    back_rows(jac, 0, img_ref, K, part_ref[0] * SLICE, put)
    lanes = lax.broadcasted_iota(jnp.int32, (1, OBS), 1)
    gram = jnp.zeros((1, OBS), F32)
    for i in range(K):
        for j in range(K):
            if j <= i:
                value = jnp.sum(img_ref[i] * img_ref[j])
                gram = jnp.where(lanes == i * K + j, value, gram)
            signs = (2 * test_ref[j] - 1).astype(F32)
            value = jnp.sum(img_ref[i, 0:CHAN, :] * signs)
            gram = jnp.where(lanes == K * K + i * K + j, value, gram)
    high = gram.astype(BF16).astype(F32)
    mid = (gram - high).astype(BF16).astype(F32)
    rows[GRAMS : GRAMS + 1, :] = high
    rows[GRAMS + 1 : GRAMS + 2, :] = mid
    rows[GRAMS + 2 : GRAMS + 3, :] = gram - high - mid
    copies(out_ref, rows[...])


def images(part, mine, other, test, jac):
    return pl.pallas_call(
        images_kernel,
        compiler_params=WIDE,
        in_specs=[SMEM_SPEC, VMEM_SPEC, VMEM_SPEC, VMEM_SPEC, HBM_SPEC],
        out_specs=[VMEM_SPEC] * 2,
        out_shape=[
            jax.ShapeDtypeStruct((TILES, SECOND, OBS), BF16),
            jax.ShapeDtypeStruct((SECOND, OBS), F32),
        ],
        scratch_shapes=JAC_SCRATCH
        + [pltpu.VMEM((K * FULL, OBS), F32), pltpu.VMEM((K, CPAD, OBS), F32)],
        cost_estimate=COST,
    )(part, mine, other, test, jac)


def test_images_kernel(part_ref, mine_ref, other_ref, jac_hbm, img_ref, jac, sems, prof):
    start_jac(jac_hbm, jac, sems)
    core = part_ref[0] % 2
    img_ref[...] = jnp.zeros_like(img_ref)
    prof[...] = jnp.where(core == 0, other_ref[...].astype(F32), mine_ref[...].astype(F32))
    forward(jac_hbm, jac, sems, prof, img_ref, K)


def test_images(part, mine, other, jac):
    return pl.pallas_call(
        test_images_kernel,
        compiler_params=WIDE,
        in_specs=[SMEM_SPEC, VMEM_SPEC, VMEM_SPEC, HBM_SPEC],
        out_specs=VMEM_SPEC,
        out_shape=jax.ShapeDtypeStruct((K, CPAD, OBS), F32),
        scratch_shapes=JAC_SCRATCH + [pltpu.VMEM((K * FULL, OBS), F32)],
        cost_estimate=COST,
    )(part, mine, other, jac)


def coefficients_kernel(size, second_ref, out_ref):
    total = jnp.zeros((1, OBS), F32)
    for d in range(TILES):
        got = second_ref[d, GRAMS : GRAMS + 8, :].astype(F32)
        total = total + jnp.sum(got, axis=0, keepdims=True)
    entry = functools.partial(lane_of, total)
    g = [[entry(i * K + j) for j in range(i + 1)] for i in range(K)]
    c = [[entry(K * K + i * K + j) for j in range(K)] for i in range(K)]
    l00 = jnp.sqrt(g[0][0])
    l10, l20 = g[1][0] / l00, g[2][0] / l00
    l11 = jnp.sqrt(g[1][1] - l10 * l10)
    l21 = (g[2][1] - l20 * l10) / l11
    l22 = jnp.sqrt(g[2][2] - l20 * l20 - l21 * l21)
    i00, i11, i22 = 1.0 / l00, 1.0 / l11, 1.0 / l22
    i10 = -l10 * i00 * i11
    i21 = -l21 * i11 * i22
    i20 = -(l20 * i00 + l21 * i10) * i22
    inv = [[i00], [i10, i11], [i20, i21, i22]]
    root = size**0.5
    lower = [[root * value for value in row] for row in inv]
    share = [
        [sum(inv[i][k] * c[k][j] for k in range(i + 1)) / root for j in range(K)] for i in range(K)
    ]
    out_ref[...] = row_of([v for row in lower for v in row] + [v for row in share for v in row])


def coefficients(size, second):
    return pl.pallas_call(
        functools.partial(coefficients_kernel, size),
        compiler_params=LIMIT,
        in_specs=[VMEM_SPEC],
        out_specs=VMEM_SPEC,
        out_shape=jax.ShapeDtypeStruct((1, OBS), F32),
    )(second)


def coefficients_of(coef_ref):
    coef = functools.partial(lane_of, coef_ref[...])
    lower = [[coef(j * (j + 1) // 2 + i) for i in range(j + 1)] for j in range(K)]
    share = [[coef(2 * K + i * K + j) for j in range(K)] for i in range(K)]
    return lower, share


def lane_of(row, k):
    lanes = lax.broadcasted_iota(jnp.int32, row.shape, 1)
    return jnp.sum(jnp.where(lanes == k, row, 0.0), axis=1, keepdims=True)


def row_of(values):
    lanes = lax.broadcasted_iota(jnp.int32, (1, OBS), 1)
    row = jnp.zeros((1, OBS), F32)
    for k, value in enumerate(values):
        row = jnp.where(lanes == k, value, row)
    return row


def second_profiles(core, mine_ref, other_ref, prof):
    half = K * FULL // 2
    mine, other = mine_ref[...].astype(F32), other_ref[...].astype(F32)
    prof[0:half, :] = jnp.where(core == 0, mine, other)
    prof[half:, :] = jnp.where(core == 0, other, mine)


def inner_kernel(
    part_ref, mine_1_ref, other_1_ref, mine_2_ref, other_2_ref, sign_ref, image_ref, out_ref,
    test_prof, prof,
):
    part = part_ref[0]
    core = part % 2
    second_profiles(core, mine_2_ref, other_2_ref, prof)
    test_prof[...] = jnp.where(
        core == 0, other_1_ref[...].astype(F32), mine_1_ref[...].astype(F32)
    )
    signs = [sign_ref[(K + j) * SLICE : (K + j + 1) * SLICE, :] for j in range(K)]
    images = [image_ref[k * SLICE : (k + 1) * SLICE, :] for k in range(K)]
    tests = [test_prof[pl.ds(j * FULL + part * SLICE, SLICE), :] for j in range(K)]
    profs = [prof[pl.ds(j * FULL + part * SLICE, SLICE), :] for j in range(K)]
    values = [jnp.sum(images[k] * profs[j]) for k in range(K) for j in range(K)]
    values += [jnp.sum(tests[j] * images[k]) for j in range(K) for k in range(K)]
    values += [jnp.sum(signs[j] * tests[j]) for j in range(K)]
    out_ref[...] = jnp.broadcast_to(row_of(values), out_ref.shape)


def inner_products(part, profiles_1, profiles_2, sign, image):
    devices = SLICES * TILES
    return pl.pallas_call(
        inner_kernel,
        compiler_params=LIMIT,
        in_specs=[SMEM_SPEC] + [VMEM_SPEC] * 6,
        out_specs=VMEM_SPEC,
        out_shape=jax.ShapeDtypeStruct((devices, OBS), F32),
        scratch_shapes=[pltpu.VMEM((K * FULL, OBS), F32), pltpu.VMEM((K * FULL, OBS), F32)],
    )(part, *profiles_1, *profiles_2, sign, image)


def outputs_kernel(
    part_ref, mine_ref, other_ref, coef_ref, z_ref, jac_hbm, q_ref, w_ref, jac, sems, prof, x
):
    start_jac(jac_hbm, jac, sems)
    x[...] = jnp.zeros_like(x)
    second_profiles(part_ref[0] % 2, mine_ref, other_ref, prof)
    lower, share = coefficients_of(coef_ref)
    forward(jac_hbm, jac, sems, prof, x, K)
    image_q = []
    for j in range(K):
        q = None
        for i in range(j + 1):
            qx = lower[j][i] * x[i, 0:CHAN, :]
            q = qx if q is None else q + qx
        q_ref[j] = q
        image_q.append(q)
    for j in range(K):
        w = z_ref[j, 0:CHAN, :]
        for i in range(K):
            w = w - share[i][j] * image_q[i]
        w_ref[j] = w


def outputs(part, mine, other, coefs, z, jac):
    return pl.pallas_call(
        outputs_kernel,
        compiler_params=WIDE,
        in_specs=[SMEM_SPEC] + [VMEM_SPEC] * 4 + [HBM_SPEC],
        out_specs=[VMEM_SPEC] * 2,
        out_shape=[jax.ShapeDtypeStruct((K, CHAN, OBS), F32)] * 2,
        scratch_shapes=JAC_SCRATCH
        + [pltpu.VMEM((K * FULL, OBS), F32), pltpu.VMEM((K, CPAD, OBS), F32)],
        cost_estimate=COST,
    )(part, mine, other, coefs, z, jac)


def traces_kernel(size, parts_ref, coef_ref, mean_ref, rayleigh_ref):
    total = functools.partial(lane_of, jnp.sum(parts_ref[...], axis=0, keepdims=True))
    lower, share = coefficients_of(coef_ref)
    yx = [[total(k * K + j) for j in range(K)] for k in range(K)]
    zy = [[total(K * K + j * K + k) for k in range(K)] for j in range(K)]
    tz = [total(2 * K * K + j) for j in range(K)]
    quad = [
        [
            sum(
                lower[i][a] * lower[k][b] * yx[a][b]
                for a in range(i + 1)
                for b in range(k + 1)
            )
            for k in range(K)
        ]
        for i in range(K)
    ]
    cross = [
        [sum(lower[i][b] * zy[j][b] for b in range(i + 1)) for j in range(K)] for i in range(K)
    ]
    trace_q = quad[0][0] + quad[1][1] + quad[2][2]
    trace_w = 0.0
    for j in range(K):
        trace_w = trace_w + tz[j]
        for i in range(K):
            trace_w = trace_w - 2.0 * share[i][j] * cross[i][j]
            for k in range(K):
                trace_w = trace_w + share[i][j] * share[k][j] * quad[i][k]
    mean = trace_q / (size * size) + trace_w / (K * size)
    mean_ref[0] = jnp.sum(mean)
    rayleigh_ref[0] = jnp.sum(trace_q / (K * size))


def traces(size, parts, coefs):
    return pl.pallas_call(
        functools.partial(traces_kernel, size),
        compiler_params=LIMIT,
        in_specs=[VMEM_SPEC, VMEM_SPEC],
        out_specs=[SMEM_SPEC, SMEM_SPEC],
        out_shape=[jax.ShapeDtypeStruct((1,), F32)] * 2,
    )(parts, coefs)


CHIPS = SLICES // 2


def parity_kernel(part_ref, members_ref, keep_ref, send_ref):
    core = part_ref[0] % 2
    for chip in range(CHIPS):
        keep_ref[chip] = members_ref[2 * chip + core]
        send_ref[chip] = members_ref[2 * chip + 1 - core]


def by_parity(part, members):
    half = jax.ShapeDtypeStruct((CHIPS, *members.shape[1:]), BF16)
    return pl.pallas_call(
        parity_kernel,
        compiler_params=LIMIT,
        in_specs=[SMEM_SPEC, VMEM_SPEC],
        out_specs=[VMEM_SPEC, VMEM_SPEC],
        out_shape=[half, half],
    )(part, members)


def split_kernel(part_ref, keep_ref, got_ref, *out_refs):
    for k in range(CHIPS):
        chip = lax.rem(part_ref[0] // 2 + k, CHIPS)
        out_refs[k][0:PIECE, :] = keep_ref[chip]
        out_refs[k][PIECE:, :] = got_ref[chip]


def split(part, keep, got):
    pair = jax.ShapeDtypeStruct((2 * PIECE, keep.shape[2]), BF16)
    return pl.pallas_call(
        split_kernel,
        compiler_params=LIMIT,
        in_specs=[SMEM_SPEC, VMEM_SPEC, VMEM_SPEC],
        out_specs=[VMEM_SPEC] * CHIPS,
        out_shape=[pair] * CHIPS,
    )(part, keep, got)


def pick_kernel(place_ref, first_ref, *refs):
    pairs = refs[:CHIPS]
    out_ref, members, chosen = refs[CHIPS:]
    cells = members.shape[1]
    core = place_ref[1] % 2
    for k in range(CHIPS):
        source = lax.rem(place_ref[1] // 2 + CHIPS - k, CHIPS) * 2
        for n, owner in enumerate((core, 1 - core)):
            at = pl.multiple_of((source + owner) * PIECE, PIECE)
            members[pl.ds(at, PIECE), :] = pairs[k][n * PIECE : (n + 1) * PIECE, :]
    tile = place_ref[0].astype(F32)
    slots = lax.broadcasted_iota(jnp.int32, (CAP, OBS), 0).astype(F32)
    lanes = lax.broadcasted_iota(jnp.int32, (CAP, cells), 1).astype(F32)
    for d in range(TILES):
        codes = first_ref[d, CODES:FIRST, :].astype(F32)
        cell = codes[0:1] * 128.0 + codes[1:2] - tile * float(cells)
        inside = (cell >= 0.0) & (cell < float(cells))
        here = jnp.where((slots == codes[2:3]) & inside, cell + 1.0, 0.0)
        at = jnp.sum(here, axis=1, keepdims=True) - 1.0
        chosen[d * CAP : (d + 1) * CAP, :] = jnp.where(lanes == at, 1.0, 0.0).astype(BF16)
    out_ref[...] = dot(chosen[...], members[...], NT).astype(BF16)


def pick(place, first, pieces):
    cells = pieces[0].shape[1]
    return pl.pallas_call(
        pick_kernel,
        compiler_params=LIMIT,
        in_specs=[SMEM_SPEC] + [VMEM_SPEC] * (1 + CHIPS),
        out_specs=VMEM_SPEC,
        out_shape=jax.ShapeDtypeStruct((TILES * CAP, SLICES * PIECE), BF16),
        scratch_shapes=[
            pltpu.VMEM((SLICES * PIECE, cells), BF16),
            pltpu.VMEM((TILES * CAP, cells), BF16),
        ],
    )(place, first, *pieces)


def own_kernel(pos_ref, recv_ref, out_ref, all_ref):
    rows = lax.broadcasted_iota(jnp.int32, (TILES * CAP, OBS), 0)
    chosen = jnp.where(rows == pos_ref[...], 1.0, 0.0).astype(BF16)
    mine = dot(recv_ref[...].T, chosen).astype(BF16)
    shape = (SLICE * MEMBERS, SLICES * PIECE)
    row = lax.broadcasted_iota(jnp.int32, shape, 0)
    lane = lax.broadcasted_iota(jnp.int32, shape, 1)
    level, member = jnp.right_shift(row, 4), row & 15
    source = jnp.right_shift(member, 1) * PIECE + 2 * level + (member & 1)
    turn = jnp.where(lane == source, 1.0, 0.0).astype(BF16)
    mine = dot(turn, mine)
    out_ref[...] = mine.astype(BF16)
    copies(all_ref, mine)


def own(position, recv):
    rows = SLICE * MEMBERS
    return pl.pallas_call(
        own_kernel,
        compiler_params=LIMIT,
        in_specs=[VMEM_SPEC, VMEM_SPEC],
        out_specs=[VMEM_SPEC, VMEM_SPEC],
        out_shape=[
            jax.ShapeDtypeStruct((rows, OBS), BF16),
            jax.ShapeDtypeStruct((TILES, rows, OBS), BF16),
        ],
    )(position, recv)


def pair_kernel(mine_ref, got_ref, out_ref):
    rows = mine_ref.shape[0]
    out_ref[0:rows, :] = mine_ref[...]
    out_ref[rows:, :] = got_ref[...]


def paired(mine, got):
    return pl.pallas_call(
        pair_kernel,
        compiler_params=LIMIT,
        in_specs=[VMEM_SPEC, VMEM_SPEC],
        out_specs=VMEM_SPEC,
        out_shape=jax.ShapeDtypeStruct((2 * mine.shape[0], OBS), BF16),
    )(mine, got)


def gathered_kernel(part_ref, *refs):
    rows = SLICE * MEMBERS
    pairs = refs[:CHIPS]
    out_ref, mem = refs[CHIPS:]
    chip, core = part_ref[0] // 2, part_ref[0] % 2
    for k in range(CHIPS):
        source = lax.rem(chip + CHIPS - k, CHIPS) * 2
        for n, owner in enumerate((core, 1 - core)):
            at = pl.multiple_of((source + owner) * rows, rows)
            mem[pl.ds(at, rows), :] = pairs[k][n * rows : (n + 1) * rows, :].astype(F32)
    for m in range(MEMBERS):
        out_ref[m * FULL : (m + 1) * FULL, :] = mem[pl.ds(m, FULL, stride=MEMBERS), :]


def gathered(part, pairs):
    return pl.pallas_call(
        gathered_kernel,
        compiler_params=LIMIT,
        in_specs=[SMEM_SPEC] + [VMEM_SPEC] * CHIPS,
        out_specs=VMEM_SPEC,
        out_shape=jax.ShapeDtypeStruct((MEMBERS * FULL, OBS), F32),
        scratch_shapes=[pltpu.VMEM((MEMBERS * FULL, OBS), F32)],
        cost_estimate=pl.CostEstimate(flops=10**6, bytes_accessed=2 * 10**6, transcendentals=0),
    )(part, *pairs)


def near_kernel(col_ref, first_ref, table_ref, out_ref):
    mine = col_ref[...]
    my_x = (mine // CB).astype(F32)
    my_b = mine % CB
    hot = jnp.where(lax.broadcasted_iota(jnp.int32, (OBS, CB), 1) == my_b, 1.0, 0.0).astype(BF16)
    reach = [dot(hot, table_ref[a]).astype(BF16) for a in range(STEPS + 1)]
    rows = lax.broadcasted_iota(jnp.int32, (CB, OBS), 0)
    for d in range(TILES):
        codes = first_ref[d, CODES:FIRST, :].astype(F32).astype(jnp.int32)
        hi, lo = codes[0:1], codes[1:2]
        x = (hi * 4 + lo // CB).astype(F32)
        there = jnp.where(rows == lo % CB, 1.0, 0.0).astype(BF16)
        gap = jnp.abs(my_x - x)
        gap = jnp.minimum(gap, float(NX) - gap)
        total = jnp.zeros((OBS, OBS), F32)
        for a in range(STEPS + 1):
            total = jnp.where(gap == float(a), dot(reach[a], there), total)
        out_ref[:, d * OBS : (d + 1) * OBS] = total.astype(BF16)


def near_of(column, first, table):
    return pl.pallas_call(
        near_kernel,
        compiler_params=LIMIT,
        in_specs=[VMEM_SPEC, VMEM_SPEC, VMEM_SPEC],
        out_specs=VMEM_SPEC,
        out_shape=jax.ShapeDtypeStruct((OBS, TILES * OBS), BF16),
        cost_estimate=pl.CostEstimate(flops=2 * 10**7, bytes_accessed=4 * 10**6, transcendentals=0),
    )(column, first, table)


def covariance_kernel(
    probes, scale, part_ref, all_ref, adj_ref, near_ref, mem_ref, vert_ref, keep_ref, send_ref,
    prod, acc, adj, out,
):
    rows = SLICE * MEMBERS
    adj[...] = adj_ref[...].astype(F32)

    def probe(p, carry):
        for d in range(TILES):
            for level in range(SLICE):
                row = adj[d, pl.ds(p * SLICE + level, 1), :]
                row = jnp.broadcast_to(row, (MEMBERS, OBS)).astype(BF16)
                at = slice(level * MEMBERS, (level + 1) * MEMBERS)
                prod[at, d * OBS : (d + 1) * OBS] = all_ref[d, at, :] * row
        acc[pl.ds(pl.multiple_of(p * rows, rows), rows), :] = dot(prod[...], near_ref[...], NT)
        return carry

    lax.fori_loop(0, probes, probe, 0)
    vert = vert_ref[...]
    for p in range(probes):
        total = None
        for m in range(MEMBERS):
            smooth = acc[pl.ds(p * rows + m, SLICE, stride=MEMBERS), :].astype(BF16)
            term = mem_ref[m * FULL : (m + 1) * FULL, :] * dot(vert, smooth)
            total = term if total is None else total + term
        out[p * FULL : (p + 1) * FULL, :] = total * scale
    half = probes * FULL // 2
    core = part_ref[0] % 2
    low, high = out[0:half, :], out[half:, :]
    keep_ref[...] = jnp.where(core == 0, low, high).astype(BF16)
    send_ref[...] = jnp.where(core == 0, high, low).astype(BF16)


def covariance(probes, scale, part, everyone, adjoints, near, mem, vert):
    rows = SLICE * MEMBERS
    half = jax.ShapeDtypeStruct((probes * FULL // 2, OBS), BF16)
    return pl.pallas_call(
        functools.partial(covariance_kernel, probes, scale),
        compiler_params=LIMIT,
        in_specs=[SMEM_SPEC] + [VMEM_SPEC] * 5,
        out_specs=[VMEM_SPEC, VMEM_SPEC],
        out_shape=[half, half],
        scratch_shapes=[
            pltpu.VMEM((rows, TILES * OBS), BF16),
            pltpu.VMEM((probes * rows, OBS), F32),
            pltpu.VMEM(adjoints.shape, F32),
            pltpu.VMEM((probes * FULL, OBS), F32),
        ],
    )(part, everyone, adjoints, near, mem, vert)


def exchange(value, axis):
    return lax.all_to_all(value, axis, 0, 0, tiled=True)


def swap_cores(value):
    return lax.ppermute(value, "mem", [(j, j ^ 1) for j in range(SLICES)])


def to_other_chip(value, k):
    return lax.ppermute(value, "mem", [(j, (j + 2 * k) % SLICES) for j in range(SLICES)])


def from_other_chips(value):
    return [to_other_chip(value, k) for k in range(1, CHIPS)]


def sum_over_mem(keep, send):
    kept = (keep.astype(F32) + swap_cores(send).astype(F32)).astype(BF16)
    others = from_other_chips(kept)
    total = (kept.astype(F32) + others[1].astype(F32)) + (
        others[0].astype(F32) + others[2].astype(F32)
    )
    total = total.astype(BF16)
    return total, swap_cores(total)


def on_device(members, vertical, jacobian, sketch_bits, test_bits, obs_column, obs_slot):
    slice_id = lax.axis_index("mem").astype(jnp.int32)
    part = slice_id.reshape(1)
    my_tile = lax.axis_index(TILE).astype(jnp.int32)
    local, levels, cells = members.shape
    size = float(OBS * TILES * CHAN)
    scale = 1.0 / ((MEMBERS - 1) * 5.0**STEPS * WALK_SCALE)

    jac = jnp.transpose(jacobian, (2, 1, 0))
    sketch = jnp.swapaxes(sketch_bits, 1, 2)
    test = jnp.swapaxes(test_bits, 1, 2)
    column, slot = obs_column.reshape(1, OBS), obs_slot.reshape(1, OBS)
    first, sign = sign_adjoints(part, sketch, test, column, slot, jac)
    first, members = lax.optimization_barrier((first, members))
    first = exchange(first, TILE)

    padded = jnp.pad(jnp.swapaxes(members, 0, 1), ((0, FULL - levels), (0, 0), (0, 0)))
    padded = padded.reshape(SLICES, SLICE * local, cells)
    padded = jnp.pad(padded, ((0, 0), (0, PIECE - SLICE * local), (0, 0)))
    keep, send = by_parity(part, padded)
    pairs = list(split(part, keep, swap_cores(send)))
    for k in range(1, CHIPS):
        pairs[k] = to_other_chip(pairs[k], k)

    place = jnp.stack([my_tile, slice_id])
    picked = pick(place, first, pairs)
    arrived = exchange(picked.reshape(TILES, CAP, -1), TILE)
    near = near_of(obs_column.reshape(OBS, 1), first, jnp.asarray(walk_table(), BF16))
    vert = jnp.pad(vertical, ((0, FULL - levels), (0, FULL - levels)))
    vert = lax.dynamic_slice_in_dim(vert, slice_id * SLICE, SLICE, axis=1)
    arrived, near, vert = lax.optimization_barrier((arrived, near, vert))
    position = (obs_column // cells * CAP + obs_slot).reshape(1, OBS)
    mine, everyone = own(position, arrived.reshape(TILES * CAP, -1))
    everyone = exchange(everyone, TILE)
    pair = paired(mine, swap_cores(mine))
    mem = gathered(part, [pair] + from_other_chips(pair))

    halves = covariance(2 * K, scale, part, everyone, first, near, mem, vert)
    mine_1, other_1 = sum_over_mem(*halves)
    second, image = images(part, mine_1, other_1, test, jac)
    second = exchange(second, TILE)
    z = test_images(part, mine_1, other_1, jac)
    second, z = lax.optimization_barrier((second, z))
    halves = covariance(K, scale, part, everyone, second, near, mem, vert)
    coefs = coefficients(size, second)
    mine_2, other_2 = sum_over_mem(*halves)
    mine_2, coefs = lax.optimization_barrier((mine_2, coefs))
    parts = inner_products(part, (mine_1, other_1), (mine_2, other_2), sign, image)
    parts = exchange(parts.reshape(-1, 1, OBS), ("mem", *TILE))
    image_q, image_w = outputs(part, mine_2, other_2, coefs, z, jac)
    mean, rayleigh = traces(size, parts.reshape(-1, OBS), coefs)
    return (
        jnp.swapaxes(image_q, 1, 2),
        jnp.swapaxes(image_w, 1, 2),
        mean.reshape(()),
        rayleigh.reshape(()),
    )


def solution(mesh):
    finer = Mesh(mesh.devices.reshape(mesh.shape["mem"], 4, 4), ("mem", "tile_0", "tile_1"))
    return jax.shard_map(
        on_device,
        mesh=finer,
        in_specs=(
            P("mem", None, TILE),
            P(),
            P(TILE, None, None),
            P(None, TILE, None),
            P(None, TILE, None),
            P(TILE),
            P(TILE),
        ),
        out_specs=(P(None, TILE, None), P(None, TILE, None), P(), P()),
        check_vma=False,
    )
```

```python
import functools

import jax
import jax.numpy as jnp
import numpy as np
from jax import lax
from jax.experimental import pallas as pl
from jax.experimental.pallas import tpu as pltpu
from jax.sharding import Mesh
from jax.sharding import PartitionSpec as P

CB = 32
NX = 256
K = 3
STEPS = 6
TILE = ("tile_0", "tile_1")
TILES = 16
SLICES = 8
LEVELS = 137
SLICE = 18
FULL = SLICES * SLICE
MEMBERS = 16
PIECE = 48
CAP = 32
OBS = 128
CHAN = 231
CPAD = 240
BLOCK = 9
BLOCKS = -(-LEVELS // BLOCK)
REST = LEVELS - (BLOCKS - 1) * BLOCK
CODES = 112
FIRST = 120
GRAMS = 56
SECOND = 64


LIMIT = pltpu.CompilerParams(vmem_limit_bytes=24 * 2**20)
WIDE = pltpu.CompilerParams(vmem_limit_bytes=59000000)
F32 = jnp.float32
BF16 = jnp.bfloat16
VMEM_SPEC = pl.BlockSpec(memory_space=pltpu.VMEM)
SMEM_SPEC = pl.BlockSpec(memory_space=pltpu.SMEM)
NT = (((1,), (1,)), ((), ()))

WALK_SCALE = 1.3338


def walk_table():
    walks = np.zeros((2 * STEPS + 1, 2 * STEPS + 1))
    walks[STEPS, STEPS] = 1
    for _ in range(STEPS):
        grown = walks.copy()
        grown[1:] += walks[:-1]
        grown[:-1] += walks[1:]
        grown[:, 1:] += walks[:, :-1]
        grown[:, :-1] += walks[:, 1:]
        walks = grown

    def count(a, d):
        return walks[STEPS + a, STEPS + d] if d <= STEPS else 0.0

    table = np.zeros((STEPS + 1, CB, CB), np.float32)
    for a in range(STEPS + 1):
        for b in range(CB):
            for c in range(CB):
                table[a, b, c] = (
                    count(a, abs(b - c)) + count(a, b + c + 1) + count(a, 2 * CB - 1 - b - c)
                )
    return table * WALK_SCALE


def dot(a, b, dims=(((1,), (0,)), ((), ()))):
    return lax.dot_general(a, b, dims, preferred_element_type=F32)


def channel_chunks():
    return [(c, min(16, CHAN - c)) for c in range(0, CHAN, 16)]


def jac_rows(jac_ref, level, c, width):
    rows = jac_ref[level, c : c + width, :].astype(F32)
    if width % 8:
        fill = jnp.zeros((8 - width % 8, OBS), F32)
        rows = jnp.concatenate([rows, fill], axis=0)
    return [rows[k : k + 8] for k in range(0, rows.shape[0], 8)]


def back_rows(jac_ref, base, vec_ref, probes, first, put):
    def trio(t, carry):
        levels = [jnp.minimum(first + 3 * t + k, LEVELS - 1) - base for k in range(3)]
        acc = {}
        for c, width in channel_chunks():
            vecs = [
                [vec_ref[p, c + 8 * k : c + 8 * k + 8, :] for k in range(-(-width // 8))]
                for p in range(probes)
            ]
            for n, level in enumerate(levels):
                for k, rows in enumerate(jac_rows(jac_ref, level, c, width)):
                    for p in range(probes):
                        term = rows * vecs[p][k]
                        acc[p, n] = acc[p, n] + term if (p, n) in acc else term
        for n in range(3):
            valid = first + 3 * t + n < LEVELS
            for p in range(probes):
                row = jnp.sum(acc[p, n], axis=0, keepdims=True)
                put(p, 3 * t + n, jnp.where(valid, row, 0.0))
        return carry

    lax.fori_loop(0, SLICE // 3, trio, 0)


def forward_block(jac_ref, prof_ref, img_ref, probes, first, count):
    weights = [
        [
            jnp.broadcast_to(prof_ref[pl.ds(p * FULL + first + level, 1), :], (8, OBS))
            for level in range(count)
        ]
        for p in range(probes)
    ]
    for c, width in channel_chunks():
        parts = -(-width // 8)
        acc = [
            [img_ref[p, c + 8 * k : c + 8 * k + 8, :] for k in range(parts)] for p in range(probes)
        ]
        for level in range(count):
            for k, rows in enumerate(jac_rows(jac_ref, first + level, c, width)):
                for p in range(probes):
                    acc[p][k] = acc[p][k] + rows * weights[p][level]
        for p in range(probes):
            for k in range(parts):
                img_ref[p, c + 8 * k : c + 8 * k + 8, :] = acc[p][k]


def jac_copy(jac_hbm, jac_ref, sems, k, count=BLOCK):
    levels = pl.ds(k * BLOCK, count)
    return pltpu.make_async_copy(jac_hbm.at[levels], jac_ref.at[levels], sems.at[k])


def start_jac(jac_hbm, jac_ref, sems):
    for k in range(BLOCKS):
        jac_copy(jac_hbm, jac_ref, sems, k, BLOCK if k < BLOCKS - 1 else REST).start()


def forward(jac_hbm, jac_ref, sems, prof_ref, img_ref, probes):
    def block(k, carry):
        jac_copy(jac_hbm, jac_ref, sems, k).wait()
        forward_block(jac_ref, prof_ref, img_ref, probes, k * BLOCK, BLOCK)
        return carry

    lax.fori_loop(0, BLOCKS - 1, block, 0)
    jac_copy(jac_hbm, jac_ref, sems, BLOCKS - 1, REST).wait()
    forward_block(jac_ref, prof_ref, img_ref, probes, (BLOCKS - 1) * BLOCK, REST)


JAC_SCRATCH = [pltpu.VMEM((LEVELS, CHAN, OBS), BF16), pltpu.SemaphoreType.DMA((BLOCKS,))]
HBM_SPEC = pl.BlockSpec(memory_space=pl.ANY)
COST = pl.CostEstimate(flops=4 * 10**7, bytes_accessed=10**7, transcendentals=0)


def copies(out_ref, message):
    message = message.astype(BF16)
    for d in range(TILES):
        out_ref[d] = message


def signs_kernel(
    part_ref, sketch_ref, test_ref, column_ref, slot_ref, jac_hbm, out_ref, rows, jac, sem, vec
):
    first = part_ref[0] * SLICE
    base = jnp.minimum(first, LEVELS - SLICE)
    copy = pltpu.make_async_copy(jac_hbm.at[pl.ds(base, SLICE)], jac, sem)
    copy.start()
    rows[...] = jnp.zeros_like(rows)
    for p in range(K):
        vec[p, 0:CHAN, :] = (2 * sketch_ref[p] - 1).astype(F32)
        vec[K + p, 0:CHAN, :] = (2 * test_ref[p] - 1).astype(F32)
        vec[p, CHAN:CPAD, :] = jnp.zeros((CPAD - CHAN, OBS), F32)
        vec[K + p, CHAN:CPAD, :] = jnp.zeros((CPAD - CHAN, OBS), F32)
    column = column_ref[...]
    rows[CODES : CODES + 1, :] = jnp.right_shift(column, 7).astype(F32)
    rows[CODES + 1 : CODES + 2, :] = (column & 127).astype(F32)
    rows[CODES + 2 : CODES + 3, :] = slot_ref[...].astype(F32)

    def put(p, level, row):
        rows[pl.ds(p * SLICE + level, 1), :] = row

    copy.wait()
    back_rows(jac, base, vec, 2 * K, first, put)
    copies(out_ref, rows[...])


def sign_adjoints(part, sketch, test, column, slot, jac):
    return pl.pallas_call(
        signs_kernel,
        compiler_params=WIDE,
        in_specs=[SMEM_SPEC] + [VMEM_SPEC] * 4 + [HBM_SPEC],
        out_specs=[VMEM_SPEC, VMEM_SPEC],
        out_shape=[
            jax.ShapeDtypeStruct((TILES, FIRST, OBS), BF16),
            jax.ShapeDtypeStruct((FIRST, OBS), F32),
        ],
        scratch_shapes=[
            pltpu.VMEM((SLICE, CHAN, OBS), BF16),
            pltpu.SemaphoreType.DMA(()),
            pltpu.VMEM((2 * K, CPAD, OBS), F32),
        ],
        cost_estimate=pl.CostEstimate(flops=10**7, bytes_accessed=2 * 10**6, transcendentals=0),
    )(part, sketch, test, column, slot, jac)


def images_kernel(
    part_ref, mine_ref, other_ref, test_ref, jac_hbm, out_ref, rows, jac, sems, prof, img_ref
):
    start_jac(jac_hbm, jac, sems)
    rows[...] = jnp.zeros_like(rows)
    img_ref[...] = jnp.zeros_like(img_ref)
    unfold(part_ref[0] % 2, mine_ref, other_ref, prof)
    forward(jac_hbm, jac, sems, prof, img_ref, K)

    def put(p, level, row):
        rows[pl.ds(p * SLICE + level, 1), :] = row

    back_rows(jac, 0, img_ref, K, part_ref[0] * SLICE, put)
    lanes = lax.broadcasted_iota(jnp.int32, (1, OBS), 1)
    gram = jnp.zeros((1, OBS), F32)
    for i in range(K):
        for j in range(K):
            if j <= i:
                value = jnp.sum(img_ref[i] * img_ref[j])
                gram = jnp.where(lanes == i * K + j, value, gram)
            signs = (2 * test_ref[j] - 1).astype(F32)
            value = jnp.sum(img_ref[i, 0:CHAN, :] * signs)
            gram = jnp.where(lanes == K * K + i * K + j, value, gram)
    high = gram.astype(BF16).astype(F32)
    mid = (gram - high).astype(BF16).astype(F32)
    rows[GRAMS : GRAMS + 1, :] = high
    rows[GRAMS + 1 : GRAMS + 2, :] = mid
    rows[GRAMS + 2 : GRAMS + 3, :] = gram - high - mid
    copies(out_ref, rows[...])


def images(part, mine, other, test, jac):
    return pl.pallas_call(
        images_kernel,
        compiler_params=WIDE,
        in_specs=[SMEM_SPEC, VMEM_SPEC, VMEM_SPEC, VMEM_SPEC, HBM_SPEC],
        out_specs=[VMEM_SPEC] * 2,
        out_shape=[
            jax.ShapeDtypeStruct((TILES, SECOND, OBS), BF16),
            jax.ShapeDtypeStruct((SECOND, OBS), F32),
        ],
        scratch_shapes=JAC_SCRATCH
        + [pltpu.VMEM((K * FULL, OBS), F32), pltpu.VMEM((K, CPAD, OBS), F32)],
        cost_estimate=COST,
    )(part, mine, other, test, jac)


def test_images_kernel(part_ref, mine_ref, other_ref, jac_hbm, img_ref, jac, sems, prof):
    start_jac(jac_hbm, jac, sems)
    img_ref[...] = jnp.zeros_like(img_ref)
    unfold(part_ref[0] % 2, mine_ref, other_ref, prof)
    forward(jac_hbm, jac, sems, prof, img_ref, K)


def test_images(part, mine, other, jac):
    return pl.pallas_call(
        test_images_kernel,
        compiler_params=WIDE,
        in_specs=[SMEM_SPEC, VMEM_SPEC, VMEM_SPEC, HBM_SPEC],
        out_specs=VMEM_SPEC,
        out_shape=jax.ShapeDtypeStruct((K, CPAD, OBS), F32),
        scratch_shapes=JAC_SCRATCH + [pltpu.VMEM((K * FULL, OBS), F32)],
        cost_estimate=COST,
    )(part, mine, other, jac)


def coefficients_kernel(size, second_ref, out_ref):
    total = jnp.zeros((1, OBS), F32)
    for d in range(TILES):
        got = second_ref[d, GRAMS : GRAMS + 8, :].astype(F32)
        total = total + jnp.sum(got, axis=0, keepdims=True)
    entry = functools.partial(lane_of, total)
    g = [[entry(i * K + j) for j in range(i + 1)] for i in range(K)]
    c = [[entry(K * K + i * K + j) for j in range(K)] for i in range(K)]
    l00 = jnp.sqrt(g[0][0])
    l10, l20 = g[1][0] / l00, g[2][0] / l00
    l11 = jnp.sqrt(g[1][1] - l10 * l10)
    l21 = (g[2][1] - l20 * l10) / l11
    l22 = jnp.sqrt(g[2][2] - l20 * l20 - l21 * l21)
    i00, i11, i22 = 1.0 / l00, 1.0 / l11, 1.0 / l22
    i10 = -l10 * i00 * i11
    i21 = -l21 * i11 * i22
    i20 = -(l20 * i00 + l21 * i10) * i22
    inv = [[i00], [i10, i11], [i20, i21, i22]]
    root = size**0.5
    lower = [[root * value for value in row] for row in inv]
    share = [
        [sum(inv[i][k] * c[k][j] for k in range(i + 1)) / root for j in range(K)] for i in range(K)
    ]
    out_ref[...] = row_of([v for row in lower for v in row] + [v for row in share for v in row])


def coefficients(size, second):
    return pl.pallas_call(
        functools.partial(coefficients_kernel, size),
        compiler_params=LIMIT,
        in_specs=[VMEM_SPEC],
        out_specs=VMEM_SPEC,
        out_shape=jax.ShapeDtypeStruct((1, OBS), F32),
    )(second)


def coefficients_of(coef_ref):
    coef = functools.partial(lane_of, coef_ref[...])
    lower = [[coef(j * (j + 1) // 2 + i) for i in range(j + 1)] for j in range(K)]
    share = [[coef(2 * K + i * K + j) for j in range(K)] for i in range(K)]
    return lower, share


def lane_of(row, k):
    lanes = lax.broadcasted_iota(jnp.int32, row.shape, 1)
    return jnp.sum(jnp.where(lanes == k, row, 0.0), axis=1, keepdims=True)


def row_of(values):
    lanes = lax.broadcasted_iota(jnp.int32, (1, OBS), 1)
    row = jnp.zeros((1, OBS), F32)
    for k, value in enumerate(values):
        row = jnp.where(lanes == k, value, row)
    return row


def unfold(core, mine_ref, other_ref, prof):
    half = K * FULL // 2
    mine, other = mine_ref[...].astype(F32), other_ref[...].astype(F32)
    prof[0:half, :] = jnp.where(core == 0, mine, other)
    prof[half:, :] = jnp.where(core == 0, other, mine)


def inner_kernel(
    part_ref, mine_1_ref, other_1_ref, mine_2_ref, other_2_ref, sign_ref, image_ref, out_ref,
    test_prof, prof,
):
    part = part_ref[0]
    core = part % 2
    unfold(core, mine_2_ref, other_2_ref, prof)
    unfold(core, mine_1_ref, other_1_ref, test_prof)
    signs = [sign_ref[(K + j) * SLICE : (K + j + 1) * SLICE, :] for j in range(K)]
    images = [image_ref[k * SLICE : (k + 1) * SLICE, :] for k in range(K)]
    tests = [test_prof[pl.ds(j * FULL + part * SLICE, SLICE), :] for j in range(K)]
    profs = [prof[pl.ds(j * FULL + part * SLICE, SLICE), :] for j in range(K)]
    values = [jnp.sum(images[k] * profs[j]) for k in range(K) for j in range(K)]
    values += [jnp.sum(tests[j] * images[k]) for j in range(K) for k in range(K)]
    values += [jnp.sum(signs[j] * tests[j]) for j in range(K)]
    out_ref[...] = jnp.broadcast_to(row_of(values), out_ref.shape)


def inner_products(part, profiles_1, profiles_2, sign, image):
    devices = SLICES * TILES
    return pl.pallas_call(
        inner_kernel,
        compiler_params=LIMIT,
        in_specs=[SMEM_SPEC] + [VMEM_SPEC] * 6,
        out_specs=VMEM_SPEC,
        out_shape=jax.ShapeDtypeStruct((devices, OBS), F32),
        scratch_shapes=[pltpu.VMEM((K * FULL, OBS), F32), pltpu.VMEM((K * FULL, OBS), F32)],
    )(part, *profiles_1, *profiles_2, sign, image)


def outputs_kernel(
    part_ref, mine_ref, other_ref, coef_ref, z_ref, jac_hbm, q_ref, w_ref, jac, sems, prof, x
):
    start_jac(jac_hbm, jac, sems)
    x[...] = jnp.zeros_like(x)
    unfold(part_ref[0] % 2, mine_ref, other_ref, prof)
    lower, share = coefficients_of(coef_ref)
    forward(jac_hbm, jac, sems, prof, x, K)
    image_q = []
    for j in range(K):
        q = None
        for i in range(j + 1):
            qx = lower[j][i] * x[i, 0:CHAN, :]
            q = qx if q is None else q + qx
        q_ref[j] = q
        image_q.append(q)
    for j in range(K):
        w = z_ref[j, 0:CHAN, :]
        for i in range(K):
            w = w - share[i][j] * image_q[i]
        w_ref[j] = w


def outputs(part, mine, other, coefs, z, jac):
    return pl.pallas_call(
        outputs_kernel,
        compiler_params=WIDE,
        in_specs=[SMEM_SPEC] + [VMEM_SPEC] * 4 + [HBM_SPEC],
        out_specs=[VMEM_SPEC] * 2,
        out_shape=[jax.ShapeDtypeStruct((K, CHAN, OBS), F32)] * 2,
        scratch_shapes=JAC_SCRATCH
        + [pltpu.VMEM((K * FULL, OBS), F32), pltpu.VMEM((K, CPAD, OBS), F32)],
        cost_estimate=COST,
    )(part, mine, other, coefs, z, jac)


def traces_kernel(size, parts_ref, coef_ref, mean_ref, rayleigh_ref):
    total = functools.partial(lane_of, jnp.sum(parts_ref[...], axis=0, keepdims=True))
    lower, share = coefficients_of(coef_ref)
    yx = [[total(k * K + j) for j in range(K)] for k in range(K)]
    zy = [[total(K * K + j * K + k) for k in range(K)] for j in range(K)]
    tz = [total(2 * K * K + j) for j in range(K)]
    quad = [
        [
            sum(
                lower[i][a] * lower[k][b] * yx[a][b]
                for a in range(i + 1)
                for b in range(k + 1)
            )
            for k in range(K)
        ]
        for i in range(K)
    ]
    cross = [
        [sum(lower[i][b] * zy[j][b] for b in range(i + 1)) for j in range(K)] for i in range(K)
    ]
    trace_q = quad[0][0] + quad[1][1] + quad[2][2]
    trace_w = 0.0
    for j in range(K):
        trace_w = trace_w + tz[j]
        for i in range(K):
            trace_w = trace_w - 2.0 * share[i][j] * cross[i][j]
            for k in range(K):
                trace_w = trace_w + share[i][j] * share[k][j] * quad[i][k]
    mean = trace_q / (size * size) + trace_w / (K * size)
    mean_ref[0] = jnp.sum(mean)
    rayleigh_ref[0] = jnp.sum(trace_q / (K * size))


def traces(size, parts, coefs):
    return pl.pallas_call(
        functools.partial(traces_kernel, size),
        compiler_params=LIMIT,
        in_specs=[VMEM_SPEC, VMEM_SPEC],
        out_specs=[SMEM_SPEC, SMEM_SPEC],
        out_shape=[jax.ShapeDtypeStruct((1,), F32)] * 2,
    )(parts, coefs)


CHIPS = SLICES // 2


def parity_kernel(part_ref, members_ref, keep_ref, send_ref):
    core = part_ref[0] % 2
    for chip in range(CHIPS):
        keep_ref[chip] = members_ref[2 * chip + core]
        send_ref[chip] = members_ref[2 * chip + 1 - core]


def by_parity(part, members):
    half = jax.ShapeDtypeStruct((CHIPS, *members.shape[1:]), BF16)
    return pl.pallas_call(
        parity_kernel,
        compiler_params=LIMIT,
        in_specs=[SMEM_SPEC, VMEM_SPEC],
        out_specs=[VMEM_SPEC, VMEM_SPEC],
        out_shape=[half, half],
    )(part, members)


def split_kernel(part_ref, keep_ref, got_ref, *out_refs):
    for k in range(CHIPS):
        chip = lax.rem(part_ref[0] // 2 + k, CHIPS)
        out_refs[k][0:PIECE, :] = keep_ref[chip]
        out_refs[k][PIECE:, :] = got_ref[chip]


def split(part, keep, got):
    pair = jax.ShapeDtypeStruct((2 * PIECE, keep.shape[2]), BF16)
    return pl.pallas_call(
        split_kernel,
        compiler_params=LIMIT,
        in_specs=[SMEM_SPEC, VMEM_SPEC, VMEM_SPEC],
        out_specs=[VMEM_SPEC] * CHIPS,
        out_shape=[pair] * CHIPS,
    )(part, keep, got)


def pick_kernel(place_ref, first_ref, *refs):
    pairs = refs[:CHIPS]
    out_ref, members, chosen = refs[CHIPS:]
    cells = members.shape[1]
    core = place_ref[1] % 2
    for k in range(CHIPS):
        source = lax.rem(place_ref[1] // 2 + CHIPS - k, CHIPS) * 2
        for n, owner in enumerate((core, 1 - core)):
            at = pl.multiple_of((source + owner) * PIECE, PIECE)
            members[pl.ds(at, PIECE), :] = pairs[k][n * PIECE : (n + 1) * PIECE, :]
    tile = place_ref[0].astype(F32)
    slots = lax.broadcasted_iota(jnp.int32, (CAP, OBS), 0).astype(F32)
    lanes = lax.broadcasted_iota(jnp.int32, (CAP, cells), 1).astype(F32)
    for d in range(TILES):
        codes = first_ref[d, CODES:FIRST, :].astype(F32)
        cell = codes[0:1] * 128.0 + codes[1:2] - tile * float(cells)
        inside = (cell >= 0.0) & (cell < float(cells))
        here = jnp.where((slots == codes[2:3]) & inside, cell + 1.0, 0.0)
        at = jnp.sum(here, axis=1, keepdims=True) - 1.0
        chosen[d * CAP : (d + 1) * CAP, :] = jnp.where(lanes == at, 1.0, 0.0).astype(BF16)
    out_ref[...] = dot(chosen[...], members[...], NT).astype(BF16)


def pick(place, first, pieces):
    cells = pieces[0].shape[1]
    return pl.pallas_call(
        pick_kernel,
        compiler_params=LIMIT,
        in_specs=[SMEM_SPEC] + [VMEM_SPEC] * (1 + CHIPS),
        out_specs=VMEM_SPEC,
        out_shape=jax.ShapeDtypeStruct((TILES * CAP, SLICES * PIECE), BF16),
        scratch_shapes=[
            pltpu.VMEM((SLICES * PIECE, cells), BF16),
            pltpu.VMEM((TILES * CAP, cells), BF16),
        ],
    )(place, first, *pieces)


def own_kernel(pos_ref, recv_ref, out_ref, all_ref):
    rows = lax.broadcasted_iota(jnp.int32, (TILES * CAP, OBS), 0)
    chosen = jnp.where(rows == pos_ref[...], 1.0, 0.0).astype(BF16)
    mine = dot(recv_ref[...].T, chosen).astype(BF16)
    shape = (SLICE * MEMBERS, SLICES * PIECE)
    row = lax.broadcasted_iota(jnp.int32, shape, 0)
    lane = lax.broadcasted_iota(jnp.int32, shape, 1)
    level, member = jnp.right_shift(row, 4), row & 15
    source = jnp.right_shift(member, 1) * PIECE + 2 * level + (member & 1)
    turn = jnp.where(lane == source, 1.0, 0.0).astype(BF16)
    mine = dot(turn, mine)
    out_ref[...] = mine.astype(BF16)
    copies(all_ref, mine)


def own(position, recv):
    rows = SLICE * MEMBERS
    return pl.pallas_call(
        own_kernel,
        compiler_params=LIMIT,
        in_specs=[VMEM_SPEC, VMEM_SPEC],
        out_specs=[VMEM_SPEC, VMEM_SPEC],
        out_shape=[
            jax.ShapeDtypeStruct((rows, OBS), BF16),
            jax.ShapeDtypeStruct((TILES, rows, OBS), BF16),
        ],
    )(position, recv)


def pair_kernel(mine_ref, got_ref, out_ref):
    rows = mine_ref.shape[0]
    out_ref[0:rows, :] = mine_ref[...]
    out_ref[rows:, :] = got_ref[...]


def paired(mine, got):
    return pl.pallas_call(
        pair_kernel,
        compiler_params=LIMIT,
        in_specs=[VMEM_SPEC, VMEM_SPEC],
        out_specs=VMEM_SPEC,
        out_shape=jax.ShapeDtypeStruct((2 * mine.shape[0], OBS), BF16),
    )(mine, got)


def gathered_kernel(part_ref, *refs):
    rows = SLICE * MEMBERS
    pairs = refs[:CHIPS]
    out_ref, mem = refs[CHIPS:]
    chip, core = part_ref[0] // 2, part_ref[0] % 2
    for k in range(CHIPS):
        source = lax.rem(chip + CHIPS - k, CHIPS) * 2
        for n, owner in enumerate((core, 1 - core)):
            at = pl.multiple_of((source + owner) * rows, rows)
            mem[pl.ds(at, rows), :] = pairs[k][n * rows : (n + 1) * rows, :].astype(F32)
    for m in range(MEMBERS):
        out_ref[m * FULL : (m + 1) * FULL, :] = mem[pl.ds(m, FULL, stride=MEMBERS), :]


def gathered(part, pairs):
    return pl.pallas_call(
        gathered_kernel,
        compiler_params=LIMIT,
        in_specs=[SMEM_SPEC] + [VMEM_SPEC] * CHIPS,
        out_specs=VMEM_SPEC,
        out_shape=jax.ShapeDtypeStruct((MEMBERS * FULL, OBS), F32),
        scratch_shapes=[pltpu.VMEM((MEMBERS * FULL, OBS), F32)],
        cost_estimate=pl.CostEstimate(flops=10**6, bytes_accessed=2 * 10**6, transcendentals=0),
    )(part, *pairs)


def near_kernel(col_ref, first_ref, table_ref, out_ref):
    mine = col_ref[...]
    my_x = (mine // CB).astype(F32)
    my_b = mine % CB
    hot = jnp.where(lax.broadcasted_iota(jnp.int32, (OBS, CB), 1) == my_b, 1.0, 0.0).astype(BF16)
    reach = [dot(hot, table_ref[a]).astype(BF16) for a in range(STEPS + 1)]
    rows = lax.broadcasted_iota(jnp.int32, (CB, OBS), 0)
    for d in range(TILES):
        codes = first_ref[d, CODES:FIRST, :].astype(F32).astype(jnp.int32)
        hi, lo = codes[0:1], codes[1:2]
        x = (hi * 4 + lo // CB).astype(F32)
        there = jnp.where(rows == lo % CB, 1.0, 0.0).astype(BF16)
        gap = jnp.abs(my_x - x)
        gap = jnp.minimum(gap, float(NX) - gap)
        total = jnp.zeros((OBS, OBS), F32)
        for a in range(STEPS + 1):
            total = jnp.where(gap == float(a), dot(reach[a], there), total)
        out_ref[:, d * OBS : (d + 1) * OBS] = total.astype(BF16)


def near_of(column, first, table):
    return pl.pallas_call(
        near_kernel,
        compiler_params=LIMIT,
        in_specs=[VMEM_SPEC, VMEM_SPEC, VMEM_SPEC],
        out_specs=VMEM_SPEC,
        out_shape=jax.ShapeDtypeStruct((OBS, TILES * OBS), BF16),
        cost_estimate=pl.CostEstimate(flops=2 * 10**7, bytes_accessed=4 * 10**6, transcendentals=0),
    )(column, first, table)


def covariance_kernel(
    probes, scale, part_ref, all_ref, adj_ref, near_ref, mem_ref, vert_ref, *refs
):
    groups = probes // K
    prod, acc, adj, out = refs[2 * groups :]
    rows = SLICE * MEMBERS
    adj[...] = adj_ref[...].astype(F32)

    def probe(p, carry):
        for d in range(TILES):
            for level in range(SLICE):
                row = adj[d, pl.ds(p * SLICE + level, 1), :]
                row = jnp.broadcast_to(row, (MEMBERS, OBS)).astype(BF16)
                at = slice(level * MEMBERS, (level + 1) * MEMBERS)
                prod[at, d * OBS : (d + 1) * OBS] = all_ref[d, at, :] * row
        acc[pl.ds(pl.multiple_of(p * rows, rows), rows), :] = dot(prod[...], near_ref[...], NT)
        return carry

    lax.fori_loop(0, probes, probe, 0)
    vert = vert_ref[...]
    for p in range(probes):
        total = None
        for m in range(MEMBERS):
            smooth = acc[pl.ds(p * rows + m, SLICE, stride=MEMBERS), :].astype(BF16)
            term = mem_ref[m * FULL : (m + 1) * FULL, :] * dot(vert, smooth)
            total = term if total is None else total + term
        out[p * FULL : (p + 1) * FULL, :] = total * scale
    half = K * FULL // 2
    core = part_ref[0] % 2
    for g in range(groups):
        at = 2 * g * half
        low, high = out[at : at + half, :], out[at + half : at + 2 * half, :]
        refs[2 * g][...] = jnp.where(core == 0, low, high).astype(BF16)
        refs[2 * g + 1][...] = jnp.where(core == 0, high, low).astype(BF16)


def covariance(probes, scale, part, everyone, adjoints, near, mem, vert):
    rows = SLICE * MEMBERS
    half = jax.ShapeDtypeStruct((K * FULL // 2, OBS), BF16)
    groups = probes // K
    return pl.pallas_call(
        functools.partial(covariance_kernel, probes, scale),
        compiler_params=LIMIT,
        in_specs=[SMEM_SPEC] + [VMEM_SPEC] * 5,
        out_specs=[VMEM_SPEC] * (2 * groups),
        out_shape=[half] * (2 * groups),
        scratch_shapes=[
            pltpu.VMEM((rows, TILES * OBS), BF16),
            pltpu.VMEM((probes * rows, OBS), F32),
            pltpu.VMEM(adjoints.shape, F32),
            pltpu.VMEM((probes * FULL, OBS), F32),
        ],
    )(part, everyone, adjoints, near, mem, vert)


def exchange(value, axis):
    return lax.all_to_all(value, axis, 0, 0, tiled=True)


def swap_cores(value):
    return lax.ppermute(value, "mem", [(j, j ^ 1) for j in range(SLICES)])


def to_other_chip(value, k):
    return lax.ppermute(value, "mem", [(j, (j + 2 * k) % SLICES) for j in range(SLICES)])


def from_other_chips(value):
    return [to_other_chip(value, k) for k in range(1, CHIPS)]


def sum_over_mem(keep, send):
    kept = (keep.astype(F32) + swap_cores(send).astype(F32)).astype(BF16)
    others = from_other_chips(kept)
    total = (kept.astype(F32) + others[1].astype(F32)) + (
        others[0].astype(F32) + others[2].astype(F32)
    )
    total = total.astype(BF16)
    return total, swap_cores(total)


def on_device(members, vertical, jacobian, sketch_bits, test_bits, obs_column, obs_slot):
    slice_id = lax.axis_index("mem").astype(jnp.int32)
    part = slice_id.reshape(1)
    my_tile = lax.axis_index(TILE).astype(jnp.int32)
    local, levels, cells = members.shape
    size = float(OBS * TILES * CHAN)
    scale = 1.0 / ((MEMBERS - 1) * 5.0**STEPS * WALK_SCALE)

    jac = jnp.transpose(jacobian, (2, 1, 0))
    sketch = jnp.swapaxes(sketch_bits, 1, 2)
    test = jnp.swapaxes(test_bits, 1, 2)
    column, slot = obs_column.reshape(1, OBS), obs_slot.reshape(1, OBS)
    first, sign = sign_adjoints(part, sketch, test, column, slot, jac)
    first, members = lax.optimization_barrier((first, members))
    first = exchange(first, TILE)

    padded = jnp.pad(jnp.swapaxes(members, 0, 1), ((0, FULL - levels), (0, 0), (0, 0)))
    padded = padded.reshape(SLICES, SLICE * local, cells)
    padded = jnp.pad(padded, ((0, 0), (0, PIECE - SLICE * local), (0, 0)))
    keep, send = by_parity(part, padded)
    pairs = list(split(part, keep, swap_cores(send)))
    for k in range(1, CHIPS):
        pairs[k] = to_other_chip(pairs[k], k)

    place = jnp.stack([my_tile, slice_id])
    picked = pick(place, first, pairs)
    arrived = exchange(picked.reshape(TILES, CAP, -1), TILE)
    near = near_of(obs_column.reshape(OBS, 1), first, jnp.asarray(walk_table(), BF16))
    vert = jnp.pad(vertical, ((0, FULL - levels), (0, FULL - levels)))
    vert = lax.dynamic_slice_in_dim(vert, slice_id * SLICE, SLICE, axis=1)
    arrived, near, vert = lax.optimization_barrier((arrived, near, vert))
    position = (obs_column // cells * CAP + obs_slot).reshape(1, OBS)
    mine, everyone = own(position, arrived.reshape(TILES * CAP, -1))
    everyone = exchange(everyone, TILE)
    pair = paired(mine, swap_cores(mine))
    mem = gathered(part, [pair] + from_other_chips(pair))

    halves = covariance(2 * K, scale, part, everyone, first, near, mem, vert)
    sketch_1 = sum_over_mem(halves[0], halves[1])
    test_1 = sum_over_mem(halves[2], halves[3])
    second, image = images(part, *sketch_1, test, jac)
    second = exchange(second, TILE)
    z = test_images(part, *test_1, jac)
    second, z = lax.optimization_barrier((second, z))
    halves = covariance(K, scale, part, everyone, second, near, mem, vert)
    coefs = coefficients(size, second)
    mine_2, other_2 = sum_over_mem(*halves)
    mine_2, coefs = lax.optimization_barrier((mine_2, coefs))
    parts = inner_products(part, test_1, (mine_2, other_2), sign, image)
    parts = exchange(parts.reshape(-1, 1, OBS), ("mem", *TILE))
    image_q, image_w = outputs(part, mine_2, other_2, coefs, z, jac)
    mean, rayleigh = traces(size, parts.reshape(-1, OBS), coefs)
    return (
        jnp.swapaxes(image_q, 1, 2),
        jnp.swapaxes(image_w, 1, 2),
        mean.reshape(()),
        rayleigh.reshape(()),
    )


def solution(mesh):
    finer = Mesh(mesh.devices.reshape(mesh.shape["mem"], 4, 4), ("mem", "tile_0", "tile_1"))
    return jax.shard_map(
        on_device,
        mesh=finer,
        in_specs=(
            P("mem", None, TILE),
            P(),
            P(TILE, None, None),
            P(None, TILE, None),
            P(None, TILE, None),
            P(TILE),
            P(TILE),
        ),
        out_specs=(P(None, TILE, None), P(None, TILE, None), P(), P()),
        check_vma=False,
    )
```

```python
import functools

import jax
import jax.numpy as jnp
import numpy as np
from jax import lax
from jax.experimental import pallas as pl
from jax.experimental.pallas import tpu as pltpu
from jax.sharding import Mesh
from jax.sharding import PartitionSpec as P

CB = 32
NX = 256
K = 3
STEPS = 6
TILE = ("tile_0", "tile_1")
TILES = 16
SLICES = 8
LEVELS = 137
SLICE = 18
FULL = SLICES * SLICE
MEMBERS = 16
PIECE = 48
CAP = 32
OBS = 128
CHAN = 231
CPAD = 240
BLOCK = 9
BLOCKS = -(-LEVELS // BLOCK)
REST = LEVELS - (BLOCKS - 1) * BLOCK
CODES = 112
FIRST = 120
GRAMS = 56
SECOND = 64
OWN = 56
HALVES = K * FULL // 2


LIMIT = pltpu.CompilerParams(vmem_limit_bytes=24 * 2**20)
WIDE = pltpu.CompilerParams(vmem_limit_bytes=59000000)
F32 = jnp.float32
BF16 = jnp.bfloat16
VMEM_SPEC = pl.BlockSpec(memory_space=pltpu.VMEM)
SMEM_SPEC = pl.BlockSpec(memory_space=pltpu.SMEM)
NT = (((1,), (1,)), ((), ()))

WALK_SCALE = 1.3338


def walk_table():
    walks = np.zeros((2 * STEPS + 1, 2 * STEPS + 1))
    walks[STEPS, STEPS] = 1
    for _ in range(STEPS):
        grown = walks.copy()
        grown[1:] += walks[:-1]
        grown[:-1] += walks[1:]
        grown[:, 1:] += walks[:, :-1]
        grown[:, :-1] += walks[:, 1:]
        walks = grown

    def count(a, d):
        return walks[STEPS + a, STEPS + d] if d <= STEPS else 0.0

    table = np.zeros((STEPS + 1, CB, CB), np.float32)
    for a in range(STEPS + 1):
        for b in range(CB):
            for c in range(CB):
                table[a, b, c] = (
                    count(a, abs(b - c)) + count(a, b + c + 1) + count(a, 2 * CB - 1 - b - c)
                )
    return table * WALK_SCALE


def dot(a, b, dims=(((1,), (0,)), ((), ()))):
    return lax.dot_general(a, b, dims, preferred_element_type=F32)


def channel_chunks():
    return [(c, min(16, CHAN - c)) for c in range(0, CHAN, 16)]


def jac_rows(jac_ref, level, c, width):
    rows = jac_ref[level, c : c + width, :].astype(F32)
    if width % 8:
        fill = jnp.zeros((8 - width % 8, OBS), F32)
        rows = jnp.concatenate([rows, fill], axis=0)
    return [rows[k : k + 8] for k in range(0, rows.shape[0], 8)]


def back_rows(jac_ref, base, vec_ref, probes, first, put):
    def trio(t, carry):
        levels = [jnp.minimum(first + 3 * t + k, LEVELS - 1) - base for k in range(3)]
        acc = {}
        for c, width in channel_chunks():
            vecs = [
                [vec_ref[p, c + 8 * k : c + 8 * k + 8, :] for k in range(-(-width // 8))]
                for p in range(probes)
            ]
            for n, level in enumerate(levels):
                for k, rows in enumerate(jac_rows(jac_ref, level, c, width)):
                    for p in range(probes):
                        term = rows * vecs[p][k]
                        acc[p, n] = acc[p, n] + term if (p, n) in acc else term
        for n in range(3):
            valid = first + 3 * t + n < LEVELS
            for p in range(probes):
                row = jnp.sum(acc[p, n], axis=0, keepdims=True)
                put(p, 3 * t + n, jnp.where(valid, row, 0.0))
        return carry

    lax.fori_loop(0, SLICE // 3, trio, 0)


def forward_block(jac_ref, prof_ref, img_ref, probes, first, count):
    weights = [
        [
            jnp.broadcast_to(prof_ref[pl.ds(p * FULL + first + level, 1), :], (8, OBS))
            for level in range(count)
        ]
        for p in range(probes)
    ]
    for c, width in channel_chunks():
        parts = -(-width // 8)
        acc = [
            [img_ref[p, c + 8 * k : c + 8 * k + 8, :] for k in range(parts)] for p in range(probes)
        ]
        for level in range(count):
            for k, rows in enumerate(jac_rows(jac_ref, first + level, c, width)):
                for p in range(probes):
                    acc[p][k] = acc[p][k] + rows * weights[p][level]
        for p in range(probes):
            for k in range(parts):
                img_ref[p, c + 8 * k : c + 8 * k + 8, :] = acc[p][k]


def jac_copy(jac_hbm, jac_ref, sems, k, count=BLOCK):
    levels = pl.ds(k * BLOCK, count)
    return pltpu.make_async_copy(jac_hbm.at[levels], jac_ref.at[levels], sems.at[k])


def start_jac(jac_hbm, jac_ref, sems):
    for k in range(BLOCKS):
        jac_copy(jac_hbm, jac_ref, sems, k, BLOCK if k < BLOCKS - 1 else REST).start()


def forward(jac_hbm, jac_ref, sems, prof_ref, img_ref, probes):
    def block(k, carry):
        jac_copy(jac_hbm, jac_ref, sems, k).wait()
        forward_block(jac_ref, prof_ref, img_ref, probes, k * BLOCK, BLOCK)
        return carry

    lax.fori_loop(0, BLOCKS - 1, block, 0)
    jac_copy(jac_hbm, jac_ref, sems, BLOCKS - 1, REST).wait()
    forward_block(jac_ref, prof_ref, img_ref, probes, (BLOCKS - 1) * BLOCK, REST)


JAC_SCRATCH = [pltpu.VMEM((LEVELS, CHAN, OBS), BF16), pltpu.SemaphoreType.DMA((BLOCKS,))]
HBM_SPEC = pl.BlockSpec(memory_space=pl.ANY)
COST = pl.CostEstimate(flops=4 * 10**7, bytes_accessed=10**7, transcendentals=0)


def copies(out_ref, message):
    message = message.astype(BF16)
    for d in range(TILES):
        out_ref[d] = message


def signs_kernel(
    part_ref, sketch_ref, test_ref, column_ref, slot_ref, jac_hbm, out_ref, rows, jac, sem, vec
):
    first = part_ref[0] * SLICE
    base = jnp.minimum(first, LEVELS - SLICE)
    copy = pltpu.make_async_copy(jac_hbm.at[pl.ds(base, SLICE)], jac, sem)
    copy.start()
    rows[...] = jnp.zeros_like(rows)
    for p in range(K):
        vec[p, 0:CHAN, :] = (2 * sketch_ref[p] - 1).astype(F32)
        vec[K + p, 0:CHAN, :] = (2 * test_ref[p] - 1).astype(F32)
        vec[p, CHAN:CPAD, :] = jnp.zeros((CPAD - CHAN, OBS), F32)
        vec[K + p, CHAN:CPAD, :] = jnp.zeros((CPAD - CHAN, OBS), F32)
    column = column_ref[...]
    rows[CODES : CODES + 1, :] = jnp.right_shift(column, 7).astype(F32)
    rows[CODES + 1 : CODES + 2, :] = (column & 127).astype(F32)
    rows[CODES + 2 : CODES + 3, :] = slot_ref[...].astype(F32)

    def put(p, level, row):
        rows[pl.ds(p * SLICE + level, 1), :] = row

    copy.wait()
    back_rows(jac, base, vec, 2 * K, first, put)
    copies(out_ref, rows[...])


def sign_adjoints(part, sketch, test, column, slot, jac):
    return pl.pallas_call(
        signs_kernel,
        compiler_params=WIDE,
        in_specs=[SMEM_SPEC] + [VMEM_SPEC] * 4 + [HBM_SPEC],
        out_specs=[VMEM_SPEC, VMEM_SPEC],
        out_shape=[
            jax.ShapeDtypeStruct((TILES, FIRST, OBS), BF16),
            jax.ShapeDtypeStruct((FIRST, OBS), F32),
        ],
        scratch_shapes=[
            pltpu.VMEM((SLICE, CHAN, OBS), BF16),
            pltpu.SemaphoreType.DMA(()),
            pltpu.VMEM((2 * K, CPAD, OBS), F32),
        ],
        cost_estimate=pl.CostEstimate(flops=10**7, bytes_accessed=2 * 10**6, transcendentals=0),
    )(part, sketch, test, column, slot, jac)


def images_kernel(
    part_ref, mine_ref, other_ref, test_ref, jac_hbm, out_ref, rows, jac, sems, prof, img_ref
):
    start_jac(jac_hbm, jac, sems)
    core = part_ref[0] % 2
    rows[...] = jnp.zeros_like(rows)
    img_ref[...] = jnp.zeros_like(img_ref)
    prof[...] = jnp.where(core == 0, mine_ref[...].astype(F32), other_ref[...].astype(F32))
    forward(jac_hbm, jac, sems, prof, img_ref, K)

    def put(p, level, row):
        rows[pl.ds(p * SLICE + level, 1), :] = row

    back_rows(jac, 0, img_ref, K, part_ref[0] * SLICE, put)
    lanes = lax.broadcasted_iota(jnp.int32, (1, OBS), 1)
    gram = jnp.zeros((1, OBS), F32)
    for i in range(K):
        for j in range(K):
            if j <= i:
                value = jnp.sum(img_ref[i] * img_ref[j])
                gram = jnp.where(lanes == i * K + j, value, gram)
            signs = (2 * test_ref[j] - 1).astype(F32)
            value = jnp.sum(img_ref[i, 0:CHAN, :] * signs)
            gram = jnp.where(lanes == K * K + i * K + j, value, gram)
    high = gram.astype(BF16).astype(F32)
    mid = (gram - high).astype(BF16).astype(F32)
    rows[GRAMS : GRAMS + 1, :] = high
    rows[GRAMS + 1 : GRAMS + 2, :] = mid
    rows[GRAMS + 2 : GRAMS + 3, :] = gram - high - mid
    copies(out_ref, rows[...])


def images(part, mine, other, test, jac):
    return pl.pallas_call(
        images_kernel,
        compiler_params=WIDE,
        in_specs=[SMEM_SPEC, VMEM_SPEC, VMEM_SPEC, VMEM_SPEC, HBM_SPEC],
        out_specs=[VMEM_SPEC] * 2,
        out_shape=[
            jax.ShapeDtypeStruct((TILES, SECOND, OBS), BF16),
            jax.ShapeDtypeStruct((SECOND, OBS), F32),
        ],
        scratch_shapes=JAC_SCRATCH
        + [pltpu.VMEM((K * FULL, OBS), F32), pltpu.VMEM((K, CPAD, OBS), F32)],
        cost_estimate=COST,
    )(part, mine, other, test, jac)


def test_images_kernel(
    part_ref, mine_ref, other_ref, test_ref, jac_hbm, img_ref, sign_ref, jac, sems, prof
):
    start_jac(jac_hbm, jac, sems)
    core = part_ref[0] % 2
    img_ref[...] = jnp.zeros_like(img_ref)
    prof[...] = jnp.where(core == 0, other_ref[...].astype(F32), mine_ref[...].astype(F32))
    forward(jac_hbm, jac, sems, prof, img_ref, K)
    values = []
    for j in range(K):
        signs = (2 * test_ref[j] - 1).astype(F32)
        values.append(jnp.sum(img_ref[j, 0:CHAN, :] * signs))
    sign_ref[...] = row_of([0.0] * (2 * K * K) + values)


def test_images(part, mine, other, test, jac):
    return pl.pallas_call(
        test_images_kernel,
        compiler_params=WIDE,
        in_specs=[SMEM_SPEC] + [VMEM_SPEC] * 3 + [HBM_SPEC],
        out_specs=[VMEM_SPEC, VMEM_SPEC],
        out_shape=[
            jax.ShapeDtypeStruct((K, CPAD, OBS), F32),
            jax.ShapeDtypeStruct((1, OBS), F32),
        ],
        scratch_shapes=JAC_SCRATCH + [pltpu.VMEM((K * FULL, OBS), F32)],
        cost_estimate=COST,
    )(part, mine, other, test, jac)


def coefficients_kernel(size, second_ref, out_ref):
    total = jnp.zeros((1, OBS), F32)
    for d in range(TILES):
        got = second_ref[d, GRAMS : GRAMS + 8, :].astype(F32)
        total = total + jnp.sum(got, axis=0, keepdims=True)
    entry = functools.partial(lane_of, total)
    g = [[entry(i * K + j) for j in range(i + 1)] for i in range(K)]
    c = [[entry(K * K + i * K + j) for j in range(K)] for i in range(K)]
    l00 = jnp.sqrt(g[0][0])
    l10, l20 = g[1][0] / l00, g[2][0] / l00
    l11 = jnp.sqrt(g[1][1] - l10 * l10)
    l21 = (g[2][1] - l20 * l10) / l11
    l22 = jnp.sqrt(g[2][2] - l20 * l20 - l21 * l21)
    i00, i11, i22 = 1.0 / l00, 1.0 / l11, 1.0 / l22
    i10 = -l10 * i00 * i11
    i21 = -l21 * i11 * i22
    i20 = -(l20 * i00 + l21 * i10) * i22
    inv = [[i00], [i10, i11], [i20, i21, i22]]
    root = size**0.5
    lower = [[root * value for value in row] for row in inv]
    share = [
        [sum(inv[i][k] * c[k][j] for k in range(i + 1)) / root for j in range(K)] for i in range(K)
    ]
    out_ref[...] = row_of([v for row in lower for v in row] + [v for row in share for v in row])


def coefficients(size, second):
    return pl.pallas_call(
        functools.partial(coefficients_kernel, size),
        compiler_params=LIMIT,
        in_specs=[VMEM_SPEC],
        out_specs=VMEM_SPEC,
        out_shape=jax.ShapeDtypeStruct((1, OBS), F32),
    )(second)


def coefficients_of(coef_ref):
    coef = functools.partial(lane_of, coef_ref[...])
    lower = [[coef(j * (j + 1) // 2 + i) for i in range(j + 1)] for j in range(K)]
    share = [[coef(2 * K + i * K + j) for j in range(K)] for i in range(K)]
    return lower, share


def lane_of(row, k):
    lanes = lax.broadcasted_iota(jnp.int32, row.shape, 1)
    return jnp.sum(jnp.where(lanes == k, row, 0.0), axis=1, keepdims=True)


def row_of(values):
    lanes = lax.broadcasted_iota(jnp.int32, (1, OBS), 1)
    row = jnp.zeros((1, OBS), F32)
    for k, value in enumerate(values):
        row = jnp.where(lanes == k, value, row)
    return row


def second_profiles(core, mine_ref, other_ref, prof):
    half = K * FULL // 2
    mine, other = mine_ref[...].astype(F32), other_ref[...].astype(F32)
    prof[0:half, :] = jnp.where(core == 0, mine, other)
    prof[half:, :] = jnp.where(core == 0, other, mine)


def inner_kernel(part_ref, mine_1_ref, other_1_ref, mine_2_ref, other_2_ref, sign_ref, *refs):
    pieces = refs[: SLICES // 2]
    out_ref, test_prof, prof, image = refs[SLICES // 2 :]
    chips = SLICES // 2
    chip, core = part_ref[0] // 2, part_ref[0] % 2
    second_profiles(core, mine_2_ref, other_2_ref, prof)
    test_prof[...] = jnp.where(
        core == 0, other_1_ref[...].astype(F32), mine_1_ref[...].astype(F32)
    )
    sums = {}
    for n in range(chips):
        image[...] = pieces[n][HALVES:, :].astype(F32)
        source = lax.rem(chip + chips - n, chips) * 2
        for side, owner in enumerate((core, 1 - core)):
            start = (source + owner) * SLICE
            rows = [
                image[side * OWN + k * SLICE : side * OWN + (k + 1) * SLICE, :] for k in range(K)
            ]
            for j in range(K):
                levels = pl.ds(j * FULL + start, SLICE)
                for kind, ref in enumerate((prof, test_prof)):
                    values = ref[levels, :]
                    for k in range(K):
                        term = rows[k] * values
                        key = (kind, k, j)
                        sums[key] = sums[key] + term if key in sums else term
    values = [jnp.sum(sums[0, k, j]) for k in range(K) for j in range(K)]
    values += [jnp.sum(sums[1, k, j]) for j in range(K) for k in range(K)]
    out_ref[...] = jnp.broadcast_to(row_of(values) + sign_ref[...], out_ref.shape)


def inner_products(part, profiles_1, profiles_2, signs, messages):
    return pl.pallas_call(
        inner_kernel,
        compiler_params=LIMIT,
        in_specs=[SMEM_SPEC] + [VMEM_SPEC] * 9,
        out_specs=VMEM_SPEC,
        out_shape=jax.ShapeDtypeStruct((TILES, OBS), F32),
        scratch_shapes=[
            pltpu.VMEM((K * FULL, OBS), F32),
            pltpu.VMEM((K * FULL, OBS), F32),
            pltpu.VMEM((2 * OWN, OBS), F32),
        ],
    )(part, *profiles_1, *profiles_2, signs, *messages)


def outputs_kernel(
    part_ref, mine_ref, other_ref, coef_ref, z_ref, jac_hbm, q_ref, w_ref, jac, sems, prof, x
):
    start_jac(jac_hbm, jac, sems)
    x[...] = jnp.zeros_like(x)
    second_profiles(part_ref[0] % 2, mine_ref, other_ref, prof)
    lower, share = coefficients_of(coef_ref)
    forward(jac_hbm, jac, sems, prof, x, K)
    image_q = []
    for j in range(K):
        q = None
        for i in range(j + 1):
            qx = lower[j][i] * x[i, 0:CHAN, :]
            q = qx if q is None else q + qx
        q_ref[j] = q
        image_q.append(q)
    for j in range(K):
        w = z_ref[j, 0:CHAN, :]
        for i in range(K):
            w = w - share[i][j] * image_q[i]
        w_ref[j] = w


def outputs(part, mine, other, coefs, z, jac):
    return pl.pallas_call(
        outputs_kernel,
        compiler_params=WIDE,
        in_specs=[SMEM_SPEC] + [VMEM_SPEC] * 4 + [HBM_SPEC],
        out_specs=[VMEM_SPEC] * 2,
        out_shape=[jax.ShapeDtypeStruct((K, CHAN, OBS), F32)] * 2,
        scratch_shapes=JAC_SCRATCH
        + [pltpu.VMEM((K * FULL, OBS), F32), pltpu.VMEM((K, CPAD, OBS), F32)],
        cost_estimate=COST,
    )(part, mine, other, coefs, z, jac)


def traces_kernel(size, parts_ref, coef_ref, mean_ref, rayleigh_ref):
    total = functools.partial(lane_of, jnp.sum(parts_ref[...], axis=0, keepdims=True))
    lower, share = coefficients_of(coef_ref)
    yx = [[total(k * K + j) for j in range(K)] for k in range(K)]
    zy = [[total(K * K + j * K + k) for k in range(K)] for j in range(K)]
    tz = [total(2 * K * K + j) for j in range(K)]
    quad = [
        [
            sum(
                lower[i][a] * lower[k][b] * yx[a][b]
                for a in range(i + 1)
                for b in range(k + 1)
            )
            for k in range(K)
        ]
        for i in range(K)
    ]
    cross = [
        [sum(lower[i][b] * zy[j][b] for b in range(i + 1)) for j in range(K)] for i in range(K)
    ]
    trace_q = quad[0][0] + quad[1][1] + quad[2][2]
    trace_w = 0.0
    for j in range(K):
        trace_w = trace_w + tz[j]
        for i in range(K):
            trace_w = trace_w - 2.0 * share[i][j] * cross[i][j]
            for k in range(K):
                trace_w = trace_w + share[i][j] * share[k][j] * quad[i][k]
    mean = trace_q / (size * size) + trace_w / (K * size)
    mean_ref[0] = jnp.sum(mean)
    rayleigh_ref[0] = jnp.sum(trace_q / (K * size))


def traces(size, parts, coefs):
    return pl.pallas_call(
        functools.partial(traces_kernel, size),
        compiler_params=LIMIT,
        in_specs=[VMEM_SPEC, VMEM_SPEC],
        out_specs=[SMEM_SPEC, SMEM_SPEC],
        out_shape=[jax.ShapeDtypeStruct((1,), F32)] * 2,
    )(parts, coefs)


CHIPS = SLICES // 2


def parity_kernel(part_ref, members_ref, keep_ref, send_ref):
    core = part_ref[0] % 2
    for chip in range(CHIPS):
        keep_ref[chip] = members_ref[2 * chip + core]
        send_ref[chip] = members_ref[2 * chip + 1 - core]


def by_parity(part, members):
    half = jax.ShapeDtypeStruct((CHIPS, *members.shape[1:]), BF16)
    return pl.pallas_call(
        parity_kernel,
        compiler_params=LIMIT,
        in_specs=[SMEM_SPEC, VMEM_SPEC],
        out_specs=[VMEM_SPEC, VMEM_SPEC],
        out_shape=[half, half],
    )(part, members)


def split_kernel(part_ref, keep_ref, got_ref, *out_refs):
    for k in range(CHIPS):
        chip = lax.rem(part_ref[0] // 2 + k, CHIPS)
        out_refs[k][0:PIECE, :] = keep_ref[chip]
        out_refs[k][PIECE:, :] = got_ref[chip]


def split(part, keep, got):
    pair = jax.ShapeDtypeStruct((2 * PIECE, keep.shape[2]), BF16)
    return pl.pallas_call(
        split_kernel,
        compiler_params=LIMIT,
        in_specs=[SMEM_SPEC, VMEM_SPEC, VMEM_SPEC],
        out_specs=[VMEM_SPEC] * CHIPS,
        out_shape=[pair] * CHIPS,
    )(part, keep, got)


def pick_kernel(place_ref, first_ref, *refs):
    pairs = refs[:CHIPS]
    out_ref, members, chosen = refs[CHIPS:]
    cells = members.shape[1]
    core = place_ref[1] % 2
    for k in range(CHIPS):
        source = lax.rem(place_ref[1] // 2 + CHIPS - k, CHIPS) * 2
        for n, owner in enumerate((core, 1 - core)):
            at = pl.multiple_of((source + owner) * PIECE, PIECE)
            members[pl.ds(at, PIECE), :] = pairs[k][n * PIECE : (n + 1) * PIECE, :]
    tile = place_ref[0].astype(F32)
    slots = lax.broadcasted_iota(jnp.int32, (CAP, OBS), 0).astype(F32)
    lanes = lax.broadcasted_iota(jnp.int32, (CAP, cells), 1).astype(F32)
    for d in range(TILES):
        codes = first_ref[d, CODES:FIRST, :].astype(F32)
        cell = codes[0:1] * 128.0 + codes[1:2] - tile * float(cells)
        inside = (cell >= 0.0) & (cell < float(cells))
        here = jnp.where((slots == codes[2:3]) & inside, cell + 1.0, 0.0)
        at = jnp.sum(here, axis=1, keepdims=True) - 1.0
        chosen[d * CAP : (d + 1) * CAP, :] = jnp.where(lanes == at, 1.0, 0.0).astype(BF16)
    out_ref[...] = dot(chosen[...], members[...], NT).astype(BF16)


def pick(place, first, pieces):
    cells = pieces[0].shape[1]
    return pl.pallas_call(
        pick_kernel,
        compiler_params=LIMIT,
        in_specs=[SMEM_SPEC] + [VMEM_SPEC] * (1 + CHIPS),
        out_specs=VMEM_SPEC,
        out_shape=jax.ShapeDtypeStruct((TILES * CAP, SLICES * PIECE), BF16),
        scratch_shapes=[
            pltpu.VMEM((SLICES * PIECE, cells), BF16),
            pltpu.VMEM((TILES * CAP, cells), BF16),
        ],
    )(place, first, *pieces)


def own_kernel(pos_ref, recv_ref, out_ref, all_ref):
    rows = lax.broadcasted_iota(jnp.int32, (TILES * CAP, OBS), 0)
    chosen = jnp.where(rows == pos_ref[...], 1.0, 0.0).astype(BF16)
    mine = dot(recv_ref[...].T, chosen).astype(BF16)
    shape = (SLICE * MEMBERS, SLICES * PIECE)
    row = lax.broadcasted_iota(jnp.int32, shape, 0)
    lane = lax.broadcasted_iota(jnp.int32, shape, 1)
    level, member = jnp.right_shift(row, 4), row & 15
    source = jnp.right_shift(member, 1) * PIECE + 2 * level + (member & 1)
    turn = jnp.where(lane == source, 1.0, 0.0).astype(BF16)
    mine = dot(turn, mine)
    out_ref[...] = mine.astype(BF16)
    copies(all_ref, mine)


def own(position, recv):
    rows = SLICE * MEMBERS
    return pl.pallas_call(
        own_kernel,
        compiler_params=LIMIT,
        in_specs=[VMEM_SPEC, VMEM_SPEC],
        out_specs=[VMEM_SPEC, VMEM_SPEC],
        out_shape=[
            jax.ShapeDtypeStruct((rows, OBS), BF16),
            jax.ShapeDtypeStruct((TILES, rows, OBS), BF16),
        ],
    )(position, recv)


def pair_kernel(mine_ref, got_ref, out_ref):
    rows = mine_ref.shape[0]
    out_ref[0:rows, :] = mine_ref[...]
    out_ref[rows:, :] = got_ref[...]


def paired(mine, got):
    return pl.pallas_call(
        pair_kernel,
        compiler_params=LIMIT,
        in_specs=[VMEM_SPEC, VMEM_SPEC],
        out_specs=VMEM_SPEC,
        out_shape=jax.ShapeDtypeStruct((2 * mine.shape[0], OBS), BF16),
    )(mine, got)


def gathered_kernel(part_ref, *refs):
    rows = SLICE * MEMBERS
    pairs = refs[:CHIPS]
    out_ref, mem = refs[CHIPS:]
    chip, core = part_ref[0] // 2, part_ref[0] % 2
    for k in range(CHIPS):
        source = lax.rem(chip + CHIPS - k, CHIPS) * 2
        for n, owner in enumerate((core, 1 - core)):
            at = pl.multiple_of((source + owner) * rows, rows)
            mem[pl.ds(at, rows), :] = pairs[k][n * rows : (n + 1) * rows, :].astype(F32)
    for m in range(MEMBERS):
        out_ref[m * FULL : (m + 1) * FULL, :] = mem[pl.ds(m, FULL, stride=MEMBERS), :]


def gathered(part, pairs):
    return pl.pallas_call(
        gathered_kernel,
        compiler_params=LIMIT,
        in_specs=[SMEM_SPEC] + [VMEM_SPEC] * CHIPS,
        out_specs=VMEM_SPEC,
        out_shape=jax.ShapeDtypeStruct((MEMBERS * FULL, OBS), F32),
        scratch_shapes=[pltpu.VMEM((MEMBERS * FULL, OBS), F32)],
        cost_estimate=pl.CostEstimate(flops=10**6, bytes_accessed=2 * 10**6, transcendentals=0),
    )(part, *pairs)


def near_kernel(col_ref, first_ref, table_ref, out_ref):
    mine = col_ref[...]
    my_x = (mine // CB).astype(F32)
    my_b = mine % CB
    hot = jnp.where(lax.broadcasted_iota(jnp.int32, (OBS, CB), 1) == my_b, 1.0, 0.0).astype(BF16)
    reach = [dot(hot, table_ref[a]).astype(BF16) for a in range(STEPS + 1)]
    rows = lax.broadcasted_iota(jnp.int32, (CB, OBS), 0)
    for d in range(TILES):
        codes = first_ref[d, CODES:FIRST, :].astype(F32).astype(jnp.int32)
        hi, lo = codes[0:1], codes[1:2]
        x = (hi * 4 + lo // CB).astype(F32)
        there = jnp.where(rows == lo % CB, 1.0, 0.0).astype(BF16)
        gap = jnp.abs(my_x - x)
        gap = jnp.minimum(gap, float(NX) - gap)
        total = jnp.zeros((OBS, OBS), F32)
        for a in range(STEPS + 1):
            total = jnp.where(gap == float(a), dot(reach[a], there), total)
        out_ref[:, d * OBS : (d + 1) * OBS] = total.astype(BF16)


def near_of(column, first, table):
    return pl.pallas_call(
        near_kernel,
        compiler_params=LIMIT,
        in_specs=[VMEM_SPEC, VMEM_SPEC, VMEM_SPEC],
        out_specs=VMEM_SPEC,
        out_shape=jax.ShapeDtypeStruct((OBS, TILES * OBS), BF16),
        cost_estimate=pl.CostEstimate(flops=2 * 10**7, bytes_accessed=4 * 10**6, transcendentals=0),
    )(column, first, table)


def covariance_kernel(
    probes, scale, part_ref, all_ref, adj_ref, near_ref, mem_ref, vert_ref, *refs
):
    carried = refs[:-6]
    keep_ref, send_ref, prod, acc, adj, out = refs[-6:]
    rows = SLICE * MEMBERS
    adj[...] = adj_ref[...].astype(F32)

    def probe(p, carry):
        for d in range(TILES):
            for level in range(SLICE):
                row = adj[d, pl.ds(p * SLICE + level, 1), :]
                row = jnp.broadcast_to(row, (MEMBERS, OBS)).astype(BF16)
                at = slice(level * MEMBERS, (level + 1) * MEMBERS)
                prod[at, d * OBS : (d + 1) * OBS] = all_ref[d, at, :] * row
        acc[pl.ds(pl.multiple_of(p * rows, rows), rows), :] = dot(prod[...], near_ref[...], NT)
        return carry

    lax.fori_loop(0, probes, probe, 0)
    vert = vert_ref[...]
    for p in range(probes):
        total = None
        for m in range(MEMBERS):
            smooth = acc[pl.ds(p * rows + m, SLICE, stride=MEMBERS), :].astype(BF16)
            term = mem_ref[m * FULL : (m + 1) * FULL, :] * dot(vert, smooth)
            total = term if total is None else total + term
        out[p * FULL : (p + 1) * FULL, :] = total * scale
    half = probes * FULL // 2
    core = part_ref[0] % 2
    low, high = out[0:half, :], out[half : 2 * half, :]
    keep_ref[...] = jnp.where(core == 0, low, high).astype(BF16)
    sent = jnp.where(core == 0, high, low)
    if carried:
        send_ref[half:, :] = carried[0][0:OWN, :].astype(BF16)
    send_ref[0:half, :] = sent.astype(BF16)


def covariance(probes, scale, part, everyone, adjoints, near, mem, vert, *carried):
    rows = SLICE * MEMBERS
    half = probes * FULL // 2
    extra = OWN * len(carried)
    return pl.pallas_call(
        functools.partial(covariance_kernel, probes, scale),
        compiler_params=LIMIT,
        in_specs=[SMEM_SPEC] + [VMEM_SPEC] * (5 + len(carried)),
        out_specs=[VMEM_SPEC, VMEM_SPEC],
        out_shape=[
            jax.ShapeDtypeStruct((half, OBS), BF16),
            jax.ShapeDtypeStruct((half + extra, OBS), BF16),
        ],
        scratch_shapes=[
            pltpu.VMEM((rows, TILES * OBS), BF16),
            pltpu.VMEM((probes * rows, OBS), F32),
            pltpu.VMEM(adjoints.shape, F32),
            pltpu.VMEM((probes * FULL + extra, OBS), F32),
        ],
    )(part, everyone, adjoints, near, mem, vert, *carried)


def exchange(value, axis):
    return lax.all_to_all(value, axis, 0, 0, tiled=True)


def swap_cores(value):
    return lax.ppermute(value, "mem", [(j, j ^ 1) for j in range(SLICES)])


def to_other_chip(value, k):
    return lax.ppermute(value, "mem", [(j, (j + 2 * k) % SLICES) for j in range(SLICES)])


def from_other_chips(value):
    return [to_other_chip(value, k) for k in range(1, CHIPS)]


def sum_over_mem(keep, send, carried=None):
    half = keep.shape[0]
    got = swap_cores(send)
    kept = (keep.astype(F32) + got[:half].astype(F32)).astype(BF16)
    message = kept
    if carried is not None:
        message = jnp.concatenate([kept, carried[:OWN].astype(BF16), got[half:]], axis=0)
    others = from_other_chips(message)
    total = (kept.astype(F32) + others[1][:half].astype(F32)) + (
        others[0][:half].astype(F32) + others[2][:half].astype(F32)
    )
    total = total.astype(BF16)
    return (total, swap_cores(total)), [message] + others


def on_device(members, vertical, jacobian, sketch_bits, test_bits, obs_column, obs_slot):
    slice_id = lax.axis_index("mem").astype(jnp.int32)
    part = slice_id.reshape(1)
    my_tile = lax.axis_index(TILE).astype(jnp.int32)
    local, levels, cells = members.shape
    size = float(OBS * TILES * CHAN)
    scale = 1.0 / ((MEMBERS - 1) * 5.0**STEPS * WALK_SCALE)

    jac = jnp.transpose(jacobian, (2, 1, 0))
    sketch = jnp.swapaxes(sketch_bits, 1, 2)
    test = jnp.swapaxes(test_bits, 1, 2)
    column, slot = obs_column.reshape(1, OBS), obs_slot.reshape(1, OBS)
    first, _ = sign_adjoints(part, sketch, test, column, slot, jac)
    first, members = lax.optimization_barrier((first, members))
    first = exchange(first, TILE)

    padded = jnp.pad(jnp.swapaxes(members, 0, 1), ((0, FULL - levels), (0, 0), (0, 0)))
    padded = padded.reshape(SLICES, SLICE * local, cells)
    padded = jnp.pad(padded, ((0, 0), (0, PIECE - SLICE * local), (0, 0)))
    keep, send = by_parity(part, padded)
    pairs = list(split(part, keep, swap_cores(send)))
    for k in range(1, CHIPS):
        pairs[k] = to_other_chip(pairs[k], k)

    place = jnp.stack([my_tile, slice_id])
    picked = pick(place, first, pairs)
    arrived = exchange(picked.reshape(TILES, CAP, -1), TILE)
    near = near_of(obs_column.reshape(OBS, 1), first, jnp.asarray(walk_table(), BF16))
    vert = jnp.pad(vertical, ((0, FULL - levels), (0, FULL - levels)))
    vert = lax.dynamic_slice_in_dim(vert, slice_id * SLICE, SLICE, axis=1)
    arrived, near, vert = lax.optimization_barrier((arrived, near, vert))
    position = (obs_column // cells * CAP + obs_slot).reshape(1, OBS)
    mine, everyone = own(position, arrived.reshape(TILES * CAP, -1))
    everyone = exchange(everyone, TILE)
    pair = paired(mine, swap_cores(mine))
    mem = gathered(part, [pair] + from_other_chips(pair))

    halves = covariance(2 * K, scale, part, everyone, first, near, mem, vert)
    (mine_1, other_1), _ = sum_over_mem(*halves)
    second, image = images(part, mine_1, other_1, test, jac)
    second = exchange(second, TILE)
    z, signs = test_images(part, mine_1, other_1, test, jac)
    second, z = lax.optimization_barrier((second, z))
    halves = covariance(K, scale, part, everyone, second, near, mem, vert, image)
    coefs = coefficients(size, second)
    (mine_2, other_2), messages = sum_over_mem(*halves, image)
    mine_2, coefs = lax.optimization_barrier((mine_2, coefs))
    parts = inner_products(part, (mine_1, other_1), (mine_2, other_2), signs, messages)
    parts = exchange(parts.reshape(-1, 1, OBS), TILE)
    image_q, image_w = outputs(part, mine_2, other_2, coefs, z, jac)
    mean, rayleigh = traces(size, parts.reshape(-1, OBS), coefs)
    return (
        jnp.swapaxes(image_q, 1, 2),
        jnp.swapaxes(image_w, 1, 2),
        mean.reshape(()),
        rayleigh.reshape(()),
    )


def solution(mesh):
    finer = Mesh(mesh.devices.reshape(mesh.shape["mem"], 4, 4), ("mem", "tile_0", "tile_1"))
    return jax.shard_map(
        on_device,
        mesh=finer,
        in_specs=(
            P("mem", None, TILE),
            P(),
            P(TILE, None, None),
            P(None, TILE, None),
            P(None, TILE, None),
            P(TILE),
            P(TILE),
        ),
        out_specs=(P(None, TILE, None), P(None, TILE, None), P(), P()),
        check_vma=False,
    )
```

```python
import functools

import jax
import jax.numpy as jnp
import numpy as np
from jax import lax
from jax.experimental import pallas as pl
from jax.experimental.pallas import tpu as pltpu
from jax.sharding import Mesh
from jax.sharding import PartitionSpec as P

CB = 32
NX = 256
K = 3
STEPS = 6
TILE = ("tile_0", "tile_1")
TILES = 16
SLICES = 8
LEVELS = 137
SLICE = 18
FULL = SLICES * SLICE
MEMBERS = 16
PIECE = 48
CAP = 32
OBS = 128
CHAN = 231
CPAD = 240
BLOCK = 9
BLOCKS = -(-LEVELS // BLOCK)
REST = LEVELS - (BLOCKS - 1) * BLOCK
CODES = 112
FIRST = 120
GRAMS = 56
SECOND = 64
OWN = 56
HALVES = K * FULL // 2


LIMIT = pltpu.CompilerParams(vmem_limit_bytes=24 * 2**20)
WIDE = pltpu.CompilerParams(vmem_limit_bytes=59000000)
F32 = jnp.float32
BF16 = jnp.bfloat16
VMEM_SPEC = pl.BlockSpec(memory_space=pltpu.VMEM)
SMEM_SPEC = pl.BlockSpec(memory_space=pltpu.SMEM)
NT = (((1,), (1,)), ((), ()))

WALK_SCALE = 1.3338


def walk_table():
    walks = np.zeros((2 * STEPS + 1, 2 * STEPS + 1))
    walks[STEPS, STEPS] = 1
    for _ in range(STEPS):
        grown = walks.copy()
        grown[1:] += walks[:-1]
        grown[:-1] += walks[1:]
        grown[:, 1:] += walks[:, :-1]
        grown[:, :-1] += walks[:, 1:]
        walks = grown

    def count(a, d):
        return walks[STEPS + a, STEPS + d] if d <= STEPS else 0.0

    table = np.zeros((STEPS + 1, CB, CB), np.float32)
    for a in range(STEPS + 1):
        for b in range(CB):
            for c in range(CB):
                table[a, b, c] = (
                    count(a, abs(b - c)) + count(a, b + c + 1) + count(a, 2 * CB - 1 - b - c)
                )
    return table * WALK_SCALE


def dot(a, b, dims=(((1,), (0,)), ((), ()))):
    return lax.dot_general(a, b, dims, preferred_element_type=F32)


def channel_chunks():
    return [(c, min(16, CHAN - c)) for c in range(0, CHAN, 16)]


def jac_rows(jac_ref, level, c, width):
    rows = jac_ref[level, c : c + width, :].astype(F32)
    if width % 8:
        fill = jnp.zeros((8 - width % 8, OBS), F32)
        rows = jnp.concatenate([rows, fill], axis=0)
    return [rows[k : k + 8] for k in range(0, rows.shape[0], 8)]


def back_rows(jac_ref, base, vec_ref, probes, first, put):
    def trio(t, carry):
        levels = [jnp.minimum(first + 3 * t + k, LEVELS - 1) - base for k in range(3)]
        acc = {}
        for c, width in channel_chunks():
            vecs = [
                [vec_ref[p, c + 8 * k : c + 8 * k + 8, :] for k in range(-(-width // 8))]
                for p in range(probes)
            ]
            for n, level in enumerate(levels):
                for k, rows in enumerate(jac_rows(jac_ref, level, c, width)):
                    for p in range(probes):
                        term = rows * vecs[p][k]
                        acc[p, n] = acc[p, n] + term if (p, n) in acc else term
        for n in range(3):
            valid = first + 3 * t + n < LEVELS
            for p in range(probes):
                row = jnp.sum(acc[p, n], axis=0, keepdims=True)
                put(p, 3 * t + n, jnp.where(valid, row, 0.0))
        return carry

    lax.fori_loop(0, SLICE // 3, trio, 0)


def forward_block(jac_ref, prof_ref, img_ref, probes, first, count):
    weights = [
        [
            jnp.broadcast_to(prof_ref[pl.ds(p * FULL + first + level, 1), :], (8, OBS))
            for level in range(count)
        ]
        for p in range(probes)
    ]
    for c, width in channel_chunks():
        parts = -(-width // 8)
        acc = [
            [img_ref[p, c + 8 * k : c + 8 * k + 8, :] for k in range(parts)] for p in range(probes)
        ]
        for level in range(count):
            for k, rows in enumerate(jac_rows(jac_ref, first + level, c, width)):
                for p in range(probes):
                    acc[p][k] = acc[p][k] + rows * weights[p][level]
        for p in range(probes):
            for k in range(parts):
                img_ref[p, c + 8 * k : c + 8 * k + 8, :] = acc[p][k]


def jac_copy(jac_hbm, jac_ref, sems, k, count=BLOCK):
    levels = pl.ds(k * BLOCK, count)
    return pltpu.make_async_copy(jac_hbm.at[levels], jac_ref.at[levels], sems.at[k])


def start_jac(jac_hbm, jac_ref, sems):
    for k in range(BLOCKS):
        jac_copy(jac_hbm, jac_ref, sems, k, BLOCK if k < BLOCKS - 1 else REST).start()


def forward(jac_hbm, jac_ref, sems, prof_ref, img_ref, probes):
    def block(k, carry):
        jac_copy(jac_hbm, jac_ref, sems, k).wait()
        forward_block(jac_ref, prof_ref, img_ref, probes, k * BLOCK, BLOCK)
        return carry

    lax.fori_loop(0, BLOCKS - 1, block, 0)
    jac_copy(jac_hbm, jac_ref, sems, BLOCKS - 1, REST).wait()
    forward_block(jac_ref, prof_ref, img_ref, probes, (BLOCKS - 1) * BLOCK, REST)


JAC_SCRATCH = [pltpu.VMEM((LEVELS, CHAN, OBS), BF16), pltpu.SemaphoreType.DMA((BLOCKS,))]
HBM_SPEC = pl.BlockSpec(memory_space=pl.ANY)
COST = pl.CostEstimate(flops=4 * 10**7, bytes_accessed=10**7, transcendentals=0)


def copies(out_ref, message):
    message = message.astype(BF16)
    for d in range(TILES):
        out_ref[d] = message


def signs_kernel(
    part_ref, sketch_hbm, test_hbm, column_ref, slot_ref, jac_hbm, out_ref,
    jac, sem, sketch_ref, test_ref, sems, vec, rows,
):
    first = part_ref[0] * SLICE
    base = jnp.minimum(first, LEVELS - SLICE)
    copy = pltpu.make_async_copy(jac_hbm.at[pl.ds(base, SLICE)], jac, sem)
    bits = [
        pltpu.make_async_copy(sketch_hbm, sketch_ref, sems.at[0]),
        pltpu.make_async_copy(test_hbm, test_ref, sems.at[1]),
    ]
    for move in (*bits, copy):
        move.start()
    rows[...] = jnp.zeros_like(rows)
    for move in bits:
        move.wait()
    for p in range(K):
        vec[p, 0:CHAN, :] = (2 * sketch_ref[p] - 1).astype(F32)
        vec[K + p, 0:CHAN, :] = (2 * test_ref[p] - 1).astype(F32)
        vec[p, CHAN:CPAD, :] = jnp.zeros((CPAD - CHAN, OBS), F32)
        vec[K + p, CHAN:CPAD, :] = jnp.zeros((CPAD - CHAN, OBS), F32)
    column = column_ref[...]
    rows[CODES : CODES + 1, :] = jnp.right_shift(column, 7).astype(F32)
    rows[CODES + 1 : CODES + 2, :] = (column & 127).astype(F32)
    rows[CODES + 2 : CODES + 3, :] = slot_ref[...].astype(F32)

    def put(p, level, row):
        rows[pl.ds(p * SLICE + level, 1), :] = row

    copy.wait()
    back_rows(jac, base, vec, 2 * K, first, put)
    copies(out_ref, rows[...])


def sign_adjoints(part, sketch, test, column, slot, jac):
    return pl.pallas_call(
        signs_kernel,
        compiler_params=WIDE,
        in_specs=[SMEM_SPEC, HBM_SPEC, HBM_SPEC, VMEM_SPEC, VMEM_SPEC, HBM_SPEC],
        out_specs=VMEM_SPEC,
        out_shape=jax.ShapeDtypeStruct((TILES, FIRST, OBS), BF16),
        scratch_shapes=[
            pltpu.VMEM((SLICE, CHAN, OBS), BF16),
            pltpu.SemaphoreType.DMA(()),
            pltpu.VMEM((K, CHAN, OBS), jnp.int32),
            pltpu.VMEM((K, CHAN, OBS), jnp.int32),
            pltpu.SemaphoreType.DMA((2,)),
            pltpu.VMEM((2 * K, CPAD, OBS), F32),
            pltpu.VMEM((FIRST, OBS), F32),
        ],
        cost_estimate=pl.CostEstimate(flops=10**7, bytes_accessed=2 * 10**6, transcendentals=0),
    )(part, sketch, test, column, slot, jac)


def images_kernel(
    part_ref, mine_ref, other_ref, test_ref, jac_hbm, out_ref, rows, jac, sems, prof, img_ref
):
    start_jac(jac_hbm, jac, sems)
    core = part_ref[0] % 2
    rows[...] = jnp.zeros_like(rows)
    img_ref[...] = jnp.zeros_like(img_ref)
    prof[...] = jnp.where(core == 0, mine_ref[...].astype(F32), other_ref[...].astype(F32))
    forward(jac_hbm, jac, sems, prof, img_ref, K)

    def put(p, level, row):
        rows[pl.ds(p * SLICE + level, 1), :] = row

    back_rows(jac, 0, img_ref, K, part_ref[0] * SLICE, put)
    lanes = lax.broadcasted_iota(jnp.int32, (1, OBS), 1)
    gram = jnp.zeros((1, OBS), F32)
    for i in range(K):
        for j in range(K):
            if j <= i:
                value = jnp.sum(img_ref[i] * img_ref[j])
                gram = jnp.where(lanes == i * K + j, value, gram)
            signs = (2 * test_ref[j] - 1).astype(F32)
            value = jnp.sum(img_ref[i, 0:CHAN, :] * signs)
            gram = jnp.where(lanes == K * K + i * K + j, value, gram)
    high = gram.astype(BF16).astype(F32)
    mid = (gram - high).astype(BF16).astype(F32)
    rows[GRAMS : GRAMS + 1, :] = high
    rows[GRAMS + 1 : GRAMS + 2, :] = mid
    rows[GRAMS + 2 : GRAMS + 3, :] = gram - high - mid
    copies(out_ref, rows[...])


def images(part, mine, other, test, jac):
    return pl.pallas_call(
        images_kernel,
        compiler_params=WIDE,
        in_specs=[SMEM_SPEC, VMEM_SPEC, VMEM_SPEC, VMEM_SPEC, HBM_SPEC],
        out_specs=[VMEM_SPEC] * 2,
        out_shape=[
            jax.ShapeDtypeStruct((TILES, SECOND, OBS), BF16),
            jax.ShapeDtypeStruct((SECOND, OBS), F32),
        ],
        scratch_shapes=JAC_SCRATCH
        + [pltpu.VMEM((K * FULL, OBS), F32), pltpu.VMEM((K, CPAD, OBS), F32)],
        cost_estimate=COST,
    )(part, mine, other, test, jac)


def test_images_kernel(
    part_ref, mine_ref, other_ref, test_ref, jac_hbm, img_ref, sign_ref, jac, sems, prof
):
    start_jac(jac_hbm, jac, sems)
    core = part_ref[0] % 2
    img_ref[...] = jnp.zeros_like(img_ref)
    prof[...] = jnp.where(core == 0, other_ref[...].astype(F32), mine_ref[...].astype(F32))
    forward(jac_hbm, jac, sems, prof, img_ref, K)
    values = []
    for j in range(K):
        signs = (2 * test_ref[j] - 1).astype(F32)
        values.append(jnp.sum(img_ref[j, 0:CHAN, :] * signs))
    sign_ref[...] = row_of([0.0] * (2 * K * K) + values)


def test_images(part, mine, other, test, jac):
    return pl.pallas_call(
        test_images_kernel,
        compiler_params=WIDE,
        in_specs=[SMEM_SPEC] + [VMEM_SPEC] * 3 + [HBM_SPEC],
        out_specs=[VMEM_SPEC, VMEM_SPEC],
        out_shape=[
            jax.ShapeDtypeStruct((K, CPAD, OBS), F32),
            jax.ShapeDtypeStruct((1, OBS), F32),
        ],
        scratch_shapes=JAC_SCRATCH + [pltpu.VMEM((K * FULL, OBS), F32)],
        cost_estimate=COST,
    )(part, mine, other, test, jac)


def coefficients_kernel(size, second_ref, out_ref):
    total = jnp.zeros((1, OBS), F32)
    for d in range(TILES):
        got = second_ref[d, GRAMS : GRAMS + 8, :].astype(F32)
        total = total + jnp.sum(got, axis=0, keepdims=True)
    entry = functools.partial(lane_of, total)
    g = [[entry(i * K + j) for j in range(i + 1)] for i in range(K)]
    c = [[entry(K * K + i * K + j) for j in range(K)] for i in range(K)]
    l00 = jnp.sqrt(g[0][0])
    l10, l20 = g[1][0] / l00, g[2][0] / l00
    l11 = jnp.sqrt(g[1][1] - l10 * l10)
    l21 = (g[2][1] - l20 * l10) / l11
    l22 = jnp.sqrt(g[2][2] - l20 * l20 - l21 * l21)
    i00, i11, i22 = 1.0 / l00, 1.0 / l11, 1.0 / l22
    i10 = -l10 * i00 * i11
    i21 = -l21 * i11 * i22
    i20 = -(l20 * i00 + l21 * i10) * i22
    inv = [[i00], [i10, i11], [i20, i21, i22]]
    root = size**0.5
    lower = [[root * value for value in row] for row in inv]
    share = [
        [sum(inv[i][k] * c[k][j] for k in range(i + 1)) / root for j in range(K)] for i in range(K)
    ]
    out_ref[...] = row_of([v for row in lower for v in row] + [v for row in share for v in row])


def coefficients(size, second):
    return pl.pallas_call(
        functools.partial(coefficients_kernel, size),
        compiler_params=LIMIT,
        in_specs=[VMEM_SPEC],
        out_specs=VMEM_SPEC,
        out_shape=jax.ShapeDtypeStruct((1, OBS), F32),
    )(second)


def coefficients_of(coef_ref):
    coef = functools.partial(lane_of, coef_ref[...])
    lower = [[coef(j * (j + 1) // 2 + i) for i in range(j + 1)] for j in range(K)]
    share = [[coef(2 * K + i * K + j) for j in range(K)] for i in range(K)]
    return lower, share


def lane_of(row, k):
    lanes = lax.broadcasted_iota(jnp.int32, row.shape, 1)
    return jnp.sum(jnp.where(lanes == k, row, 0.0), axis=1, keepdims=True)


def row_of(values):
    lanes = lax.broadcasted_iota(jnp.int32, (1, OBS), 1)
    row = jnp.zeros((1, OBS), F32)
    for k, value in enumerate(values):
        row = jnp.where(lanes == k, value, row)
    return row


def second_profiles(core, mine_ref, other_ref, prof):
    half = K * FULL // 2
    mine, other = mine_ref[...].astype(F32), other_ref[...].astype(F32)
    prof[0:half, :] = jnp.where(core == 0, mine, other)
    prof[half:, :] = jnp.where(core == 0, other, mine)


def inner_kernel(part_ref, mine_1_ref, other_1_ref, mine_2_ref, other_2_ref, sign_ref, *refs):
    pieces = refs[: SLICES // 2]
    out_ref, test_prof, prof, image = refs[SLICES // 2 :]
    chips = SLICES // 2
    chip, core = part_ref[0] // 2, part_ref[0] % 2
    second_profiles(core, mine_2_ref, other_2_ref, prof)
    test_prof[...] = jnp.where(
        core == 0, other_1_ref[...].astype(F32), mine_1_ref[...].astype(F32)
    )
    sums = {}
    for n in range(chips):
        image[...] = pieces[n][HALVES:, :].astype(F32)
        source = lax.rem(chip + chips - n, chips) * 2
        for side, owner in enumerate((core, 1 - core)):
            start = (source + owner) * SLICE
            rows = [
                image[side * OWN + k * SLICE : side * OWN + (k + 1) * SLICE, :] for k in range(K)
            ]
            for j in range(K):
                levels = pl.ds(j * FULL + start, SLICE)
                for kind, ref in enumerate((prof, test_prof)):
                    values = ref[levels, :]
                    for k in range(K):
                        term = rows[k] * values
                        key = (kind, k, j)
                        sums[key] = sums[key] + term if key in sums else term
    values = [jnp.sum(sums[0, k, j]) for k in range(K) for j in range(K)]
    values += [jnp.sum(sums[1, k, j]) for j in range(K) for k in range(K)]
    out_ref[...] = jnp.broadcast_to(row_of(values) + sign_ref[...], out_ref.shape)


def inner_products(part, profiles_1, profiles_2, signs, messages):
    return pl.pallas_call(
        inner_kernel,
        compiler_params=LIMIT,
        in_specs=[SMEM_SPEC] + [VMEM_SPEC] * 9,
        out_specs=VMEM_SPEC,
        out_shape=jax.ShapeDtypeStruct((TILES, OBS), F32),
        scratch_shapes=[
            pltpu.VMEM((K * FULL, OBS), F32),
            pltpu.VMEM((K * FULL, OBS), F32),
            pltpu.VMEM((2 * OWN, OBS), F32),
        ],
    )(part, *profiles_1, *profiles_2, signs, *messages)


def outputs_kernel(
    part_ref, mine_ref, other_ref, coef_ref, z_ref, jac_hbm, q_ref, w_ref, jac, sems, prof, x
):
    start_jac(jac_hbm, jac, sems)
    x[...] = jnp.zeros_like(x)
    second_profiles(part_ref[0] % 2, mine_ref, other_ref, prof)
    lower, share = coefficients_of(coef_ref)
    forward(jac_hbm, jac, sems, prof, x, K)
    image_q = []
    for j in range(K):
        q = None
        for i in range(j + 1):
            qx = lower[j][i] * x[i, 0:CHAN, :]
            q = qx if q is None else q + qx
        q_ref[j] = q
        image_q.append(q)
    for j in range(K):
        w = z_ref[j, 0:CHAN, :]
        for i in range(K):
            w = w - share[i][j] * image_q[i]
        w_ref[j] = w


def outputs(part, mine, other, coefs, z, jac):
    return pl.pallas_call(
        outputs_kernel,
        compiler_params=WIDE,
        in_specs=[SMEM_SPEC] + [VMEM_SPEC] * 4 + [HBM_SPEC],
        out_specs=[VMEM_SPEC] * 2,
        out_shape=[jax.ShapeDtypeStruct((K, CHAN, OBS), F32)] * 2,
        scratch_shapes=JAC_SCRATCH
        + [pltpu.VMEM((K * FULL, OBS), F32), pltpu.VMEM((K, CPAD, OBS), F32)],
        cost_estimate=COST,
    )(part, mine, other, coefs, z, jac)


def traces_kernel(size, parts_ref, coef_ref, mean_ref, rayleigh_ref):
    total = functools.partial(lane_of, jnp.sum(parts_ref[...], axis=0, keepdims=True))
    lower, share = coefficients_of(coef_ref)
    yx = [[total(k * K + j) for j in range(K)] for k in range(K)]
    zy = [[total(K * K + j * K + k) for k in range(K)] for j in range(K)]
    tz = [total(2 * K * K + j) for j in range(K)]
    quad = [
        [
            sum(
                lower[i][a] * lower[k][b] * yx[a][b]
                for a in range(i + 1)
                for b in range(k + 1)
            )
            for k in range(K)
        ]
        for i in range(K)
    ]
    cross = [
        [sum(lower[i][b] * zy[j][b] for b in range(i + 1)) for j in range(K)] for i in range(K)
    ]
    trace_q = quad[0][0] + quad[1][1] + quad[2][2]
    trace_w = 0.0
    for j in range(K):
        trace_w = trace_w + tz[j]
        for i in range(K):
            trace_w = trace_w - 2.0 * share[i][j] * cross[i][j]
            for k in range(K):
                trace_w = trace_w + share[i][j] * share[k][j] * quad[i][k]
    mean = trace_q / (size * size) + trace_w / (K * size)
    mean_ref[0] = jnp.sum(mean)
    rayleigh_ref[0] = jnp.sum(trace_q / (K * size))


def traces(size, parts, coefs):
    return pl.pallas_call(
        functools.partial(traces_kernel, size),
        compiler_params=LIMIT,
        in_specs=[VMEM_SPEC, VMEM_SPEC],
        out_specs=[SMEM_SPEC, SMEM_SPEC],
        out_shape=[jax.ShapeDtypeStruct((1,), F32)] * 2,
    )(parts, coefs)


CHIPS = SLICES // 2


def parity_kernel(part_ref, members_ref, keep_ref, send_ref):
    core = part_ref[0] % 2
    for chip in range(CHIPS):
        keep_ref[chip] = members_ref[2 * chip + core]
        send_ref[chip] = members_ref[2 * chip + 1 - core]


def by_parity(part, members):
    half = jax.ShapeDtypeStruct((CHIPS, *members.shape[1:]), BF16)
    return pl.pallas_call(
        parity_kernel,
        compiler_params=LIMIT,
        in_specs=[SMEM_SPEC, VMEM_SPEC],
        out_specs=[VMEM_SPEC, VMEM_SPEC],
        out_shape=[half, half],
    )(part, members)


def split_kernel(part_ref, keep_ref, got_ref, *out_refs):
    for k in range(CHIPS):
        chip = lax.rem(part_ref[0] // 2 + k, CHIPS)
        out_refs[k][0:PIECE, :] = keep_ref[chip]
        out_refs[k][PIECE:, :] = got_ref[chip]


def split(part, keep, got):
    pair = jax.ShapeDtypeStruct((2 * PIECE, keep.shape[2]), BF16)
    return pl.pallas_call(
        split_kernel,
        compiler_params=LIMIT,
        in_specs=[SMEM_SPEC, VMEM_SPEC, VMEM_SPEC],
        out_specs=[VMEM_SPEC] * CHIPS,
        out_shape=[pair] * CHIPS,
    )(part, keep, got)


def pick_kernel(place_ref, first_ref, *refs):
    pairs = refs[:CHIPS]
    out_ref, members, chosen = refs[CHIPS:]
    cells = members.shape[1]
    core = place_ref[1] % 2
    for k in range(CHIPS):
        source = lax.rem(place_ref[1] // 2 + CHIPS - k, CHIPS) * 2
        for n, owner in enumerate((core, 1 - core)):
            at = pl.multiple_of((source + owner) * PIECE, PIECE)
            members[pl.ds(at, PIECE), :] = pairs[k][n * PIECE : (n + 1) * PIECE, :]
    tile = place_ref[0].astype(F32)
    slots = lax.broadcasted_iota(jnp.int32, (CAP, OBS), 0).astype(F32)
    lanes = lax.broadcasted_iota(jnp.int32, (CAP, cells), 1).astype(F32)
    for d in range(TILES):
        codes = first_ref[d, CODES:FIRST, :].astype(F32)
        cell = codes[0:1] * 128.0 + codes[1:2] - tile * float(cells)
        inside = (cell >= 0.0) & (cell < float(cells))
        here = jnp.where((slots == codes[2:3]) & inside, cell + 1.0, 0.0)
        at = jnp.sum(here, axis=1, keepdims=True) - 1.0
        chosen[d * CAP : (d + 1) * CAP, :] = jnp.where(lanes == at, 1.0, 0.0).astype(BF16)
    out_ref[...] = dot(chosen[...], members[...], NT).astype(BF16)


def pick(place, first, pieces):
    cells = pieces[0].shape[1]
    return pl.pallas_call(
        pick_kernel,
        compiler_params=LIMIT,
        in_specs=[SMEM_SPEC] + [VMEM_SPEC] * (1 + CHIPS),
        out_specs=VMEM_SPEC,
        out_shape=jax.ShapeDtypeStruct((TILES * CAP, SLICES * PIECE), BF16),
        scratch_shapes=[
            pltpu.VMEM((SLICES * PIECE, cells), BF16),
            pltpu.VMEM((TILES * CAP, cells), BF16),
        ],
    )(place, first, *pieces)


def own_kernel(pos_ref, recv_ref, out_ref, all_ref):
    slots = lax.broadcasted_iota(jnp.int32, (OBS, TILES * CAP), 1)
    chosen = jnp.where(slots == pos_ref[...], 1.0, 0.0).astype(BF16)
    mine = dot(chosen, recv_ref[...]).astype(BF16)
    shape = (SLICE * MEMBERS, SLICES * PIECE)
    row = lax.broadcasted_iota(jnp.int32, shape, 0)
    lane = lax.broadcasted_iota(jnp.int32, shape, 1)
    level, member = jnp.right_shift(row, 4), row & 15
    source = jnp.right_shift(member, 1) * PIECE + 2 * level + (member & 1)
    turn = jnp.where(lane == source, 1.0, 0.0).astype(BF16)
    mine = dot(turn, mine, NT)
    out_ref[...] = mine.astype(BF16)
    copies(all_ref, mine)


def own(position, recv):
    rows = SLICE * MEMBERS
    return pl.pallas_call(
        own_kernel,
        compiler_params=LIMIT,
        in_specs=[VMEM_SPEC, VMEM_SPEC],
        out_specs=[VMEM_SPEC, VMEM_SPEC],
        out_shape=[
            jax.ShapeDtypeStruct((rows, OBS), BF16),
            jax.ShapeDtypeStruct((TILES, rows, OBS), BF16),
        ],
    )(position, recv)


def pair_kernel(mine_ref, got_ref, out_ref):
    rows = mine_ref.shape[0]
    out_ref[0:rows, :] = mine_ref[...]
    out_ref[rows:, :] = got_ref[...]


def paired(mine, got):
    return pl.pallas_call(
        pair_kernel,
        compiler_params=LIMIT,
        in_specs=[VMEM_SPEC, VMEM_SPEC],
        out_specs=VMEM_SPEC,
        out_shape=jax.ShapeDtypeStruct((2 * mine.shape[0], OBS), BF16),
    )(mine, got)


def gathered_kernel(part_ref, *refs):
    rows = SLICE * MEMBERS
    pairs = refs[:CHIPS]
    out_ref, mem = refs[CHIPS:]
    chip, core = part_ref[0] // 2, part_ref[0] % 2
    for k in range(CHIPS):
        source = lax.rem(chip + CHIPS - k, CHIPS) * 2
        for n, owner in enumerate((core, 1 - core)):
            at = pl.multiple_of((source + owner) * rows, rows)
            mem[pl.ds(at, rows), :] = pairs[k][n * rows : (n + 1) * rows, :].astype(F32)
    for m in range(MEMBERS):
        out_ref[m * FULL : (m + 1) * FULL, :] = mem[pl.ds(m, FULL, stride=MEMBERS), :]


def gathered(part, pairs):
    return pl.pallas_call(
        gathered_kernel,
        compiler_params=LIMIT,
        in_specs=[SMEM_SPEC] + [VMEM_SPEC] * CHIPS,
        out_specs=VMEM_SPEC,
        out_shape=jax.ShapeDtypeStruct((MEMBERS * FULL, OBS), F32),
        scratch_shapes=[pltpu.VMEM((MEMBERS * FULL, OBS), F32)],
        cost_estimate=pl.CostEstimate(flops=10**6, bytes_accessed=2 * 10**6, transcendentals=0),
    )(part, *pairs)


def near_kernel(col_ref, first_ref, table_ref, out_ref):
    mine = col_ref[...]
    my_x = (mine // CB).astype(F32)
    my_b = mine % CB
    hot = jnp.where(lax.broadcasted_iota(jnp.int32, (OBS, CB), 1) == my_b, 1.0, 0.0).astype(BF16)
    reach = [dot(hot, table_ref[a]).astype(BF16) for a in range(STEPS + 1)]
    rows = lax.broadcasted_iota(jnp.int32, (CB, OBS), 0)
    for d in range(TILES):
        codes = first_ref[d, CODES:FIRST, :].astype(F32).astype(jnp.int32)
        hi, lo = codes[0:1], codes[1:2]
        x = (hi * 4 + lo // CB).astype(F32)
        there = jnp.where(rows == lo % CB, 1.0, 0.0).astype(BF16)
        gap = jnp.abs(my_x - x)
        gap = jnp.minimum(gap, float(NX) - gap)
        total = jnp.zeros((OBS, OBS), F32)
        for a in range(STEPS + 1):
            total = jnp.where(gap == float(a), dot(reach[a], there), total)
        out_ref[:, d * OBS : (d + 1) * OBS] = total.astype(BF16)


def near_of(column, first, table):
    return pl.pallas_call(
        near_kernel,
        compiler_params=LIMIT,
        in_specs=[VMEM_SPEC, VMEM_SPEC, VMEM_SPEC],
        out_specs=VMEM_SPEC,
        out_shape=jax.ShapeDtypeStruct((OBS, TILES * OBS), BF16),
        cost_estimate=pl.CostEstimate(flops=2 * 10**7, bytes_accessed=4 * 10**6, transcendentals=0),
    )(column, first, table)


def covariance_kernel(
    probes, scale, part_ref, all_ref, adj_ref, near_ref, mem_ref, vert_ref, *refs
):
    carried = refs[:-6]
    keep_ref, send_ref, prod, acc, adj, out = refs[-6:]
    rows = SLICE * MEMBERS
    adj[...] = adj_ref[...].astype(F32)

    def probe(p, carry):
        for d in range(TILES):
            for level in range(SLICE):
                row = adj[d, pl.ds(p * SLICE + level, 1), :]
                row = jnp.broadcast_to(row, (MEMBERS, OBS)).astype(BF16)
                at = slice(level * MEMBERS, (level + 1) * MEMBERS)
                prod[at, d * OBS : (d + 1) * OBS] = all_ref[d, at, :] * row
        acc[pl.ds(pl.multiple_of(p * rows, rows), rows), :] = dot(prod[...], near_ref[...], NT)
        return carry

    lax.fori_loop(0, probes, probe, 0)
    vert = vert_ref[...]
    for p in range(probes):
        total = None
        for m in range(MEMBERS):
            smooth = acc[pl.ds(p * rows + m, SLICE, stride=MEMBERS), :].astype(BF16)
            term = mem_ref[m * FULL : (m + 1) * FULL, :] * dot(vert, smooth)
            total = term if total is None else total + term
        out[p * FULL : (p + 1) * FULL, :] = total * scale
    half = probes * FULL // 2
    core = part_ref[0] % 2
    low, high = out[0:half, :], out[half : 2 * half, :]
    keep_ref[...] = jnp.where(core == 0, low, high).astype(BF16)
    sent = jnp.where(core == 0, high, low)
    if carried:
        send_ref[half:, :] = carried[0][0:OWN, :].astype(BF16)
    send_ref[0:half, :] = sent.astype(BF16)


def covariance(probes, scale, part, everyone, adjoints, near, mem, vert, *carried):
    rows = SLICE * MEMBERS
    half = probes * FULL // 2
    extra = OWN * len(carried)
    return pl.pallas_call(
        functools.partial(covariance_kernel, probes, scale),
        compiler_params=LIMIT,
        in_specs=[SMEM_SPEC] + [VMEM_SPEC] * (5 + len(carried)),
        out_specs=[VMEM_SPEC, VMEM_SPEC],
        out_shape=[
            jax.ShapeDtypeStruct((half, OBS), BF16),
            jax.ShapeDtypeStruct((half + extra, OBS), BF16),
        ],
        scratch_shapes=[
            pltpu.VMEM((rows, TILES * OBS), BF16),
            pltpu.VMEM((probes * rows, OBS), F32),
            pltpu.VMEM(adjoints.shape, F32),
            pltpu.VMEM((probes * FULL + extra, OBS), F32),
        ],
    )(part, everyone, adjoints, near, mem, vert, *carried)


def exchange(value, axis):
    return lax.all_to_all(value, axis, 0, 0, tiled=True)


def swap_cores(value):
    return lax.ppermute(value, "mem", [(j, j ^ 1) for j in range(SLICES)])


def to_other_chip(value, k):
    return lax.ppermute(value, "mem", [(j, (j + 2 * k) % SLICES) for j in range(SLICES)])


def from_other_chips(value):
    return [to_other_chip(value, k) for k in range(1, CHIPS)]


def sum_over_mem(keep, send, carried=None):
    half = keep.shape[0]
    got = swap_cores(send)
    kept = (keep.astype(F32) + got[:half].astype(F32)).astype(BF16)
    message = kept
    if carried is not None:
        message = jnp.concatenate([kept, carried[:OWN].astype(BF16), got[half:]], axis=0)
    others = from_other_chips(message)
    total = (kept.astype(F32) + others[1][:half].astype(F32)) + (
        others[0][:half].astype(F32) + others[2][:half].astype(F32)
    )
    total = total.astype(BF16)
    return (total, swap_cores(total)), [message] + others


def on_device(members, vertical, jacobian, sketch_bits, test_bits, obs_column, obs_slot):
    slice_id = lax.axis_index("mem").astype(jnp.int32)
    part = slice_id.reshape(1)
    my_tile = lax.axis_index(TILE).astype(jnp.int32)
    local, levels, cells = members.shape
    size = float(OBS * TILES * CHAN)
    scale = 1.0 / ((MEMBERS - 1) * 5.0**STEPS * WALK_SCALE)

    jac = jnp.transpose(jacobian, (2, 1, 0))
    sketch = jnp.swapaxes(sketch_bits, 1, 2)
    test = jnp.swapaxes(test_bits, 1, 2)
    column, slot = obs_column.reshape(1, OBS), obs_slot.reshape(1, OBS)
    first = sign_adjoints(part, sketch, test, column, slot, jac)
    first, members = lax.optimization_barrier((first, members))
    first = exchange(first, TILE)

    padded = jnp.pad(jnp.swapaxes(members, 0, 1), ((0, FULL - levels), (0, 0), (0, 0)))
    padded = padded.reshape(SLICES, SLICE * local, cells)
    padded = jnp.pad(padded, ((0, 0), (0, PIECE - SLICE * local), (0, 0)))
    keep, send = by_parity(part, padded)
    pairs = list(split(part, keep, swap_cores(send)))
    for k in range(1, CHIPS):
        pairs[k] = to_other_chip(pairs[k], k)

    place = jnp.stack([my_tile, slice_id])
    picked = pick(place, first, pairs)
    arrived = exchange(picked.reshape(TILES, CAP, -1), TILE)
    near = near_of(obs_column.reshape(OBS, 1), first, jnp.asarray(walk_table(), BF16))
    vert = jnp.pad(vertical, ((0, FULL - levels), (0, FULL - levels)))
    vert = lax.dynamic_slice_in_dim(vert, slice_id * SLICE, SLICE, axis=1)
    arrived, near, vert = lax.optimization_barrier((arrived, near, vert))
    position = (obs_column // cells * CAP + obs_slot).reshape(OBS, 1)
    mine, everyone = own(position, arrived.reshape(TILES * CAP, -1))
    everyone = exchange(everyone, TILE)
    pair = paired(mine, swap_cores(mine))
    mem = gathered(part, [pair] + from_other_chips(pair))

    halves = covariance(2 * K, scale, part, everyone, first, near, mem, vert)
    (mine_1, other_1), _ = sum_over_mem(*halves)
    second, image = images(part, mine_1, other_1, test, jac)
    second = exchange(second, TILE)
    z, signs = test_images(part, mine_1, other_1, test, jac)
    second, z = lax.optimization_barrier((second, z))
    halves = covariance(K, scale, part, everyone, second, near, mem, vert, image)
    coefs = coefficients(size, second)
    (mine_2, other_2), messages = sum_over_mem(*halves, image)
    mine_2, coefs = lax.optimization_barrier((mine_2, coefs))
    parts = inner_products(part, (mine_1, other_1), (mine_2, other_2), signs, messages)
    parts = exchange(parts.reshape(-1, 1, OBS), TILE)
    image_q, image_w = outputs(part, mine_2, other_2, coefs, z, jac)
    mean, rayleigh = traces(size, parts.reshape(-1, OBS), coefs)
    return (
        jnp.swapaxes(image_q, 1, 2),
        jnp.swapaxes(image_w, 1, 2),
        mean.reshape(()),
        rayleigh.reshape(()),
    )


def solution(mesh):
    finer = Mesh(mesh.devices.reshape(mesh.shape["mem"], 4, 4), ("mem", "tile_0", "tile_1"))
    return jax.shard_map(
        on_device,
        mesh=finer,
        in_specs=(
            P("mem", None, TILE),
            P(),
            P(TILE, None, None),
            P(None, TILE, None),
            P(None, TILE, None),
            P(TILE),
            P(TILE),
        ),
        out_specs=(P(None, TILE, None), P(None, TILE, None), P(), P()),
        check_vma=False,
    )
```
